32 devices in a mesh: wide: 8 (over z, y), narrow: 4 (over x, core).
Axes of the slice: x: 2, y: 2, z: 4, core: 2. Of those that a mesh axis runs over, the one named last changes fastest.
Arguments:
- media_feats: bfloat16 [8, 2048, 1536], P('wide', 'narrow'), may hold values from -6 to 6
- latents: bfloat16 [8, 64, 1536], P('wide', 'narrow'), may hold values from -6 to 6
- frame_counts: int32 [8], P('wide'), may hold values from 1 to 8, as said below
- media_mask: int32 [8, 2048], P('wide'), may hold values 0 or 1
- time_embed: bfloat16 [8, 1536], replicated, may hold values from -3 to 3
- media_gain: float32 [1536], replicated, may hold values from 0.1 to 1.9
- media_bias: float32 [1536], replicated, may hold values from -1.75 to 1.75
- latent_gain: float32 [1536], replicated, may hold values from 0.1 to 1.9
- latent_bias: float32 [1536], replicated, may hold values from -1.75 to 1.75
- ffn_gain: float32 [1536], replicated, may hold values from 0.1 to 1.9
- ffn_bias: float32 [1536], replicated, may hold values from -1.75 to 1.75
- query_weight: bfloat16 [1536, 1536], P('wide', 'narrow'), may hold values from -0.3125 to 0.3125
- keyval_weight: bfloat16 [1536, 2, 1536], P('wide', None, 'narrow'), may hold values from -0.15625 to 0.15625
- output_weight: bfloat16 [1536, 1536], P('narrow', 'wide'), may hold values from -0.625 to 0.625
- up_weight: bfloat16 [1536, 6144], P(None, 'narrow'), may hold values from -0.15625 to 0.15625
- down_weight: bfloat16 [6144, 1536], P('narrow'), may hold values from -0.078125 to 0.078125
- cotangent: bfloat16 [8, 64, 1536], P('wide', 'narrow'), may hold values from -6 to 6
Outputs:
- out_latents: bfloat16 [8, 64, 1536], P('wide', 'narrow')
- grad_media: bfloat16 [8, 2048, 1536], P('wide', 'narrow')
- grad_latents: bfloat16 [8, 64, 1536], P('wide', 'narrow')
- grad_time_embed: float32 [8, 1536], P(None, ('wide', 'narrow'))
- grad_media_gain: float32 [1536], P(('wide', 'narrow'))
- grad_media_bias: float32 [1536], P(('wide', 'narrow'))
- grad_latent_gain: float32 [1536], P(('wide', 'narrow'))
- grad_latent_bias: float32 [1536], P(('wide', 'narrow'))
- grad_ffn_gain: float32 [1536], P(('wide', 'narrow'))
- grad_ffn_bias: float32 [1536], P(('wide', 'narrow'))
- grad_query_weight: float32 [1536, 1536], P('wide', 'narrow')
- grad_keyval_weight: float32 [1536, 2, 1536], P('wide', None, 'narrow')
- grad_output_weight: float32 [1536, 1536], P('narrow', 'wide')
- grad_up_weight: float32 [1536, 6144], P('wide', 'narrow')
- grad_down_weight: float32 [6144, 1536], P('narrow', 'wide')
The draws below stay inside these ranges and needn't reach their ends.
Inputs may be any that keep to these rules, and one draw needn't show every extreme that they name: `frame_counts`: frames of each item; some item has exactly 8.
All inputs are finite; a program needn't handle non-finite values. No bound on the sum of `media_mask` on one device may be relied on, other than what follows from the above.
Results may differ from the reference program's by a relative error of at most 0.02.
Values may be sent and summed in bfloat16 or wider, within the bound.
A program may use at most 128 MiB of HBM per device.

```python
import jax
import jax.numpy as jnp
from jax import lax

D = 1536
HEADS = 16
HEAD_DIM = 96
FF = 6144
LATENTS = 64
FRAMES_MAX = 8
PATCHES = 256
ITEM_DEV = 1
ITEMS = 8
MEDIA = 2048


def draw_frame_counts(key, part):
    slots = jnp.arange(ITEMS, dtype=jnp.int32)
    groups = ITEMS // ITEM_DEV
    group = slots // ITEM_DEV
    ceiling = 2 + (FRAMES_MAX - 2) * group // max(groups - 1, 1)
    raw_bits = jax.random.randint(key, (ITEMS,), 0, 1 << 20, dtype=jnp.int32)
    counts = 1 + raw_bits % ceiling
    counts = jnp.where(slots == ITEMS - 1, FRAMES_MAX, counts)
    return counts.astype(jnp.int32)


def with_ends(drawn, rng, least, largest):
    place = [jax.random.randint(jax.random.fold_in(rng, axis), (), 0, length) for axis, length in enumerate(drawn.shape)]
    longest = drawn.shape.index(max(drawn.shape))
    neighbour = place[:longest] + [(place[longest] + 1) % drawn.shape[longest]] + place[longest + 1:]
    return drawn.at[tuple(place)].set(least).at[tuple(neighbour)].set(largest)


def level_of(rng, dims, cuts, low, top_value):
    gain = 1.0
    for dim, shards_of in cuts:
        heights = jax.random.uniform(jax.random.fold_in(jax.random.fold_in(rng, 6), dim), (shards_of,), jnp.float32, low / len(cuts), top_value / len(cuts))
        gain = gain * jnp.repeat(jnp.exp(heights), dims[dim] // shards_of).reshape((-1,) + (1,) * (len(dims) - 1 - dim))
    return gain


def bell_draw(key, dims, scale, bound, shards=(), kind=jnp.bfloat16):
    level = level_of(key, dims, shards, -0.22, 0.18) if shards else 1.0
    entries = jax.random.normal(key, dims, jnp.float32) * scale * level
    return jnp.minimum(jnp.maximum(entries, -bound), bound).astype(kind)


def setup_inputs(seed: int = 0) -> dict:
    key_of = jax.random.split(jax.random.key(seed), 18)
    return {
        "media_feats": bell_draw(key_of[0], (ITEMS, MEDIA, D), 1.0, 6.0, ((0, 8), (1, 4))),
        "latents": bell_draw(key_of[1], (ITEMS, LATENTS, D), 1.0, 6.0, ((0, 8), (1, 4))),
        "frame_counts": draw_frame_counts(jax.random.fold_in(key_of[17], 71), 0),
        "media_mask": with_ends((jax.random.randint(key_of[3], (ITEMS, MEDIA), 0, 8) < 7).astype(jnp.int32), jax.random.fold_in(key_of[3], 1), 0, 1),
        "time_embed": bell_draw(key_of[4], (FRAMES_MAX, D), 0.5, 3.0),
        "media_gain": jnp.clip(1.0 + 0.18 * jax.random.normal(key_of[5], (D,), jnp.float32), 0.1, 1.9),
        "media_bias": bell_draw(key_of[6], (D,), 0.3, 1.75, (), jnp.float32),
        "latent_gain": jnp.clip(1.0 + 0.18 * jax.random.normal(key_of[7], (D,), jnp.float32), 0.1, 1.9),
        "latent_bias": bell_draw(key_of[8], (D,), 0.3, 1.75, (), jnp.float32),
        "ffn_gain": jnp.clip(1.0 + 0.18 * jax.random.normal(key_of[9], (D,), jnp.float32), 0.1, 1.9),
        "ffn_bias": bell_draw(key_of[10], (D,), 0.3, 1.75, (), jnp.float32),
        "query_weight": bell_draw(key_of[11], (D, D), (D // 4) ** -0.5, 0.3125, ((0, 8), (1, 4))),
        "keyval_weight": bell_draw(key_of[12], (D, 2, D), D ** -0.5, 0.15625, ((0, 8), (2, 4))),
        "output_weight": bell_draw(key_of[13], (D, D), (D // 16) ** -0.5, 0.625, ((0, 4), (1, 8))),
        "up_weight": bell_draw(key_of[14], (D, FF), D ** -0.5, 0.15625, ((1, 4),)),
        "down_weight": bell_draw(key_of[15], (FF, D), FF ** -0.5, 0.078125, ((0, 4),)),
        "cotangent": bell_draw(key_of[16], (ITEMS, LATENTS, D), 1.0, 6.0, ((0, 8), (1, 4))),
    }


@jax.custom_vjp
def low(v):
    return lax.optimization_barrier(v.astype(jnp.bfloat16)).astype(jnp.float32)

@jax.custom_vjp
def low_back(v):
    return v

def low_keep(v):
    return (low(v), None)

def low_pass(kept, grad):
    return (grad,)

def back_keep(v):
    return (v, None)

def back_low(kept, grad):
    return (low(grad),)
low.defvjp(low_keep, low_pass)
low_back.defvjp(back_keep, back_low)
EPS = 1e-05
ENT_COEF = 4.0
HIGH = lax.Precision.HIGHEST

def layer_norm(values, norm_gain, norm_bias):
    row_mean = lax.optimization_barrier(jnp.mean(values, axis=-1, keepdims=True))
    centered = values - row_mean
    variance = lax.optimization_barrier(jnp.mean(centered * centered, axis=-1, keepdims=True))
    return centered * lax.rsqrt(variance + EPS) * norm_gain + norm_bias

def one_item(params, item):
    time_embed, media_gain, media_bias, latent_gain, latent_bias, ffn_gain, ffn_bias, query_weight, keyval_weight, output_weight, up_weight, down_weight = params
    media_one, latent_one, valid_one = item
    width = query_weight.shape[0]
    frame_rows = jnp.repeat(time_embed, PATCHES, axis=0)
    media_normed = low(layer_norm(media_one + frame_rows, media_gain, media_bias))
    latent_normed = low(layer_norm(latent_one, latent_gain, latent_bias))
    query = low(low_back(jnp.matmul(latent_normed, query_weight, precision=HIGH)))
    keys_in = jnp.concatenate([media_normed, latent_normed], axis=0)
    keys = low(low_back(jnp.matmul(keys_in, keyval_weight[:, 0, :], precision=HIGH)))
    values = low(low_back(jnp.matmul(keys_in, keyval_weight[:, 1, :], precision=HIGH)))
    key_heads = keys.reshape(-1, HEADS, HEAD_DIM)
    value_heads = values.reshape(-1, HEADS, HEAD_DIM)
    query_heads = query.reshape(LATENTS, HEADS, HEAD_DIM)
    scores = jnp.einsum('lhd,khd->hlk', query_heads, key_heads, precision=HIGH) * HEAD_DIM ** (-0.5)
    scores = low_back(scores)
    key_valid = jnp.concatenate([valid_one, jnp.ones((LATENTS,), dtype=bool)])
    masked = jnp.where(key_valid, scores, -1e+30)
    probs = jax.nn.softmax(masked, axis=-1)
    log_total = jax.nn.logsumexp(masked, axis=-1)
    plain_scores = jnp.where(key_valid, scores, 0.0)
    entropy = jnp.sum(log_total - lax.optimization_barrier(jnp.sum(probs * plain_scores, axis=-1)))
    attention = jnp.einsum('hlk,khd->lhd', low(probs), value_heads, precision=HIGH).reshape(LATENTS, width)
    attention = low(low_back(attention))
    branch = low_back(jnp.matmul(attention, output_weight, precision=HIGH))
    latent_mid = latent_one + branch
    hidden = low(layer_norm(latent_mid, ffn_gain, ffn_bias))
    pre_act = low_back(jnp.matmul(hidden, up_weight, precision=HIGH))
    act_low = low(jax.nn.gelu(pre_act, approximate=False))
    result = latent_mid + low_back(jnp.matmul(act_low, down_weight, precision=HIGH))
    return (result, entropy)

def forward(valid, media_feats, latents, *params):

    def scan_step(carry, item):
        result, entropy = jax.checkpoint(one_item)(params, item)
        return (carry + entropy, result)
    total, results = lax.scan(scan_step, jnp.zeros((), media_feats.dtype), (media_feats, latents, valid))
    return (results, total)

def reference(media_feats, latents, frame_counts, media_mask, time_embed, media_gain, media_bias, latent_gain, latent_bias, ffn_gain, ffn_bias, query_weight, keyval_weight, output_weight, up_weight, down_weight, cotangent):
    frame_ids = (jnp.arange(MEDIA, dtype=jnp.int32) // PATCHES).astype(jnp.int32)
    valid = (frame_ids[None, :] < frame_counts[:, None]) & (media_mask > 0)
    key_count = jnp.sum(valid.astype(jnp.float32)) + float(ITEMS * LATENTS)
    ent_weight = ENT_COEF * float(ITEMS * MEDIA) / key_count
    floats = [value.astype(jnp.float32) for value in (media_feats, latents, time_embed, media_gain, media_bias, latent_gain, latent_bias, ffn_gain, ffn_bias, query_weight, keyval_weight, output_weight, up_weight, down_weight)]

    def wrapped(*arrays):
        return forward(valid, *arrays)
    results, vjp_fn = jax.vjp(wrapped, *floats)
    gradients = vjp_fn((cotangent.astype(results[0].dtype), jnp.asarray(ent_weight, results[1].dtype)))
    return (results[0].astype(jnp.bfloat16), gradients[0].astype(jnp.bfloat16), gradients[1].astype(jnp.bfloat16), gradients[2], gradients[3], gradients[4], gradients[5], gradients[6], gradients[7], gradients[8], gradients[9], gradients[10], gradients[11], gradients[12], gradients[13])
```

```python
import math

import jax
import jax.numpy as jnp
from jax import lax
from jax.sharding import PartitionSpec as P

HEADS = 16
HEAD_DIM = 96
FRAMES_MAX = 8
PATCHES = 256


EPS = 1e-05
ENT_COEF = 4.0
HIGH = lax.Precision.HIGHEST


def norm_forward(values, norm_gain, norm_bias):
    row_mean = jnp.mean(values, axis=-1, keepdims=True)
    centered = values - row_mean
    inv_std = lax.rsqrt(jnp.mean(centered * centered, axis=-1, keepdims=True) + EPS)
    normed = centered * inv_std
    return (normed * norm_gain + norm_bias, normed, inv_std)


def norm_backward(grad_out, normed, inv_std, norm_gain):
    scaled = grad_out * norm_gain
    grad_in = inv_std * (
        scaled
        - jnp.mean(scaled, axis=-1, keepdims=True)
        - normed * jnp.mean(scaled * normed, axis=-1, keepdims=True)
    )
    return (grad_in, jnp.sum(grad_out * normed, axis=0), jnp.sum(grad_out, axis=0))


def gelu_slope(pre_act):
    cdf_part = 0.5 * (1.0 + lax.erf(pre_act * (1.0 / math.sqrt(2.0))))
    density = jnp.exp(-0.5 * pre_act * pre_act) * (1.0 / math.sqrt(2.0 * math.pi))
    return cdf_part + pre_act * density


def body(
    media_feats,
    latents,
    frame_counts,
    media_mask,
    time_embed,
    media_gain,
    media_bias,
    latent_gain,
    latent_bias,
    ffn_gain,
    ffn_bias,
    query_weight,
    keyval_weight,
    output_weight,
    up_weight,
    down_weight,
    cotangent,
):
    width = media_feats.shape[2]
    own_media = media_feats.shape[1]
    own_latent = latents.shape[1]
    narrow_size = lax.axis_size("narrow")
    wide_size = lax.axis_size("wide")
    narrow_pos = lax.axis_index("narrow")
    media_total = own_media * narrow_size
    latent_total = own_latent * narrow_size
    head_local = HEADS // narrow_size
    cols = head_local * HEAD_DIM
    key_total = media_total + latent_total
    f32, bf16 = jnp.float32, jnp.bfloat16

    def mm(spec, a, b):
        return jnp.einsum(spec, a, b, preferred_element_type=f32)

    all_ids = jnp.arange(media_total, dtype=jnp.int32) // PATCHES
    valid_one = (all_ids < frame_counts[0]) & (media_mask[0] > 0)
    local_count = jnp.sum(valid_one.astype(f32)) + float(latent_total)
    total_count = lax.psum(local_count, "wide")
    ent_weight = ENT_COEF * float(wide_size * media_total) / total_count
    kv_own = lax.all_gather(keyval_weight, "wide", axis=0, tiled=True).reshape(width, 2 * cols)
    query_own = lax.all_gather(query_weight, "wide", axis=0, tiled=True)
    output_own = lax.all_gather(output_weight, "wide", axis=1, tiled=True)
    own_ids = (narrow_pos * own_media + jnp.arange(own_media, dtype=jnp.int32)) // PATCHES
    frame_onehot = own_ids[:, None] == jnp.arange(FRAMES_MAX, dtype=jnp.int32)[None, :]
    time_rows = jnp.dot(frame_onehot.astype(bf16), time_embed, preferred_element_type=f32)
    score_scale = HEAD_DIM ** (-0.5)
    media_one, latent_one, cot_one = media_feats[0], latents[0], cotangent[0]
    media_nf, media_hat, media_istd = norm_forward(
        media_one.astype(f32) + time_rows, media_gain, media_bias
    )
    latent_f32 = latent_one.astype(f32)
    latent_nf, latent_hat, latent_istd = norm_forward(latent_f32, latent_gain, latent_bias)
    latent_all = lax.all_gather(latent_nf.astype(bf16), "narrow", axis=0, tiled=True)
    cot_all = lax.all_gather(cot_one, "narrow", axis=0, tiled=True)
    media_all = lax.all_gather(media_nf.astype(bf16), "narrow", axis=0, tiled=True)
    keys_in = jnp.concatenate([media_all, latent_all], axis=0)
    query_act = mm("ld,dc->lc", latent_all, query_own).astype(bf16)
    key_vals = mm("kd,dc->kc", keys_in, kv_own).astype(bf16)
    query_heads = query_act.reshape(latent_total, head_local, HEAD_DIM)
    key_heads = key_vals[:, :cols].reshape(key_total, head_local, HEAD_DIM)
    value_heads = key_vals[:, cols:].reshape(key_total, head_local, HEAD_DIM)
    key_valid = jnp.concatenate([valid_one, jnp.ones((latent_total,), dtype=bool)])
    scores = mm("lhd,khd->hlk", query_heads, key_heads) * score_scale
    open_keys = key_valid[None, None, :]
    masked = jnp.where(open_keys, scores, -1e30)
    row_top = jnp.max(masked, axis=-1)
    expo = jnp.exp(masked - row_top[..., None])
    prob_all = expo / jnp.sum(expo, axis=-1)[..., None]
    prob_low = prob_all.astype(bf16)
    plain_scores = jnp.where(open_keys, scores, 0.0)
    mean_score = jnp.sum(prob_all * plain_scores, axis=-1)
    attn_out = mm("hlk,khd->lhd", prob_low, value_heads).reshape(latent_total, cols)
    attn_low = attn_out.astype(bf16)
    branch_part = mm("lc,cd->ld", attn_low, output_own)
    branch_own = lax.psum_scatter(
        branch_part.astype(bf16), "narrow", scatter_dimension=0, tiled=True
    ).astype(f32)
    latent_mid = latent_f32 + branch_own
    hidden_f, hidden_hat, hidden_istd = norm_forward(latent_mid, ffn_gain, ffn_bias)
    hidden_all = lax.all_gather(hidden_f.astype(bf16), "narrow", axis=0, tiled=True)
    pre_act = mm("ld,df->lf", hidden_all, up_weight)
    act_low = jax.nn.gelu(pre_act, approximate=False).astype(bf16)
    grad_act = mm("ld,fd->lf", cot_all, down_weight)
    grad_pre = (grad_act * gelu_slope(pre_act)).astype(bf16)
    hidden_part = mm("lf,df->ld", grad_pre, up_weight)
    grad_hidden = lax.psum_scatter(
        hidden_part.astype(bf16), "narrow", scatter_dimension=0, tiled=True
    ).astype(f32)
    grad_norm, fg_part, fb_part = norm_backward(grad_hidden, hidden_hat, hidden_istd, ffn_gain)
    grad_mid = cot_one.astype(f32) + grad_norm
    grad_branch_all = lax.all_gather(grad_mid.astype(bf16), "narrow", axis=0, tiled=True)
    ffn_part = mm("lf,fd->ld", act_low, down_weight)
    ffn_own = lax.psum_scatter(
        ffn_part.astype(bf16), "narrow", scatter_dimension=0, tiled=True
    ).astype(f32)
    out_one = (latent_mid + ffn_own).astype(bf16)
    grad_attn = mm("ld,cd->lc", grad_branch_all, output_own).astype(bf16)
    row_dots = jnp.sum(
        (grad_attn.astype(f32) * attn_out).reshape(latent_total, head_local, HEAD_DIM), axis=-1
    )
    shift_rows = (jnp.transpose(row_dots, (1, 0)) - ent_weight * mean_score)[..., None]
    grad_heads = grad_attn.reshape(latent_total, head_local, HEAD_DIM)
    grad_prob = mm("lhd,khd->hlk", grad_heads, value_heads)
    grad_scores = (prob_all * (grad_prob - ent_weight * plain_scores - shift_rows)).astype(bf16)
    grad_values = mm("hlk,lhd->khd", prob_low, grad_heads).reshape(key_total, cols)
    grad_keys = mm("hlk,lhd->khd", grad_scores, query_heads).reshape(key_total, cols) * score_scale
    grad_query = (
        mm("hlk,khd->lhd", grad_scores, key_heads).reshape(latent_total, cols) * score_scale
    ).astype(bf16)
    grad_pairs = jnp.concatenate([grad_keys, grad_values], axis=-1).astype(bf16)
    rows_part = mm("ke,de->kd", grad_pairs, kv_own)
    grad_media_rows = lax.psum_scatter(
        rows_part[:media_total].astype(bf16), "narrow", scatter_dimension=0, tiled=True
    ).astype(f32)
    latent_part = rows_part[media_total:] + mm("lc,dc->ld", grad_query, query_own)
    grad_latent_normed = lax.psum_scatter(
        latent_part.astype(bf16), "narrow", scatter_dimension=0, tiled=True
    ).astype(f32)
    keyval_grad = mm("kd,ke->de", keys_in, grad_pairs)
    keyval_sum = lax.psum_scatter(
        keyval_grad.astype(bf16), "wide", scatter_dimension=0, tiled=True
    ).astype(f32).reshape(width // wide_size, 2, cols)
    tall = lax.all_gather(
        jnp.concatenate([act_low, grad_pre, attn_low, grad_query], axis=1), "wide", axis=0, tiled=True
    )
    ff = up_weight.shape[1]
    act_g, pre_g, attn_g, query_g = (
        tall[:, :ff], tall[:, ff : 2 * ff], tall[:, 2 * ff : 2 * ff + cols], tall[:, 2 * ff + cols :]
    )
    cut = jnp.stack([latent_all, cot_all, hidden_all, grad_branch_all], axis=0)
    cut = cut.reshape(4, latent_total, wide_size, width // wide_size).transpose(2, 0, 1, 3)
    cut = lax.all_to_all(cut, "wide", split_axis=0, concat_axis=0, tiled=True)
    cut = cut.transpose(1, 0, 2, 3).reshape(4, wide_size * latent_total, width // wide_size)
    up_sum = mm("rd,rf->df", cut[2], pre_g)
    down_sum = mm("rf,rd->fd", act_g, cut[1])
    output_sum = mm("rc,rd->cd", attn_g, cut[3])
    query_sum = mm("rd,rc->dc", cut[0], query_g)
    grad_media_in, mg_part, mb_part = norm_backward(
        grad_media_rows, media_hat, media_istd, media_gain
    )
    time_part = jnp.einsum(
        "mf,md->fd", frame_onehot.astype(f32), grad_media_in, precision=HIGH
    )
    grad_latent_in, lg_part, lb_part = norm_backward(
        grad_latent_normed, latent_hat, latent_istd, latent_gain
    )
    grad_latent_one = (grad_mid + grad_latent_in).astype(bf16)
    vectors = jnp.concatenate(
        [time_part, jnp.stack([mg_part, mb_part, lg_part, lb_part, fg_part, fb_part])], axis=0
    )
    vec = lax.psum_scatter(vectors, ("wide", "narrow"), scatter_dimension=1, tiled=True)
    return (
        out_one[None],
        grad_media_in.astype(bf16)[None],
        grad_latent_one[None],
        vec[:FRAMES_MAX],
        vec[FRAMES_MAX],
        vec[FRAMES_MAX + 1],
        vec[FRAMES_MAX + 2],
        vec[FRAMES_MAX + 3],
        vec[FRAMES_MAX + 4],
        vec[FRAMES_MAX + 5],
        query_sum,
        keyval_sum,
        output_sum,
        up_sum,
        down_sum,
    )


def solution(mesh):
    placed = (
        P("wide", "narrow", None),
        P("wide", "narrow", None),
        P("wide"),
        P("wide", None),
        P(),
        P(),
        P(),
        P(),
        P(),
        P(),
        P(),
        P("wide", "narrow"),
        P("wide", None, "narrow"),
        P("narrow", "wide"),
        P(None, "narrow"),
        P("narrow", None),
        P("wide", "narrow", None),
    )
    return jax.shard_map(
        body,
        mesh=mesh,
        in_specs=placed,
        out_specs=(
            P("wide", "narrow", None),
            P("wide", "narrow", None),
            P("wide", "narrow", None),
            P(None, ("wide", "narrow")),
            P(("wide", "narrow")),
            P(("wide", "narrow")),
            P(("wide", "narrow")),
            P(("wide", "narrow")),
            P(("wide", "narrow")),
            P(("wide", "narrow")),
            P("wide", "narrow"),
            P("wide", None, "narrow"),
            P("narrow", "wide"),
            P("wide", "narrow"),
            P("narrow", "wide"),
        ),
        check_vma=False,
    )
```

```python
import functools
import math

import jax
import jax.numpy as jnp
from jax import lax
from jax.experimental import pallas as pl
from jax.experimental.pallas import tpu as pltpu
from jax.sharding import PartitionSpec as P

HEADS = 16
HEAD_DIM = 96
FRAMES_MAX = 8
PATCHES = 256
EPS = 1e-05
ENT_COEF = 4.0
NEG = -1e30
LANES = 128
MESH = pl.DeviceIdType.MESH
F32 = jnp.float32
BF16 = jnp.bfloat16


def nn(a, b):
    return lax.dot_general(a, b, (((1,), (0,)), ((), ())), preferred_element_type=F32)


def nt(a, b):
    return lax.dot_general(a, b, (((1,), (1,)), ((), ())), preferred_element_type=F32)


def tn(a, b):
    return lax.dot_general(a, b, (((0,), (0,)), ((), ())), preferred_element_type=F32)


def rows_mean(v):
    return jnp.mean(v, axis=-1, keepdims=True)


def norm_stats(v):
    mean = rows_mean(v)
    centered = v - mean
    inv_std = lax.rsqrt(rows_mean(centered * centered) + EPS)
    return mean, inv_std, centered * inv_std


def norm_back(dy, hat, inv_std, gain):
    scaled = dy * gain
    return inv_std * (scaled - rows_mean(scaled) - hat * rows_mean(scaled * hat))


def fold8(v):
    return jnp.sum(v.reshape(v.shape[0] // 8, 8, v.shape[1]), axis=0)


class Plan:
    def __init__(self, mesh, media, latents, up):
        self.N = mesh.shape["narrow"]
        self.W = mesh.shape["wide"]
        self.X = self.N // 2
        self.W2 = self.W // 2
        self.Mo, self.D = media.shape[1], media.shape[2]
        self.Lo = latents.shape[1]
        self.M = self.Mo * self.N
        self.L = self.Lo * self.N
        self.HL = HEADS // self.N
        self.C = self.HL * HEAD_DIM
        self.KT = self.M + -(-self.L // LANES) * LANES
        self.F = up.shape[1]
        self.S = self.D // self.W
        self.V = self.S // self.N
        self.R = self.HL * self.L
        self.CH = 128
        self.NC = self.Mo // self.CH
        self.reuse = self.F == self.D and self.X * self.Mo <= self.D


def body_kernel(p, sem_counts, *refs):
    (
        media_h, lat_ref, fc_ref, mm_ref, te_ref, mg_ref, mb_ref, lg_ref, lb_ref, fg_ref, fb_ref,
        wq_h, wkv_h, wo_ref, up_h, down_h, cot_ref,
        out_lat, out_gm, out_gl, out_vec, out_q, out_kv, out_o, out_up, out_down,
        media, x_all, kvw, wq, wot, up, down, kv, st, pt, pn, gpair, mt, te32, mean_s, istd_s,
        lat_nf, lat_ag, cot_ag, cnt_ag,
        rs_st, rs_rc, hid_ag, gb_ag, mate_st, mate_rc, x_st, x_rc, own_sum,
        kvg, kvg_y, kvg_z, act_g, pre_g, att_g, gq_g, sl_st, sl_rc, ga, acc8, stat, vec_st, vec_rc, vec2_st, vec2_rc,
        o_up, o_down, o_o, o_q, o_kv, o_vec, ssem, rsem, lsem,
    ) = refs
    N, W, X, W2 = p.N, p.W, p.X, p.W2
    Mo, Lo, M, L, D, C, R, S, F, KT = p.Mo, p.Lo, p.M, p.L, p.D, p.C, p.R, p.S, p.F, p.KT
    CH, NC, HL, V = p.CH, p.NC, p.HL, p.V
    n = lax.axis_index("narrow")
    w = lax.axis_index("wide")
    core = lax.rem(n, 2)
    xpos = lax.div(n, 2)
    mate = n + 1 - 2 * core
    par = lax.rem(w, 2)
    partner = w + 1 - 2 * par
    scale = HEAD_DIM ** (-0.5)

    if p.reuse:
        mate_st, x_st = up, down

    counters = {"s": 0, "r": 0, "l": 0}
    sends = []
    local = []

    def new(kind, count=1):
        base = counters[kind]
        counters[kind] = base + count
        return base

    def put(src, dst, recv, axis, peer):
        d = pltpu.make_async_remote_copy(
            src, dst, ssem.at[new("s")], rsem.at[recv], device_id={axis: peer}, device_id_type=MESH
        )
        d.start()
        sends.append(d)

    def got(dst, recv):
        pltpu.make_async_remote_copy(
            dst, dst, ssem.at[0], rsem.at[recv], device_id={"narrow": mate}, device_id_type=MESH
        ).wait_recv()

    def here(src, dst, keep=True):
        d = pltpu.make_async_copy(src, dst, lsem.at[new("l")])
        d.start()
        if keep:
            local.append(d)
        return d

    def rows(ref, start, count):
        return ref.at[pl.ds(start, count), :]

    def al(v, m):
        return pl.multiple_of(v, m)

    def npeer(k):
        return lax.rem(n + k, N)

    def nsrc(k):
        return lax.rem(n + N - k, N)

    def wpeer(k):
        return lax.rem(w + k, W)

    def wsrc(k):
        return lax.rem(w + W - k, W)

    media_in = [here(rows(media_h, c * CH, CH), rows(media, c * CH, CH), False) for c in range(NC)]
    down_in = here(down_h, down, False)
    up_in = here(up_h, up, False)

    barrier = pltpu.get_barrier_semaphore()
    for k in range(1, N):
        pl.semaphore_signal(barrier, inc=1, device_id={"narrow": npeer(k)}, device_id_type=MESH)
    for k in range(1, W):
        pl.semaphore_signal(barrier, inc=1, device_id={"wide": wpeer(k)}, device_id_type=MESH)
    pl.semaphore_wait(barrier, N - 1 + W - 1)

    def wide_gather(src, buf, count):
        at = lambda b: rows(buf, al(b * count, 16), count)
        direct = new("r", W2)
        fwd = new("r", W2)
        for k in range(1, W2):
            put(src, at(w), direct + k, "wide", wpeer(2 * k))
        put(src, at(w), direct, "wide", partner)

        def forward(k):
            b = wsrc(2 * k)
            got(at(b), direct + k)
            put(at(b), at(b), fwd + k, "wide", partner)

        def finish():
            got(at(partner), direct)
            for k in range(1, W2):
                b = lax.rem(partner + W - 2 * k, W)
                got(at(b), fwd + k)

        return forward, finish

    own_w = [
        here(wkv_h, rows(kvw, al(w * S, 16), S), False),
        here(wq_h, rows(wq, al(w * S, 16), S), False),
    ]
    kv_fwd, kv_fin = wide_gather(wkv_h, kvw, S)
    q_fwd, q_fin = wide_gather(wq_h, wq, S)

    lat = lat_ref[...].astype(F32)
    lat_mean, lat_istd, lat_hat = norm_stats(lat)
    lat_ag[n] = (lat_hat * lg_ref[...] + lb_ref[...]).astype(BF16)
    cot_ag[n] = cot_ref[...]

    def narrow_gather(buf):
        base = new("r", N)
        for k in range(1, N):
            put(buf.at[n], buf.at[n], base + k, "narrow", npeer(k))

        def finish():
            for k in range(1, N):
                got(buf.at[nsrc(k)], base + k)
            return jnp.concatenate([buf[i].astype(F32) for i in range(N)], axis=0).astype(BF16)

        return finish

    te32[...] = te_ref[...].astype(F32)
    gain_m, bias_m = mg_ref[...], mb_ref[...]

    m_direct = new("r", NC * X)
    m_fwd = new("r", NC * X)

    def m_rows(block, c):
        return rows(x_all, al(block * Mo + c * CH, 16), CH)

    def frame_of(c):
        return lax.div(n * Mo + c * CH, PATCHES)

    for c in range(NC):
        media_in[c].wait()
        te_row = te32[pl.ds(frame_of(c), 1), :]

        def norm_rows(i, carry, c=c, te_row=te_row):
            r = al(c * CH + i * 16, 16)
            v = media[pl.ds(r, 16), :].astype(F32) + te_row
            mean, inv_std, hat = norm_stats(v)
            mean_s[pl.ds(r, 16), :] = jnp.broadcast_to(mean, (16, LANES))
            istd_s[pl.ds(r, 16), :] = jnp.broadcast_to(inv_std, (16, LANES))
            x_all[pl.ds(al(n * Mo + r, 16), 16), :] = (hat * gain_m + bias_m).astype(BF16)
            return carry

        lax.fori_loop(0, CH // 16, norm_rows, 0, unroll=2)
        for j in range(1, X):
            peer = lax.rem(xpos + j, X) * 2 + core
            put(m_rows(n, c), m_rows(n, c), m_direct + c * X + j, "narrow", peer)
        put(m_rows(n, c), m_rows(n, c), m_direct + c * X, "narrow", mate)
        if c == 0:
            lat_fin = narrow_gather(lat_ag)
            cot_fin = narrow_gather(cot_ag)

    def media_forward(c):
        for j in range(1, X):
            block = lax.rem(xpos + X - j, X) * 2 + core
            got(m_rows(block, c), m_direct + c * X + j)
            put(m_rows(block, c), m_rows(block, c), m_fwd + c * X + j, "narrow", mate)

    wot_st = wo_ref[...].astype(F32).T.astype(BF16)
    wot[pl.ds(al(w * S, 16), S), :] = wot_st

    slot_frame = lax.div(lax.broadcasted_iota(jnp.int32, (M // LANES, LANES), 0), PATCHES // LANES)
    ok = (slot_frame < fc_ref[0]) & (mm_ref[...] > 0)
    okf = jnp.where(ok, 1.0, 0.0).astype(F32)
    tail = jnp.where(
        lax.broadcasted_iota(jnp.int32, (1, KT - M), 1) < L, 1.0, 0.0
    ).astype(F32)
    for j in range(KT // LANES):
        row = okf[j : j + 1, :] if j < M // LANES else tail[:, j * LANES - M : j * LANES - M + LANES]
        mt[j * LANES : (j + 1) * LANES, :] = jnp.broadcast_to(row, (LANES, LANES)).T
    count = jnp.sum(okf, keepdims=True) + float(L)
    cnt_ag[w] = jnp.broadcast_to(count, (8, LANES))
    cnt_base = new("r", W)
    for k in range(1, W):
        put(cnt_ag.at[w], cnt_ag.at[w], cnt_base + k, "wide", wpeer(k))

    kv_fwd(1)
    o_fwd, o_fin = wide_gather(rows(wot, al(w * S, 16), S), wot, S)
    for k in range(2, W2):
        kv_fwd(k)
    media_forward(0)

    def spread(which, value):
        for b in range(W):
            sl_st[which, b * L : (b + 1) * L, :] = value[:, b * S : (b + 1) * S]
        base = new("r", W)
        at = lambda ref, b: ref.at[which, pl.ds(al(b * L, 16), L), :]
        for k in range(1, W):
            put(at(sl_st, wpeer(k)), at(sl_rc, w), base + k, "wide", wpeer(k))
        sl_rc[which, pl.ds(al(w * L, 16), L), :] = sl_st[which, pl.ds(al(w * L, 16), L), :]

        def finish():
            for k in range(1, W):
                got(at(sl_rc, wsrc(k)), base + k)

        return finish

    lat_all = lat_fin()
    cot_all = cot_fin()
    x_all[M : M + L, :] = lat_all
    if KT > M + L:
        x_all[M + L : KT, :] = jnp.zeros((KT - M - L, D), BF16)
    slat_fin = spread(0, lat_all)
    scot_fin = spread(1, cot_all)

    down_in.wait()

    def act_grad(j, carry):
        r = al(j * 256, 256)
        ga[:, pl.ds(r, 256)] = nt(cot_all, down[pl.ds(r, 256), :])
        return carry

    lax.fori_loop(0, F // 256, act_grad, 0)

    for k in range(1, W2):
        q_fwd(k)
    if NC > 1:
        media_forward(1)
    for d in own_w:
        d.wait()
    kv_fin()

    def project(start, count):
        def step(i, carry):
            r = al(start + i * CH, 16)
            kv[pl.ds(r, CH), :] = nn(x_all[pl.ds(r, CH), :], kvw[...]).astype(BF16)
            return carry

        lax.fori_loop(0, count // CH, step, 0)

    project(n * Mo, Mo)
    project(M, KT - M)
    for k in range(1, W2):
        o_fwd(k)
    for c in range(NC):
        got(m_rows(mate, c), m_direct + c * X)
    project(mate * Mo, Mo)
    q_fin()
    q_act = nn(lat_all, wq[...]).astype(BF16).astype(F32)
    head_of = lax.div(lax.broadcasted_iota(jnp.int32, (L, C), 1), HEAD_DIM)

    def per_head(v):
        return jnp.concatenate([jnp.where(head_of == h, v, 0.0) for h in range(HL)], axis=0)

    def from_heads(v):
        total = jnp.where(head_of == 0, v[0:L], 0.0)
        for h in range(1, HL):
            total = total + jnp.where(head_of == h, v[h * L : (h + 1) * L], 0.0)
        return total

    q_big32 = per_head(q_act)
    q_big = q_big32.astype(BF16)
    q_big_t = q_big32.T.astype(BF16)
    for c in range(2, NC):
        media_forward(c)
    for c in range(NC):
        for j in range(1, X):
            block = lax.rem(xpos + X - j, X) * 2 + core
            project(block * Mo + c * CH, CH)
            block = lax.rem(xpos + X - j, X) * 2 + 1 - core
            got(m_rows(block, c), m_fwd + c * X + j)
            project(block * Mo + c * CH, CH)

    KB = 128

    def wide_mask(r):
        m = mt[pl.ds(r, KB), :]
        return jnp.concatenate([m] * (R // LANES), axis=1) > 0.0

    def score_step(j, top):
        r = al(j * KB, KB)
        s = nn(kv[pl.ds(r, KB), 0:C], q_big_t) * scale
        s = jnp.where(wide_mask(r), s, NEG)
        st[pl.ds(r, KB), :] = s
        return jnp.maximum(top, jnp.max(s, axis=0, keepdims=True))

    top = lax.fori_loop(0, KT // KB, score_step, jnp.full((1, R), NEG, F32))

    def exp_step(j, carry):
        total, dot = carry
        r = al(j * KB, KB)
        s = st[pl.ds(r, KB), :]
        e = jnp.exp(s - top)
        pt[pl.ds(r, KB), :] = e
        s = jnp.where(wide_mask(r), s, 0.0)
        st[pl.ds(r, KB), :] = s
        return (
            total + jnp.sum(e, axis=0, keepdims=True),
            dot + jnp.sum(e * s, axis=0, keepdims=True),
        )

    zero_row = jnp.zeros((1, R), F32)
    total, dot = lax.fori_loop(0, KT // KB, exp_step, (zero_row, zero_row))
    inv_total = 1.0 / total
    mean_score = dot * inv_total

    def prob_step(j, carry):
        r = al(j * KB, KB)
        pr = pt[pl.ds(r, KB), :] * inv_total
        pt[pl.ds(r, KB), :] = pr
        pn[:, pl.ds(r, KB)] = pr.T.astype(BF16)
        return carry

    lax.fori_loop(0, KT // KB, prob_step, 0)
    attn = from_heads(nn(pn[...], kv[:, C : 2 * C]))
    attn_low = attn.astype(BF16)

    at_w = lambda ref: rows(ref, al(w * L, 16), L)
    att_g[pl.ds(al(w * L, 16), L), :] = attn_low

    def narrow_sum(slot, parts):
        base = new("r", N)
        for k in range(1, N):
            put(rs_st.at[slot, npeer(k)], rs_rc.at[slot, k], base + k, "narrow", npeer(k))

        def finish():
            v = rs_st[slot, n].astype(F32)
            for k in range(1, N):
                got(rs_rc.at[slot, k], base + k)
                v = v + rs_rc[slot, k].astype(F32)
            return v

        return finish

    def stage(slot, cols, v):
        for i in range(N):
            rs_st[slot, i, :, cols] = v[i * Lo : (i + 1) * Lo].astype(BF16)

    for d in (o_fin,):
        d()

    def branch_step(j, carry):
        r = al(j * 256, 256)
        stage(0, pl.ds(r, 256), nt(attn_low, wot[pl.ds(r, 256), :]))
        return carry

    lax.fori_loop(0, D // 256, branch_step, 0)
    branch_fin = narrow_sum(0, None)
    att_fwd, att_fin = wide_gather(at_w(att_g), att_g, L)
    mid = lat + branch_fin()
    mid_mean, mid_istd, mid_hat = norm_stats(mid)
    hid_ag[n] = (mid_hat * fg_ref[...] + fb_ref[...]).astype(BF16)
    hid_fin = narrow_gather(hid_ag)
    up_in.wait()
    hid_all = hid_fin()

    own64 = pl.ds(al(w * L, 16), L)

    def ffn_step(j, carry):
        cs = pl.ds(al(j * 256, 256), 256)
        pre = nn(hid_all, up[:, cs])
        cdf = 0.5 * (1.0 + lax.erf(pre * (1.0 / math.sqrt(2.0))))
        density = jnp.exp(-0.5 * pre * pre) * (1.0 / math.sqrt(2.0 * math.pi))
        act_g[own64, cs] = (pre * cdf).astype(BF16)
        pre_g[own64, cs] = (ga[:, cs] * (cdf + pre * density)).astype(BF16)
        return carry

    lax.fori_loop(0, F // 256, ffn_step, 0)
    gpre = pre_g[own64, :]

    def hid_back(j, carry):
        r = al(j * 256, 256)
        stage(1, pl.ds(r, 256), nt(gpre, up[pl.ds(r, 256), :]))
        return carry

    lax.fori_loop(0, D // 256, hid_back, 0)
    ghid_fin = narrow_sum(1, None)
    act_fwd, act_fin = wide_gather(at_w(act_g), act_g, L)
    pre_fwd, pre_fin = wide_gather(at_w(pre_g), pre_g, L)
    act_own = act_g[own64, :]

    def ffn_out(j, carry):
        cs = pl.ds(al(j * 256, 256), 256)
        stage(2, cs, nn(act_own, down[:, cs]))
        return carry

    lax.fori_loop(0, D // 256, ffn_out, 0)
    ffn_fin = narrow_sum(2, None)
    shid_fin = spread(2, hid_all)

    ghid = ghid_fin()
    grad_mid = cot_ref[...].astype(F32) + norm_back(ghid, mid_hat, mid_istd, fg_ref[...])
    gb_ag[n] = grad_mid.astype(BF16)
    gb_fin = narrow_gather(gb_ag)
    acc8[...] = jnp.zeros_like(acc8)
    stat[...] = jnp.zeros_like(stat)
    stat[FRAMES_MAX + 4 : FRAMES_MAX + 5, :] = jnp.sum(ghid * mid_hat, axis=0, keepdims=True)
    stat[FRAMES_MAX + 5 : FRAMES_MAX + 6, :] = jnp.sum(ghid, axis=0, keepdims=True)
    for k in range(1, W2):
        att_fwd(k)
    for k in range(1, W):
        got(cnt_ag.at[wsrc(k)], cnt_base + k)
    keys = cnt_ag[0]
    for i in range(1, W):
        keys = keys + cnt_ag[i]
    ent1 = ENT_COEF * float(W * M) / keys[0:1, :]
    ent = jnp.concatenate([ent1] * (R // LANES), axis=1)
    gb_all = gb_fin()

    g_attn = nn(gb_all, wot[...]).astype(BF16).astype(F32)
    g_big32 = per_head(g_attn)
    g_big = g_big32.astype(BF16)
    g_big_t = g_big32.T.astype(BF16)
    row_dot = jnp.sum(per_head(g_attn * attn).T, axis=0, keepdims=True)
    shift = row_dot - ent * mean_score

    def back_step(j, carry):
        r = al(j * KB, KB)
        pr = pt[pl.ds(r, KB), :]
        gp = nn(kv[pl.ds(r, KB), C : 2 * C], g_big_t)
        gs = pr * (gp - ent * st[pl.ds(r, KB), :] - shift)
        pn[:, pl.ds(r, KB)] = gs.T.astype(BF16)
        gpair[pl.ds(r, KB), 0:C] = (nn(gs.astype(BF16), q_big) * scale).astype(BF16)
        gpair[pl.ds(r, KB), C : 2 * C] = nn(pr.astype(BF16), g_big).astype(BF16)
        return carry

    lax.fori_loop(0, KT // KB, back_step, 0)

    mate_base = new("r", X * NC)
    xs_base = new("r", X * NC)

    def part(block, c):
        r = al(block * Mo + c * CH, 16)
        return nt(gpair[pl.ds(r, CH), :], kvw[...])

    def x_of(j):
        return lax.rem(xpos + j, X)

    def to_mate(j, c):
        b = x_of(j) * 2 + 1 - core
        mate_st[(j * NC + c) * CH : (j * NC + c + 1) * CH, :] = part(b, c).astype(BF16)
        piece = lambda ref: rows(ref, (j * NC + c) * CH, CH)
        put(piece(mate_st), piece(mate_rc), mate_base + j * NC + c, "narrow", mate)

    def from_mate(j, c):
        i = (j * NC + c) * CH
        got(rows(mate_rc, i, CH), mate_base + j * NC + c)
        return part(x_of(j) * 2 + core, c) + mate_rc[i : i + CH, :].astype(F32)

    for j in range(1, X):
        for c in range(NC):
            to_mate(j, c)
        for c in range(NC):
            i = ((j - 1) * NC + c) * CH
            x_st[i : i + CH, :] = from_mate(j, c).astype(BF16)
            put(
                rows(x_st, i, CH), rows(x_rc, i, CH), xs_base + (j - 1) * NC + c,
                "narrow", x_of(j) * 2 + core,
            )
    for k in range(1, W2):
        act_fwd(k)
        pre_fwd(k)

    gq = (from_heads(nn(pn[...], kv[:, 0:C])) * scale).astype(BF16)
    gq_g[own64, :] = gq
    gpl = gpair[M : M + L, :]

    def lat_back(j, carry):
        r = al(j * 256, 256)
        stage(3, pl.ds(r, 256), nt(gpl, kvw[pl.ds(r, 256), :]) + nt(gq, wq[pl.ds(r, 256), :]))
        return carry

    lax.fori_loop(0, D // 256, lat_back, 0)
    glat_fin = narrow_sum(3, None)
    gq_fwd, gq_fin = wide_gather(at_w(gq_g), gq_g, L)
    sgb_fin = spread(3, gb_all)

    def kvg_step(j, carry):
        r = al(j * 256, 256)
        kvg[pl.ds(r, 256), :] = tn(x_all[:, pl.ds(r, 256)], gpair[...]).astype(BF16)
        return carry

    lax.fori_loop(0, D // 256, kvg_step, 0)
    y_base = new("r", W2)
    z_base = new("r", W2)
    kb = lambda g, q: rows(kvg, al((2 * g + q) * S, 16), S)
    for g in range(W2):
        put(kb(g, 1 - par), rows(kvg_y, g * S, S), y_base + g, "wide", partner)

    for c in range(NC):
        to_mate(0, c)
    for c in range(NC):
        own_sum[c * CH : (c + 1) * CH, :] = from_mate(0, c)

    half = lax.div(w, 2)
    for k in list(range(1, W2)) + [0]:
        g = lax.rem(half + k, W2)
        yr = rows(kvg_y, al(g * S, 16), S)
        got(yr, y_base) if W2 == 1 else None
        if W2 > 1:
            pltpu.make_async_remote_copy(
                yr, yr, ssem.at[0], rsem.at[y_base + g], device_id={"narrow": mate}, device_id_type=MESH
            ).wait_recv()
        mine = pl.ds(al((2 * g + par) * S, 16), S)
        summed = kvg[mine, :].astype(F32) + kvg_y[pl.ds(al(g * S, 16), S), :].astype(F32)
        if k:
            kvg[mine, :] = summed.astype(BF16)
            put(rows(kvg, al((2 * g + par) * S, 16), S), rows(kvg_z, k * S, S), z_base + k, "wide", 2 * g + par)
        else:
            o_kv[...] = summed

    out_l = (mid + ffn_fin()).astype(BF16)
    lat_nf[0] = out_l
    here(lat_nf.at[0], out_lat)
    glat = glat_fin()
    g_lat = grad_mid + norm_back(glat, lat_hat, lat_istd, lg_ref[...])
    lat_nf[1] = g_lat.astype(BF16)
    here(lat_nf.at[1], out_gl)
    stat[FRAMES_MAX + 2 : FRAMES_MAX + 3, :] = jnp.sum(glat * lat_hat, axis=0, keepdims=True)
    stat[FRAMES_MAX + 3 : FRAMES_MAX + 4, :] = jnp.sum(glat, axis=0, keepdims=True)

    for k in range(1, W2):
        gq_fwd(k)
    att_fin()
    sgb_fin()
    o_o[...] = tn(att_g[...], sl_rc[3])
    here(o_o, out_o)
    act_fin()
    scot_fin()

    def down_step(j, carry):
        r = al(j * 256, 256)
        o_down[pl.ds(r, 256), :] = tn(act_g[:, pl.ds(r, 256)], sl_rc[1])
        return carry

    lax.fori_loop(0, F // 256, down_step, 0)
    here(o_down, out_down)
    pre_fin()
    shid_fin()

    def up_step(j, carry):
        cs = pl.ds(al(j * 256, 256), 256)
        o_up[:, cs] = tn(sl_rc[2], pre_g[:, cs])
        return carry

    lax.fori_loop(0, F // 256, up_step, 0)
    here(o_up, out_up)
    gq_fin()
    slat_fin()
    o_q[...] = tn(sl_rc[0], gq_g[...])
    here(o_q, out_q)

    gm_out = []
    for c in range(NC):
        for j in range(1, X):
            i = ((j - 1) * NC + c) * CH
            got(rows(x_rc, i, CH), xs_base + (j - 1) * NC + c)
        f = frame_of(c)
        te_row = te32[pl.ds(f, 1), :]

        def back_rows(i, carry, c=c, te_row=te_row):
            r = al(c * CH + i * 16, 16)
            dy = own_sum[pl.ds(r, 16), :]
            for j in range(1, X):
                dy = dy + x_rc[pl.ds(al((j - 1) * Mo + r, 16), 16), :].astype(F32)
            mean = mean_s[pl.ds(r, 16), 0:1]
            inv_std = istd_s[pl.ds(r, 16), 0:1]
            hat = (media[pl.ds(r, 16), :].astype(F32) + te_row - mean) * inv_std
            dx = norm_back(dy, hat, inv_std, gain_m)
            media[pl.ds(r, 16), :] = dx.astype(BF16)
            acc8[0:8, :] += fold8(dy * hat)
            acc8[8:16, :] += fold8(dy)
            acc8[16:24, :] += fold8(dx)
            return carry

        lax.fori_loop(0, CH // 16, back_rows, 0)
        stat[pl.ds(f, 1), :] += jnp.sum(acc8[16:24, :], axis=0, keepdims=True)
        acc8[16:24, :] = jnp.zeros((8, D), F32)
        here(rows(media, c * CH, CH), rows(out_gm, c * CH, CH))
    stat[FRAMES_MAX : FRAMES_MAX + 1, :] = jnp.sum(acc8[0:8, :], axis=0, keepdims=True)
    stat[FRAMES_MAX + 1 : FRAMES_MAX + 2, :] = jnp.sum(acc8[8:16, :], axis=0, keepdims=True)

    vec = stat[...]
    for b in range(W):
        vec_st[b] = vec[:, b * S : (b + 1) * S]
    v_base = new("r", W)
    for k in range(1, W):
        put(vec_st.at[wpeer(k)], vec_rc.at[k], v_base + k, "wide", wpeer(k))
    for k in range(1, W2):
        got(rows(kvg_z, k * S, S), z_base + k)
        o_kv[...] += kvg_z[k * S : (k + 1) * S, :].astype(F32)
    here(o_kv, out_kv)
    vs = vec_st[w]
    for k in range(1, W):
        got(vec_rc.at[k], v_base + k)
        vs = vs + vec_rc[k]
    for i in range(N):
        vec2_st[i] = vs[:, i * V : (i + 1) * V]
    v2_base = new("r", N)
    for k in range(1, N):
        put(vec2_st.at[npeer(k)], vec2_rc.at[k], v2_base + k, "narrow", npeer(k))
    vs = vec2_st[n]
    for k in range(1, N):
        got(vec2_rc.at[k], v2_base + k)
        vs = vs + vec2_rc[k]
    o_vec[...] = vs
    here(o_vec, out_vec)

    for d in sends:
        d.wait_send()
    for d in local:
        d.wait()
    sem_counts.update(counters)


def make_body(mesh):
    def body(
        media_feats, latents, frame_counts, media_mask, time_embed, media_gain, media_bias, latent_gain,
        latent_bias, ffn_gain, ffn_bias, query_weight, keyval_weight, output_weight, up_weight,
        down_weight, cotangent,
    ):
        p = Plan(mesh, media_feats, latents, up_weight)
        D, C, S, L, Lo, KT, R, F, N, W, Mo = p.D, p.C, p.S, p.L, p.Lo, p.KT, p.R, p.F, p.N, p.W, p.Mo
        X, W2, NC, V = p.X, p.W2, p.NC, p.V
        vm = pl.BlockSpec(memory_space=pltpu.VMEM)
        hbm = pl.BlockSpec(memory_space=pl.ANY)
        smem = pl.BlockSpec(memory_space=pltpu.SMEM)
        row = lambda v: v.reshape(1, D)
        sds = jax.ShapeDtypeStruct
        vmem = pltpu.VMEM
        scratch = [
            vmem((Mo, D), BF16),
            vmem((KT, D), BF16),
            vmem((D, 2 * C), BF16),
            vmem((D, C), BF16),
            vmem((D, C), BF16),
            vmem((D, F), BF16),
            vmem((F, D), BF16),
            vmem((KT, 2 * C), BF16),
            vmem((KT, R), F32),
            vmem((KT, R), F32),
            vmem((R, KT), BF16),
            vmem((KT, 2 * C), BF16),
            vmem((KT, LANES), F32),
            vmem((FRAMES_MAX, D), F32),
            vmem((Mo, LANES), F32),
            vmem((Mo, LANES), F32),
            vmem((2, Lo, D), BF16),
            vmem((N, Lo, D), BF16),
            vmem((N, Lo, D), BF16),
            vmem((W, 8, LANES), F32),
            vmem((4, N, Lo, D), BF16),
            vmem((4, N, Lo, D), BF16),
            vmem((N, Lo, D), BF16),
            vmem((N, Lo, D), BF16),
            vmem((8, LANES) if p.reuse else (X * Mo, D), BF16),
            vmem((X * Mo, D), BF16),
            vmem((8, LANES) if p.reuse else ((X - 1) * Mo, D), BF16),
            vmem(((X - 1) * Mo, D), BF16),
            vmem((Mo, D), F32),
            vmem((D, 2 * C), BF16),
            vmem((W2 * S, 2 * C), BF16),
            vmem((W2 * S, 2 * C), BF16),
            vmem((W * L, F), BF16),
            vmem((W * L, F), BF16),
            vmem((W * L, C), BF16),
            vmem((W * L, C), BF16),
            vmem((4, W * L, S), BF16),
            vmem((4, W * L, S), BF16),
            vmem((L, F), F32),
            vmem((24, D), F32),
            vmem((16, D), F32),
            vmem((W, 16, S), F32),
            vmem((W, 16, S), F32),
            vmem((N, 16, V), F32),
            vmem((N, 16, V), F32),
            vmem((S, F), F32),
            vmem((F, S), F32),
            vmem((C, S), F32),
            vmem((S, C), F32),
            vmem((S, 2 * C), F32),
            vmem((16, V), F32),
            pltpu.SemaphoreType.DMA((24 * W + 8 * N * p.NC + 64,)),
            pltpu.SemaphoreType.DMA((24 * W + 8 * N * p.NC + 64,)),
            pltpu.SemaphoreType.DMA((64,)),
        ]
        outs = pl.pallas_call(
            functools.partial(body_kernel, p, {}),
            out_shape=(
                sds((Lo, D), BF16),
                sds((Mo, D), BF16),
                sds((Lo, D), BF16),
                sds((16, V), F32),
                sds((S, C), F32),
                sds((S, 2 * C), F32),
                sds((C, S), F32),
                sds((S, F), F32),
                sds((F, S), F32),
            ),
            in_specs=[hbm, vm, smem, vm, vm, vm, vm, vm, vm, vm, vm, hbm, hbm, vm, hbm, hbm, vm],
            out_specs=[hbm] * 9,
            scratch_shapes=scratch,
            compiler_params=pltpu.CompilerParams(
                collective_id=0, has_side_effects=True, vmem_limit_bytes=67_043_328
            ),
        )(
            media_feats[0], latents[0], frame_counts, media_mask.reshape(p.M // LANES, LANES), time_embed,
            row(media_gain), row(media_bias), row(latent_gain), row(latent_bias), row(ffn_gain), row(ffn_bias),
            query_weight, keyval_weight.reshape(S, 2 * C), output_weight, up_weight, down_weight, cotangent[0],
        )
        lat, gm, gl, vec, gq, gkv, go, gup, gdown = outs
        return (
            lat[None], gm[None], gl[None], vec[:FRAMES_MAX], vec[FRAMES_MAX], vec[FRAMES_MAX + 1],
            vec[FRAMES_MAX + 2], vec[FRAMES_MAX + 3], vec[FRAMES_MAX + 4], vec[FRAMES_MAX + 5], gq,
            gkv.reshape(S, 2, C), go, gup, gdown,
        )

    return body


def solution(mesh):
    both = P(("wide", "narrow"))
    rows = P("wide", "narrow", None)
    return jax.shard_map(
        make_body(mesh),
        mesh=mesh,
        in_specs=(
            rows, rows, P("wide"), P("wide", None), P(), P(), P(), P(), P(), P(), P(), P("wide", "narrow"),
            P("wide", None, "narrow"), P("narrow", "wide"), P(None, "narrow"), P("narrow", None), rows,
        ),
        out_specs=(
            rows, rows, rows, P(None, ("wide", "narrow")), both, both, both, both, both, both,
            P("wide", "narrow"), P("wide", None, "narrow"), P("narrow", "wide"), P("wide", "narrow"),
            P("narrow", "wide"),
        ),
        check_vma=False,
    )
```

```python
import functools
import math

import jax
import jax.numpy as jnp
from jax import lax
from jax.experimental import pallas as pl
from jax.experimental.pallas import tpu as pltpu
from jax.sharding import PartitionSpec as P

HEADS = 16
HEAD_DIM = 96
FRAMES_MAX = 8
PATCHES = 256
EPS = 1e-05
ENT_COEF = 4.0
NEG = -1e30
LANES = 128
MESH = pl.DeviceIdType.MESH
F32 = jnp.float32
BF16 = jnp.bfloat16


def nn(a, b):
    return lax.dot_general(a, b, (((1,), (0,)), ((), ())), preferred_element_type=F32)


def nt(a, b):
    return lax.dot_general(a, b, (((1,), (1,)), ((), ())), preferred_element_type=F32)


def tn(a, b):
    return lax.dot_general(a, b, (((0,), (0,)), ((), ())), preferred_element_type=F32)


def rows_mean(v):
    return jnp.mean(v, axis=-1, keepdims=True)


def norm_stats(v):
    mean = rows_mean(v)
    centered = v - mean
    inv_std = lax.rsqrt(rows_mean(centered * centered) + EPS)
    return mean, inv_std, centered * inv_std


def norm_back(dy, hat, inv_std, gain):
    scaled = dy * gain
    return inv_std * (scaled - rows_mean(scaled) - hat * rows_mean(scaled * hat))


def fold8(v):
    return jnp.sum(v.reshape(v.shape[0] // 8, 8, v.shape[1]), axis=0)


class Plan:
    def __init__(self, mesh, media, latents, up):
        self.N = mesh.shape["narrow"]
        self.W = mesh.shape["wide"]
        self.X = self.N // 2
        self.W2 = self.W // 2
        self.Mo, self.D = media.shape[1], media.shape[2]
        self.Lo = latents.shape[1]
        self.M = self.Mo * self.N
        self.L = self.Lo * self.N
        self.HL = HEADS // self.N
        self.C = self.HL * HEAD_DIM
        self.KT = self.M + -(-self.L // LANES) * LANES
        self.F = up.shape[1]
        self.S = self.D // self.W
        self.V = self.S // self.N
        self.R = self.HL * self.L
        self.CH = 128
        self.NC = self.Mo // self.CH
        self.reuse = self.F == self.D and self.X * self.Mo <= self.D


def body_kernel(p, sem_counts, *refs):
    (
        media_h, lat_ref, fc_ref, mm_ref, te_ref, mg_ref, mb_ref, lg_ref, lb_ref, fg_ref, fb_ref,
        wq_h, wkv_ref, wot_h, up_h, down_h, cot_ref,
        out_lat, out_gm, out_gl, out_vec, out_q, out_kv, out_o, out_up, out_down,
        media, x_all, kvw, wq, wot, up, down, kv, st, pt, pn, gpair, mt, te32, mean_s, istd_s,
        lat_nf, lat_ag, cot_ag, cnt_ag,
        rs_st, rs_rc, hid_ag, gb_ag, mate_st, mate_rc, x_st, x_rc, own_sum,
        kvg, kvg_y, kvg_z, act_g, pre_g, att_g, gq_g, sl_st, sl_rc, ga, acc8, stat, vec_st, vec_rc, vec2_st, vec2_rc,
        o_up, o_down, o_o, o_q, o_kv, o_vec, ssem, rsem, lsem,
    ) = refs
    N, W, X, W2 = p.N, p.W, p.X, p.W2
    Mo, Lo, M, L, D, C, R, S, F, KT = p.Mo, p.Lo, p.M, p.L, p.D, p.C, p.R, p.S, p.F, p.KT
    CH, NC, HL, V = p.CH, p.NC, p.HL, p.V
    n = lax.axis_index("narrow")
    w = lax.axis_index("wide")
    core = lax.rem(n, 2)
    xpos = lax.div(n, 2)
    mate = n + 1 - 2 * core
    par = lax.rem(w, 2)
    partner = w + 1 - 2 * par
    scale = HEAD_DIM ** (-0.5)
    gain_m, bias_m, gain_l, bias_l, gain_f, bias_f = (
        ref[...].reshape(1, D) for ref in (mg_ref, mb_ref, lg_ref, lb_ref, fg_ref, fb_ref)
    )

    if p.reuse:
        mate_st, x_st = up, down

    counters = {"s": 0, "r": 0, "l": 0}
    sends = []
    local = []

    def new(kind, count=1):
        base = counters[kind]
        counters[kind] = base + count
        return base

    def put(src, dst, recv, axis, peer):
        d = pltpu.make_async_remote_copy(
            src, dst, ssem.at[new("s")], rsem.at[recv], device_id={axis: peer}, device_id_type=MESH
        )
        d.start()
        sends.append(d)

    def got(dst, recv):
        pltpu.make_async_remote_copy(
            dst, dst, ssem.at[0], rsem.at[recv], device_id={"narrow": mate}, device_id_type=MESH
        ).wait_recv()

    def here(src, dst, keep=True):
        d = pltpu.make_async_copy(src, dst, lsem.at[new("l")])
        d.start()
        if keep:
            local.append(d)
        return d

    def rows(ref, start, count):
        return ref.at[pl.ds(start, count), :]

    def al(v, m):
        return pl.multiple_of(v, m)

    def npeer(k):
        return lax.rem(n + k, N)

    def nsrc(k):
        return lax.rem(n + N - k, N)

    def wpeer(k):
        return lax.rem(w + k, W)

    def wsrc(k):
        return lax.rem(w + W - k, W)

    media_in = [here(rows(media_h, c * CH, CH), rows(media, c * CH, CH), False) for c in range(NC)]
    down_in = here(down_h, down, False)
    up_in = here(up_h, up, False)

    wkv = wkv_ref[...].astype(F32)
    kvw[pl.ds(al(w * S, 16), S), 0:C] = wkv[:, 0, :].astype(BF16)
    kvw[pl.ds(al(w * S, 16), S), C : 2 * C] = wkv[:, 1, :].astype(BF16)

    barrier = pltpu.get_barrier_semaphore()
    for k in range(1, N):
        pl.semaphore_signal(barrier, inc=1, device_id={"narrow": npeer(k)}, device_id_type=MESH)
    for k in range(1, W):
        pl.semaphore_signal(barrier, inc=1, device_id={"wide": wpeer(k)}, device_id_type=MESH)
    pl.semaphore_wait(barrier, N - 1 + W - 1)

    def wide_gather(src, buf, count):
        at = lambda b: rows(buf, al(b * count, 16), count)
        direct = new("r", W2)
        fwd = new("r", W2)
        for k in range(1, W2):
            put(src, at(w), direct + k, "wide", wpeer(2 * k))
        put(src, at(w), direct, "wide", partner)

        def forward(k):
            b = wsrc(2 * k)
            got(at(b), direct + k)
            put(at(b), at(b), fwd + k, "wide", partner)

        def finish():
            got(at(partner), direct)
            for k in range(1, W2):
                b = lax.rem(partner + W - 2 * k, W)
                got(at(b), fwd + k)

        return forward, finish

    own_w = [
        here(wq_h, rows(wq, al(w * S, 16), S), False),
        here(wot_h, rows(wot, al(w * S, 16), S), False),
    ]
    kv_fwd, kv_fin = wide_gather(rows(kvw, al(w * S, 16), S), kvw, S)
    q_fwd, q_fin = wide_gather(wq_h, wq, S)
    o_fwd, o_fin = wide_gather(wot_h, wot, S)

    lat = lat_ref[...].astype(F32)
    lat_mean, lat_istd, lat_hat = norm_stats(lat)
    lat_ag[n] = (lat_hat * gain_l + bias_l).astype(BF16)
    cot_ag[n] = cot_ref[...]

    def narrow_gather(buf):
        base = new("r", N)
        for k in range(1, N):
            put(buf.at[n], buf.at[n], base + k, "narrow", npeer(k))

        def finish():
            for k in range(1, N):
                got(buf.at[nsrc(k)], base + k)
            return jnp.concatenate([buf[i].astype(F32) for i in range(N)], axis=0).astype(BF16)

        return finish

    te32[...] = te_ref[...].astype(F32)

    m_direct = new("r", NC * X)
    m_fwd = new("r", NC * X)

    def m_rows(block, c):
        return rows(x_all, al(block * Mo + c * CH, 16), CH)

    def frame_of(c):
        return lax.div(n * Mo + c * CH, PATCHES)

    for c in range(NC):
        media_in[c].wait()
        te_row = te32[pl.ds(frame_of(c), 1), :]

        def norm_rows(i, carry, c=c, te_row=te_row):
            r = al(c * CH + i * 16, 16)
            v = media[pl.ds(r, 16), :].astype(F32) + te_row
            mean, inv_std, hat = norm_stats(v)
            mean_s[pl.ds(r, 16), :] = jnp.broadcast_to(mean, (16, LANES))
            istd_s[pl.ds(r, 16), :] = jnp.broadcast_to(inv_std, (16, LANES))
            x_all[pl.ds(al(n * Mo + r, 16), 16), :] = (hat * gain_m + bias_m).astype(BF16)
            return carry

        lax.fori_loop(0, CH // 16, norm_rows, 0, unroll=2)
        for j in range(1, X):
            peer = lax.rem(xpos + j, X) * 2 + core
            put(m_rows(n, c), m_rows(n, c), m_direct + c * X + j, "narrow", peer)
        put(m_rows(n, c), m_rows(n, c), m_direct + c * X, "narrow", mate)
        if c == 0:
            lat_fin = narrow_gather(lat_ag)
            cot_fin = narrow_gather(cot_ag)

    def media_forward(c):
        for j in range(1, X):
            block = lax.rem(xpos + X - j, X) * 2 + core
            got(m_rows(block, c), m_direct + c * X + j)
            put(m_rows(block, c), m_rows(block, c), m_fwd + c * X + j, "narrow", mate)

    slot_frame = lax.div(lax.broadcasted_iota(jnp.int32, (M // LANES, LANES), 0), PATCHES // LANES)
    ok = (slot_frame < fc_ref[0]) & (mm_ref[...] > 0)
    okf = jnp.where(ok, 1.0, 0.0).astype(F32)
    tail = jnp.where(
        lax.broadcasted_iota(jnp.int32, (1, KT - M), 1) < L, 1.0, 0.0
    ).astype(F32)
    for j in range(KT // LANES):
        row = okf[j : j + 1, :] if j < M // LANES else tail[:, j * LANES - M : j * LANES - M + LANES]
        mt[j * LANES : (j + 1) * LANES, :] = jnp.broadcast_to(row, (LANES, LANES)).T
    count = jnp.sum(okf, keepdims=True) + float(L)
    cnt_ag[w] = jnp.broadcast_to(count, (8, LANES))
    cnt_base = new("r", W)
    for k in range(1, W):
        put(cnt_ag.at[w], cnt_ag.at[w], cnt_base + k, "wide", wpeer(k))

    kv_fwd(1)
    for k in range(2, W2):
        kv_fwd(k)
    media_forward(0)

    def spread(which, value):
        for b in range(W):
            sl_st[which, b * L : (b + 1) * L, :] = value[:, b * S : (b + 1) * S]
        base = new("r", W)
        at = lambda ref, b: ref.at[which, pl.ds(al(b * L, 16), L), :]
        for k in range(1, W):
            put(at(sl_st, wpeer(k)), at(sl_rc, w), base + k, "wide", wpeer(k))
        sl_rc[which, pl.ds(al(w * L, 16), L), :] = sl_st[which, pl.ds(al(w * L, 16), L), :]

        def finish():
            for k in range(1, W):
                got(at(sl_rc, wsrc(k)), base + k)

        return finish

    lat_all = lat_fin()
    cot_all = cot_fin()
    x_all[M : M + L, :] = lat_all
    if KT > M + L:
        x_all[M + L : KT, :] = jnp.zeros((KT - M - L, D), BF16)
    slat_fin = spread(0, lat_all)
    scot_fin = spread(1, cot_all)

    down_in.wait()

    def act_grad(j, carry):
        r = al(j * 256, 256)
        ga[:, pl.ds(r, 256)] = nt(cot_all, down[pl.ds(r, 256), :])
        return carry

    lax.fori_loop(0, F // 256, act_grad, 0)

    for k in range(1, W2):
        q_fwd(k)
    if NC > 1:
        media_forward(1)
    for d in own_w:
        d.wait()
    kv_fin()

    def project(start, count):
        def step(i, carry):
            r = al(start + i * CH, 16)
            kv[pl.ds(r, CH), :] = nn(x_all[pl.ds(r, CH), :], kvw[...]).astype(BF16)
            return carry

        lax.fori_loop(0, count // CH, step, 0)

    project(n * Mo, Mo)
    project(M, KT - M)
    for k in range(1, W2):
        o_fwd(k)
    for c in range(NC):
        got(m_rows(mate, c), m_direct + c * X)
    project(mate * Mo, Mo)
    q_fin()
    q_act = nn(lat_all, wq[...]).astype(BF16).astype(F32)
    head_of = lax.div(lax.broadcasted_iota(jnp.int32, (L, C), 1), HEAD_DIM)

    def per_head(v):
        return jnp.concatenate([jnp.where(head_of == h, v, 0.0) for h in range(HL)], axis=0)

    def from_heads(v):
        total = jnp.where(head_of == 0, v[0:L], 0.0)
        for h in range(1, HL):
            total = total + jnp.where(head_of == h, v[h * L : (h + 1) * L], 0.0)
        return total

    q_big32 = per_head(q_act)
    q_big = q_big32.astype(BF16)
    q_big_t = q_big32.T.astype(BF16)
    for c in range(2, NC):
        media_forward(c)
    for c in range(NC):
        for j in range(1, X):
            block = lax.rem(xpos + X - j, X) * 2 + core
            project(block * Mo + c * CH, CH)
            block = lax.rem(xpos + X - j, X) * 2 + 1 - core
            got(m_rows(block, c), m_fwd + c * X + j)
            project(block * Mo + c * CH, CH)

    KB = 128

    def wide_mask(r):
        m = mt[pl.ds(r, KB), :]
        return jnp.concatenate([m] * (R // LANES), axis=1) > 0.0

    def score_step(j, top):
        r = al(j * KB, KB)
        s = nn(kv[pl.ds(r, KB), 0:C], q_big_t) * scale
        s = jnp.where(wide_mask(r), s, NEG)
        st[pl.ds(r, KB), :] = s
        return jnp.maximum(top, jnp.max(s, axis=0, keepdims=True))

    top = lax.fori_loop(0, KT // KB, score_step, jnp.full((1, R), NEG, F32))

    def exp_step(j, carry):
        total, dot = carry
        r = al(j * KB, KB)
        s = st[pl.ds(r, KB), :]
        e = jnp.exp(s - top)
        pt[pl.ds(r, KB), :] = e
        s = jnp.where(wide_mask(r), s, 0.0)
        st[pl.ds(r, KB), :] = s
        return (
            total + jnp.sum(e, axis=0, keepdims=True),
            dot + jnp.sum(e * s, axis=0, keepdims=True),
        )

    zero_row = jnp.zeros((1, R), F32)
    total, dot = lax.fori_loop(0, KT // KB, exp_step, (zero_row, zero_row))
    inv_total = 1.0 / total
    mean_score = dot * inv_total

    def prob_step(j, carry):
        r = al(j * KB, KB)
        pr = pt[pl.ds(r, KB), :] * inv_total
        pt[pl.ds(r, KB), :] = pr
        pn[:, pl.ds(r, KB)] = pr.T.astype(BF16)
        return carry

    lax.fori_loop(0, KT // KB, prob_step, 0)
    attn = from_heads(nn(pn[...], kv[:, C : 2 * C]))
    attn_low = attn.astype(BF16)

    at_w = lambda ref: rows(ref, al(w * L, 16), L)
    att_g[pl.ds(al(w * L, 16), L), :] = attn_low

    def narrow_sum(slot, parts):
        base = new("r", N)
        for k in range(1, N):
            put(rs_st.at[slot, npeer(k)], rs_rc.at[slot, k], base + k, "narrow", npeer(k))

        def finish():
            v = rs_st[slot, n].astype(F32)
            for k in range(1, N):
                got(rs_rc.at[slot, k], base + k)
                v = v + rs_rc[slot, k].astype(F32)
            return v

        return finish

    def stage(slot, cols, v):
        for i in range(N):
            rs_st[slot, i, :, cols] = v[i * Lo : (i + 1) * Lo].astype(BF16)

    for d in (o_fin,):
        d()

    def branch_step(j, carry):
        r = al(j * 256, 256)
        stage(0, pl.ds(r, 256), nt(attn_low, wot[pl.ds(r, 256), :]))
        return carry

    lax.fori_loop(0, D // 256, branch_step, 0)
    branch_fin = narrow_sum(0, None)
    att_fwd, att_fin = wide_gather(at_w(att_g), att_g, L)
    mid = lat + branch_fin()
    mid_mean, mid_istd, mid_hat = norm_stats(mid)
    hid_ag[n] = (mid_hat * gain_f + bias_f).astype(BF16)
    hid_fin = narrow_gather(hid_ag)
    up_in.wait()
    hid_all = hid_fin()

    own64 = pl.ds(al(w * L, 16), L)

    def ffn_step(j, carry):
        cs = pl.ds(al(j * 256, 256), 256)
        pre = nn(hid_all, up[:, cs])
        cdf = 0.5 * (1.0 + lax.erf(pre * (1.0 / math.sqrt(2.0))))
        density = jnp.exp(-0.5 * pre * pre) * (1.0 / math.sqrt(2.0 * math.pi))
        act_g[own64, cs] = (pre * cdf).astype(BF16)
        pre_g[own64, cs] = (ga[:, cs] * (cdf + pre * density)).astype(BF16)
        return carry

    lax.fori_loop(0, F // 256, ffn_step, 0)
    gpre = pre_g[own64, :]

    def hid_back(j, carry):
        r = al(j * 256, 256)
        stage(1, pl.ds(r, 256), nt(gpre, up[pl.ds(r, 256), :]))
        return carry

    lax.fori_loop(0, D // 256, hid_back, 0)
    ghid_fin = narrow_sum(1, None)
    act_fwd, act_fin = wide_gather(at_w(act_g), act_g, L)
    pre_fwd, pre_fin = wide_gather(at_w(pre_g), pre_g, L)
    act_own = act_g[own64, :]

    def ffn_out(j, carry):
        cs = pl.ds(al(j * 256, 256), 256)
        stage(2, cs, nn(act_own, down[:, cs]))
        return carry

    lax.fori_loop(0, D // 256, ffn_out, 0)
    ffn_fin = narrow_sum(2, None)
    shid_fin = spread(2, hid_all)

    ghid = ghid_fin()
    grad_mid = cot_ref[...].astype(F32) + norm_back(ghid, mid_hat, mid_istd, gain_f)
    gb_ag[n] = grad_mid.astype(BF16)
    gb_fin = narrow_gather(gb_ag)
    acc8[...] = jnp.zeros_like(acc8)
    stat[...] = jnp.zeros_like(stat)
    stat[FRAMES_MAX + 4 : FRAMES_MAX + 5, :] = jnp.sum(ghid * mid_hat, axis=0, keepdims=True)
    stat[FRAMES_MAX + 5 : FRAMES_MAX + 6, :] = jnp.sum(ghid, axis=0, keepdims=True)
    for k in range(1, W2):
        att_fwd(k)
    for k in range(1, W):
        got(cnt_ag.at[wsrc(k)], cnt_base + k)
    keys = cnt_ag[0]
    for i in range(1, W):
        keys = keys + cnt_ag[i]
    ent1 = ENT_COEF * float(W * M) / keys[0:1, :]
    ent = jnp.concatenate([ent1] * (R // LANES), axis=1)
    gb_all = gb_fin()

    g_attn = nn(gb_all, wot[...]).astype(BF16).astype(F32)
    g_big32 = per_head(g_attn)
    g_big = g_big32.astype(BF16)
    g_big_t = g_big32.T.astype(BF16)
    row_dot = jnp.sum(per_head(g_attn * attn).T, axis=0, keepdims=True)
    shift = row_dot - ent * mean_score

    def back_step(j, carry):
        r = al(j * KB, KB)
        pr = pt[pl.ds(r, KB), :]
        gp = nn(kv[pl.ds(r, KB), C : 2 * C], g_big_t)
        gs = pr * (gp - ent * st[pl.ds(r, KB), :] - shift)
        pn[:, pl.ds(r, KB)] = gs.T.astype(BF16)
        gpair[pl.ds(r, KB), 0:C] = (nn(gs.astype(BF16), q_big) * scale).astype(BF16)
        gpair[pl.ds(r, KB), C : 2 * C] = nn(pr.astype(BF16), g_big).astype(BF16)
        return carry

    lax.fori_loop(0, KT // KB, back_step, 0)

    mate_base = new("r", X * NC)
    xs_base = new("r", X * NC)

    def part(block, c):
        r = al(block * Mo + c * CH, 16)
        return nt(gpair[pl.ds(r, CH), :], kvw[...])

    def x_of(j):
        return lax.rem(xpos + j, X)

    def to_mate(j, c):
        b = x_of(j) * 2 + 1 - core
        mate_st[(j * NC + c) * CH : (j * NC + c + 1) * CH, :] = part(b, c).astype(BF16)
        piece = lambda ref: rows(ref, (j * NC + c) * CH, CH)
        put(piece(mate_st), piece(mate_rc), mate_base + j * NC + c, "narrow", mate)

    def from_mate(j, c):
        i = (j * NC + c) * CH
        got(rows(mate_rc, i, CH), mate_base + j * NC + c)
        return part(x_of(j) * 2 + core, c) + mate_rc[i : i + CH, :].astype(F32)

    for j in range(1, X):
        for c in range(NC):
            to_mate(j, c)
        for c in range(NC):
            i = ((j - 1) * NC + c) * CH
            x_st[i : i + CH, :] = from_mate(j, c).astype(BF16)
            put(
                rows(x_st, i, CH), rows(x_rc, i, CH), xs_base + (j - 1) * NC + c,
                "narrow", x_of(j) * 2 + core,
            )
    for k in range(1, W2):
        act_fwd(k)
        pre_fwd(k)

    gq = (from_heads(nn(pn[...], kv[:, 0:C])) * scale).astype(BF16)
    gq_g[own64, :] = gq
    gpl = gpair[M : M + L, :]

    def lat_back(j, carry):
        r = al(j * 256, 256)
        stage(3, pl.ds(r, 256), nt(gpl, kvw[pl.ds(r, 256), :]) + nt(gq, wq[pl.ds(r, 256), :]))
        return carry

    lax.fori_loop(0, D // 256, lat_back, 0)
    glat_fin = narrow_sum(3, None)
    gq_fwd, gq_fin = wide_gather(at_w(gq_g), gq_g, L)
    sgb_fin = spread(3, gb_all)

    def kvg_step(j, carry):
        r = al(j * 256, 256)
        kvg[pl.ds(r, 256), :] = tn(x_all[:, pl.ds(r, 256)], gpair[...]).astype(BF16)
        return carry

    lax.fori_loop(0, D // 256, kvg_step, 0)
    y_base = new("r", W2)
    z_base = new("r", W2)
    kb = lambda g, q: rows(kvg, al((2 * g + q) * S, 16), S)
    for g in range(W2):
        put(kb(g, 1 - par), rows(kvg_y, g * S, S), y_base + g, "wide", partner)

    for c in range(NC):
        to_mate(0, c)
    for c in range(NC):
        own_sum[c * CH : (c + 1) * CH, :] = from_mate(0, c)

    half = lax.div(w, 2)
    for k in list(range(1, W2)) + [0]:
        g = lax.rem(half + k, W2)
        yr = rows(kvg_y, al(g * S, 16), S)
        got(yr, y_base) if W2 == 1 else None
        if W2 > 1:
            pltpu.make_async_remote_copy(
                yr, yr, ssem.at[0], rsem.at[y_base + g], device_id={"narrow": mate}, device_id_type=MESH
            ).wait_recv()
        mine = pl.ds(al((2 * g + par) * S, 16), S)
        summed = kvg[mine, :].astype(F32) + kvg_y[pl.ds(al(g * S, 16), S), :].astype(F32)
        if k:
            kvg[mine, :] = summed.astype(BF16)
            put(rows(kvg, al((2 * g + par) * S, 16), S), rows(kvg_z, k * S, S), z_base + k, "wide", 2 * g + par)
        else:
            o_kv[...] = summed

    out_l = (mid + ffn_fin()).astype(BF16)
    lat_nf[0] = out_l
    here(lat_nf.at[0], out_lat)
    glat = glat_fin()
    g_lat = grad_mid + norm_back(glat, lat_hat, lat_istd, gain_l)
    lat_nf[1] = g_lat.astype(BF16)
    here(lat_nf.at[1], out_gl)
    stat[FRAMES_MAX + 2 : FRAMES_MAX + 3, :] = jnp.sum(glat * lat_hat, axis=0, keepdims=True)
    stat[FRAMES_MAX + 3 : FRAMES_MAX + 4, :] = jnp.sum(glat, axis=0, keepdims=True)

    for k in range(1, W2):
        gq_fwd(k)
    att_fin()
    sgb_fin()
    o_o[...] = tn(sl_rc[3], att_g[...])
    here(o_o, out_o)
    act_fin()
    scot_fin()

    def down_step(j, carry):
        cs = pl.ds(al(j * 256, 256), 256)
        o_down[:, cs] = tn(sl_rc[1], act_g[:, cs])
        return carry

    lax.fori_loop(0, F // 256, down_step, 0)
    here(o_down, out_down)
    pre_fin()
    shid_fin()

    def up_step(j, carry):
        cs = pl.ds(al(j * 256, 256), 256)
        o_up[:, cs] = tn(sl_rc[2], pre_g[:, cs])
        return carry

    lax.fori_loop(0, F // 256, up_step, 0)
    here(o_up, out_up)
    gq_fin()
    slat_fin()
    o_q[...] = tn(sl_rc[0], gq_g[...])
    here(o_q, out_q)

    gm_out = []
    for c in range(NC):
        for j in range(1, X):
            i = ((j - 1) * NC + c) * CH
            got(rows(x_rc, i, CH), xs_base + (j - 1) * NC + c)
        f = frame_of(c)
        te_row = te32[pl.ds(f, 1), :]

        def back_rows(i, carry, c=c, te_row=te_row):
            r = al(c * CH + i * 16, 16)
            dy = own_sum[pl.ds(r, 16), :]
            for j in range(1, X):
                dy = dy + x_rc[pl.ds(al((j - 1) * Mo + r, 16), 16), :].astype(F32)
            mean = mean_s[pl.ds(r, 16), 0:1]
            inv_std = istd_s[pl.ds(r, 16), 0:1]
            hat = (media[pl.ds(r, 16), :].astype(F32) + te_row - mean) * inv_std
            dx = norm_back(dy, hat, inv_std, gain_m)
            media[pl.ds(r, 16), :] = dx.astype(BF16)
            acc8[0:8, :] += fold8(dy * hat)
            acc8[8:16, :] += fold8(dy)
            acc8[16:24, :] += fold8(dx)
            return carry

        lax.fori_loop(0, CH // 16, back_rows, 0)
        stat[pl.ds(f, 1), :] += jnp.sum(acc8[16:24, :], axis=0, keepdims=True)
        acc8[16:24, :] = jnp.zeros((8, D), F32)
        here(rows(media, c * CH, CH), rows(out_gm, c * CH, CH))
    stat[FRAMES_MAX : FRAMES_MAX + 1, :] = jnp.sum(acc8[0:8, :], axis=0, keepdims=True)
    stat[FRAMES_MAX + 1 : FRAMES_MAX + 2, :] = jnp.sum(acc8[8:16, :], axis=0, keepdims=True)

    vec = stat[...]
    for b in range(W):
        vec_st[b] = vec[:, b * S : (b + 1) * S]
    v_base = new("r", W)
    for k in range(1, W):
        put(vec_st.at[wpeer(k)], vec_rc.at[k], v_base + k, "wide", wpeer(k))
    for k in range(1, W2):
        got(rows(kvg_z, k * S, S), z_base + k)
        o_kv[...] += kvg_z[k * S : (k + 1) * S, :].astype(F32)
    here(o_kv, out_kv)
    vs = vec_st[w]
    for k in range(1, W):
        got(vec_rc.at[k], v_base + k)
        vs = vs + vec_rc[k]
    for i in range(N):
        vec2_st[i] = vs[:, i * V : (i + 1) * V]
    v2_base = new("r", N)
    for k in range(1, N):
        put(vec2_st.at[npeer(k)], vec2_rc.at[k], v2_base + k, "narrow", npeer(k))
    vs = vec2_st[n]
    for k in range(1, N):
        got(vec2_rc.at[k], v2_base + k)
        vs = vs + vec2_rc[k]
    o_vec[...] = vs
    here(o_vec, out_vec)

    for d in sends:
        d.wait_send()
    for d in local:
        d.wait()
    sem_counts.update(counters)


def finish_kernel(p, pieces, *refs):
    src, dst, buf, sem_in, sem_out = refs[:9], refs[9:24], refs[24:33], refs[33], refs[34]
    V, C = p.V, p.C
    loads = []
    for i in range(9):
        count = src[i].shape[0] // pieces[i]
        for c in range(pieces[i]):
            at = pl.ds(c * count, count)
            d = pltpu.make_async_copy(src[i].at[at, :], buf[i].at[at, :], sem_in.at[len(loads)])
            d.start()
            loads.append((i, at, d))
    stores = []

    def store(a, b):
        d = pltpu.make_async_copy(a, b, sem_out.at[len(stores)])
        d.start()
        stores.append(d)

    first = {0: 0, 1: 1, 2: 2, 4: 10, 5: 11, 6: 12, 7: 13, 8: 14}
    for i, at, d in loads:
        d.wait()
        if i == 3:
            store(buf[3].at[pl.ds(0, FRAMES_MAX), :], dst[3])
            for k in range(6):
                store(buf[3].at[FRAMES_MAX + k], dst[4 + k])
        elif i == 5 and C % LANES == 0:
            for k in range(2):
                store(buf[5].at[:, pl.ds(k * C, C)], dst[11].at[:, k, :])
        else:
            store(buf[i].at[at, :], dst[first[i]].at[at, :])
    for d in stores:
        d.wait()


def finish(p, outs):
    sds = jax.ShapeDtypeStruct
    hbm = pl.BlockSpec(memory_space=pl.ANY)
    pieces = [1, 4, 1, 1, 1, 1, 1, 2, 2]
    shapes = [sds(a.shape, a.dtype) for a in outs]
    vec = [sds((FRAMES_MAX, p.V), F32)] + [sds((p.V,), F32)] * 6
    res = pl.pallas_call(
        functools.partial(finish_kernel, p, pieces),
        out_shape=tuple(shapes[:3] + vec + [shapes[4], sds((p.S, 2, p.C), F32) if p.C % LANES == 0 else shapes[5]] + shapes[6:]),
        in_specs=[hbm] * 9,
        out_specs=[hbm] * 15,
        scratch_shapes=[pltpu.VMEM(a.shape, a.dtype) for a in outs]
        + [pltpu.SemaphoreType.DMA((sum(pieces),)), pltpu.SemaphoreType.DMA((sum(pieces) + 7,))],
        compiler_params=pltpu.CompilerParams(has_side_effects=True),
    )(*outs)
    return res[0], res[1], res[2], res[3:10], res[10], res[11].reshape(p.S, 2, p.C), res[12], res[13], res[14]


def make_body(mesh):
    def body(
        media_feats, latents, frame_counts, media_mask, time_embed, media_gain, media_bias, latent_gain,
        latent_bias, ffn_gain, ffn_bias, query_weight, keyval_weight, output_weight, up_weight,
        down_weight, cotangent,
    ):
        p = Plan(mesh, media_feats, latents, up_weight)
        D, C, S, L, Lo, KT, R, F, N, W, Mo = p.D, p.C, p.S, p.L, p.Lo, p.KT, p.R, p.F, p.N, p.W, p.Mo
        X, W2, NC, V = p.X, p.W2, p.NC, p.V
        vm = pl.BlockSpec(memory_space=pltpu.VMEM)
        hbm = pl.BlockSpec(memory_space=pl.ANY)
        smem = pl.BlockSpec(memory_space=pltpu.SMEM)
        sds = jax.ShapeDtypeStruct
        vmem = pltpu.VMEM
        scratch = [
            vmem((Mo, D), BF16),
            vmem((KT, D), BF16),
            vmem((D, 2 * C), BF16),
            vmem((D, C), BF16),
            vmem((D, C), BF16),
            vmem((D, F), BF16),
            vmem((F, D), BF16),
            vmem((KT, 2 * C), BF16),
            vmem((KT, R), F32),
            vmem((KT, R), F32),
            vmem((R, KT), BF16),
            vmem((KT, 2 * C), BF16),
            vmem((KT, LANES), F32),
            vmem((FRAMES_MAX, D), F32),
            vmem((Mo, LANES), F32),
            vmem((Mo, LANES), F32),
            vmem((2, Lo, D), BF16),
            vmem((N, Lo, D), BF16),
            vmem((N, Lo, D), BF16),
            vmem((W, 8, LANES), F32),
            vmem((4, N, Lo, D), BF16),
            vmem((4, N, Lo, D), BF16),
            vmem((N, Lo, D), BF16),
            vmem((N, Lo, D), BF16),
            vmem((8, LANES) if p.reuse else (X * Mo, D), BF16),
            vmem((X * Mo, D), BF16),
            vmem((8, LANES) if p.reuse else ((X - 1) * Mo, D), BF16),
            vmem(((X - 1) * Mo, D), BF16),
            vmem((Mo, D), F32),
            vmem((D, 2 * C), BF16),
            vmem((W2 * S, 2 * C), BF16),
            vmem((W2 * S, 2 * C), BF16),
            vmem((W * L, F), BF16),
            vmem((W * L, F), BF16),
            vmem((W * L, C), BF16),
            vmem((W * L, C), BF16),
            vmem((4, W * L, S), BF16),
            vmem((4, W * L, S), BF16),
            vmem((L, F), F32),
            vmem((24, D), F32),
            vmem((16, D), F32),
            vmem((W, 16, S), F32),
            vmem((W, 16, S), F32),
            vmem((N, 16, V), F32),
            vmem((N, 16, V), F32),
            vmem((S, F), F32),
            vmem((S, F), F32),
            vmem((S, C), F32),
            vmem((S, C), F32),
            vmem((S, 2 * C), F32),
            vmem((16, V), F32),
            pltpu.SemaphoreType.DMA((24 * W + 8 * N * p.NC + 64,)),
            pltpu.SemaphoreType.DMA((24 * W + 8 * N * p.NC + 64,)),
            pltpu.SemaphoreType.DMA((64,)),
        ]
        outs = pl.pallas_call(
            functools.partial(body_kernel, p, {}),
            out_shape=(
                sds((Lo, D), BF16),
                sds((Mo, D), BF16),
                sds((Lo, D), BF16),
                sds((16, V), F32),
                sds((S, C), F32),
                sds((S, 2 * C), F32),
                sds((S, C), F32),
                sds((S, F), F32),
                sds((S, F), F32),
            ),
            in_specs=[hbm, vm, smem, vm, vm, vm, vm, vm, vm, vm, vm, hbm, vm, hbm, hbm, hbm, vm],
            out_specs=[hbm] * 9,
            scratch_shapes=scratch,
            compiler_params=pltpu.CompilerParams(
                collective_id=0, has_side_effects=True, vmem_limit_bytes=67_043_328
            ),
        )(
            media_feats[0], latents[0], frame_counts, media_mask.reshape(p.M // LANES, LANES), time_embed,
            media_gain, media_bias, latent_gain, latent_bias, ffn_gain, ffn_bias,
            query_weight, keyval_weight, output_weight.T, up_weight, down_weight, cotangent[0],
        )
        lat, gm, gl, vec, gq, gkv, go, gup, gdown = finish(p, outs)
        return (lat[None], gm[None], gl[None]) + tuple(vec) + (gq, gkv, go.T, gup, gdown.T)

    return body


def solution(mesh):
    both = P(("wide", "narrow"))
    rows = P("wide", "narrow", None)
    return jax.shard_map(
        make_body(mesh),
        mesh=mesh,
        in_specs=(
            rows, rows, P("wide"), P("wide", None), P(), P(), P(), P(), P(), P(), P(), P("wide", "narrow"),
            P("wide", None, "narrow"), P("narrow", "wide"), P(None, "narrow"), P("narrow", None), rows,
        ),
        out_specs=(
            rows, rows, rows, P(None, ("wide", "narrow")), both, both, both, both, both, both,
            P("wide", "narrow"), P("wide", None, "narrow"), P("narrow", "wide"), P("wide", "narrow"),
            P("narrow", "wide"),
        ),
        check_vma=False,
    )
```

```python
import functools
import math

import jax
import jax.numpy as jnp
from jax import lax
from jax.experimental import pallas as pl
from jax.experimental.pallas import tpu as pltpu
from jax.sharding import PartitionSpec as P

HEADS = 16
HEAD_DIM = 96
FRAMES_MAX = 8
PATCHES = 256
EPS = 1e-05
ENT_COEF = 4.0
NEG = -1e30
LANES = 128
MESH = pl.DeviceIdType.MESH
F32 = jnp.float32
BF16 = jnp.bfloat16


def nn(a, b):
    return lax.dot_general(a, b, (((1,), (0,)), ((), ())), preferred_element_type=F32)


def nt(a, b):
    return lax.dot_general(a, b, (((1,), (1,)), ((), ())), preferred_element_type=F32)


def tn(a, b):
    return lax.dot_general(a, b, (((0,), (0,)), ((), ())), preferred_element_type=F32)


def rows_mean(v):
    return jnp.mean(v, axis=-1, keepdims=True)


def norm_stats(v):
    mean = rows_mean(v)
    centered = v - mean
    inv_std = lax.rsqrt(rows_mean(centered * centered) + EPS)
    return mean, inv_std, centered * inv_std


def norm_back(dy, hat, inv_std, gain):
    scaled = dy * gain
    return inv_std * (scaled - rows_mean(scaled) - hat * rows_mean(scaled * hat))


def fold8(v):
    return jnp.sum(v.reshape(v.shape[0] // 8, 8, v.shape[1]), axis=0)


class Plan:
    def __init__(self, mesh, media, latents, up):
        self.N = mesh.shape["narrow"]
        self.W = mesh.shape["wide"]
        self.X = self.N // 2
        self.W2 = self.W // 2
        self.Mo, self.D = media.shape[1], media.shape[2]
        self.Lo = latents.shape[1]
        self.M = self.Mo * self.N
        self.L = self.Lo * self.N
        self.HL = HEADS // self.N
        self.C = self.HL * HEAD_DIM
        self.KT = self.M + -(-self.L // LANES) * LANES
        self.F = up.shape[1]
        self.S = self.D // self.W
        self.V = self.S // self.N
        self.R = self.HL * self.L
        self.CH = 128
        self.NC = self.Mo // self.CH


def body_kernel(p, sem_counts, *refs):
    (
        media_h, lat_ref, fc_ref, mm_ref, te_ref, mg_ref, mb_ref, lg_ref, lb_ref, fg_ref, fb_ref,
        wq_h, wkv_ref, wot_h, up_h, down_h, cot_ref,
        out_lat, out_gm, out_gl, out_vec, out_q, out_kv, out_o, out_up, out_down,
        media, x_all, kvw, wq, wot, up, down, kv, st, pt, pn, gpair, mt, te32, mean_s, istd_s,
        lat_nf, lat_ag, cot_ag, cnt_ag,
        rs_st, rs_rc, hid_ag, gb_ag, mate_st, mate_rc, x_st, x_rc, own_sum,
        kvg_y, kvg_z, act_own, pre_own, hid_g, cot_g, att_g, gq_g, sl_st, sl_rc, cot_sl, hid_sl, ga, acc8, stat, vec_st, vec_rc, vec2_st, vec2_rc,
        o_up, o_down, o_o, o_q, o_kv, o_vec, ssem, rsem, lsem,
    ) = refs
    N, W, X, W2 = p.N, p.W, p.X, p.W2
    Mo, Lo, M, L, D, C, R, S, F, KT = p.Mo, p.Lo, p.M, p.L, p.D, p.C, p.R, p.S, p.F, p.KT
    CH, NC, HL, V = p.CH, p.NC, p.HL, p.V
    n = lax.axis_index("narrow")
    w = lax.axis_index("wide")
    core = lax.rem(n, 2)
    xpos = lax.div(n, 2)
    mate = n + 1 - 2 * core
    par = lax.rem(w, 2)
    partner = w + 1 - 2 * par
    scale = HEAD_DIM ** (-0.5)
    gain_m, bias_m, gain_l, bias_l, gain_f, bias_f = (
        ref[...].reshape(1, D) for ref in (mg_ref, mb_ref, lg_ref, lb_ref, fg_ref, fb_ref)
    )

    kvg = kv

    counters = {"s": 0, "r": 0, "l": 0}
    sends = []
    local = []

    def new(kind, count=1):
        base = counters[kind]
        counters[kind] = base + count
        return base

    def put(src, dst, recv, axis, peer):
        d = pltpu.make_async_remote_copy(
            src, dst, ssem.at[new("s")], rsem.at[recv], device_id={axis: peer}, device_id_type=MESH
        )
        d.start()
        sends.append(d)
        return d

    def got(dst, recv):
        pltpu.make_async_remote_copy(
            dst, dst, ssem.at[0], rsem.at[recv], device_id={"narrow": mate}, device_id_type=MESH
        ).wait_recv()

    def here(src, dst, keep=True):
        d = pltpu.make_async_copy(src, dst, lsem.at[new("l")])
        d.start()
        if keep:
            local.append(d)
        return d

    def rows(ref, start, count):
        return ref.at[pl.ds(start, count), :]

    def al(v, m):
        return pl.multiple_of(v, m)

    def npeer(k):
        return lax.rem(n + k, N)

    def nsrc(k):
        return lax.rem(n + N - k, N)

    def wpeer(k):
        return lax.rem(w + k, W)

    def wsrc(k):
        return lax.rem(w + W - k, W)

    media_in = [here(rows(media_h, c * CH, CH), rows(media, c * CH, CH), False) for c in range(NC)]
    down_in = here(down_h, down, False)
    up_in = here(up_h, up, False)

    def own_kv(i, carry):
        v = wkv_ref[pl.ds(i * 16, 16)].astype(F32)
        at = pl.ds(al(w * S + i * 16, 16), 16)
        kvw[at, 0:C] = v[:, 0, :].astype(BF16)
        kvw[at, C : 2 * C] = v[:, 1, :].astype(BF16)
        return carry

    lax.fori_loop(0, S // 16, own_kv, 0)

    barrier = pltpu.get_barrier_semaphore()
    for k in range(1, N):
        pl.semaphore_signal(barrier, inc=1, device_id={"narrow": npeer(k)}, device_id_type=MESH)
    for k in range(1, W):
        pl.semaphore_signal(barrier, inc=1, device_id={"wide": wpeer(k)}, device_id_type=MESH)
    pl.semaphore_wait(barrier, N - 1 + W - 1)

    def wide_gather(src, at, link_y=True):
        direct = new("r", W2)
        fwd = new("r", W2)
        for k in range(1, W2):
            put(src, at(w), direct + k, "wide", wpeer(2 * k))

        def to_partner():
            put(src, at(w), direct, "wide", partner)

        if link_y:
            to_partner()

        def forward(k):
            b = wsrc(2 * k)
            got(at(b), direct + k)
            put(at(b), at(b), fwd + k, "wide", partner)

        def finish():
            got(at(partner), direct)
            for k in range(1, W2):
                b = lax.rem(partner + W - 2 * k, W)
                got(at(b), fwd + k)

        return (forward, finish) if link_y else (forward, finish, to_partner)

    def blocks(buf, count):
        return lambda b: rows(buf, al(b * count, 16), count)

    half_of = lambda c: pl.ds(al(c * (L // 2), 16), L // 2)
    mine_half, mate_half = half_of(core), half_of(1 - core)

    def hand_over(buf, base):
        for k in range(1, W):
            at = buf.at[wsrc(k), mine_half, :]
            put(at, at, base + k, "narrow", mate)

        def finish():
            for k in range(1, W):
                got(buf.at[wsrc(k), mate_half, :], base + k)

        return finish

    def row_gather(buf):
        at = lambda b: buf.at[b, mine_half, :]
        forward, finish = wide_gather(at(w), at)
        base = new("r", W)

        def share():
            finish()
            return hand_over(buf, base)

        return forward, share

    def spread(which, value):
        for b in range(W):
            sl_st[which, b] = value[:, b * S : (b + 1) * S]
        base = new("r", W)
        base2 = new("r", W)
        for k in range(1, W):
            put(
                sl_st.at[which, wpeer(k), mine_half, :], sl_rc.at[which, w, mine_half, :],
                base + k, "wide", wpeer(k),
            )
        sl_rc[which, w] = sl_st[which, w]

        def share():
            for k in range(1, W):
                got(sl_rc.at[which, wsrc(k), mine_half, :], base + k)
            return hand_over(sl_rc.at[which], base2)

        return share

    own_w = [
        here(wq_h, rows(wq, al(w * S, 16), S), False),
        here(wot_h, rows(wot, al(w * S, 16), S), False),
    ]
    kv_fwd, kv_fin = wide_gather(rows(kvw, al(w * S, 16), S), blocks(kvw, S))
    q_fwd, q_fin = wide_gather(wq_h, blocks(wq, S))
    o_fwd, o_fin, o_partner = wide_gather(wot_h, blocks(wot, S), False)

    lat = lat_ref[...].astype(F32)
    lat_mean, lat_istd, lat_hat = norm_stats(lat)
    lat_ag[n] = (lat_hat * gain_l + bias_l).astype(BF16)
    cot_ag[n] = cot_ref[...]

    def narrow_gather(buf):
        base = new("r", N)
        for k in range(1, N):
            put(buf.at[n], buf.at[n], base + k, "narrow", npeer(k))

        def finish():
            for k in range(1, N):
                got(buf.at[nsrc(k)], base + k)
            return jnp.concatenate([buf[i].astype(F32) for i in range(N)], axis=0).astype(BF16)

        return finish

    te32[...] = te_ref[...].astype(F32)

    m_direct = new("r", NC * X)
    m_fwd = new("r", NC * X)

    def m_rows(block, c):
        return rows(x_all, al(block * Mo + c * CH, 16), CH)

    def frame_of(c):
        return lax.div(n * Mo + c * CH, PATCHES)

    for c in range(NC):
        media_in[c].wait()
        te_row = te32[pl.ds(frame_of(c), 1), :]

        def norm_rows(i, carry, c=c, te_row=te_row):
            r = al(c * CH + i * 16, 16)
            v = media[pl.ds(r, 16), :].astype(F32) + te_row
            mean, inv_std, hat = norm_stats(v)
            mean_s[pl.ds(r, 16), :] = jnp.broadcast_to(mean, (16, LANES))
            istd_s[pl.ds(r, 16), :] = jnp.broadcast_to(inv_std, (16, LANES))
            x_all[pl.ds(al(n * Mo + r, 16), 16), :] = (hat * gain_m + bias_m).astype(BF16)
            return carry

        lax.fori_loop(0, CH // 16, norm_rows, 0, unroll=2)
        for j in range(1, X):
            peer = lax.rem(xpos + j, X) * 2 + core
            put(m_rows(n, c), m_rows(n, c), m_direct + c * X + j, "narrow", peer)
        put(m_rows(n, c), m_rows(n, c), m_direct + c * X, "narrow", mate)
        if c == 0:
            lat_fin = narrow_gather(lat_ag)
            cot_fin = narrow_gather(cot_ag)

    def media_forward(c):
        for j in range(1, X):
            block = lax.rem(xpos + X - j, X) * 2 + core
            got(m_rows(block, c), m_direct + c * X + j)
            put(m_rows(block, c), m_rows(block, c), m_fwd + c * X + j, "narrow", mate)

    slot_frame = lax.div(lax.broadcasted_iota(jnp.int32, (M // LANES, LANES), 0), PATCHES // LANES)
    ok = (slot_frame < fc_ref[0]) & (mm_ref[...] > 0)
    okf = jnp.where(ok, 1.0, 0.0).astype(F32)
    tail = jnp.where(
        lax.broadcasted_iota(jnp.int32, (1, KT - M), 1) < L, 1.0, 0.0
    ).astype(F32)
    for j in range(KT // LANES):
        row = okf[j : j + 1, :] if j < M // LANES else tail[:, j * LANES - M : j * LANES - M + LANES]
        mt[j * LANES : (j + 1) * LANES, :] = jnp.broadcast_to(row, (LANES, LANES)).T
    count = jnp.sum(okf, keepdims=True) + float(L)
    cnt_ag[w] = jnp.broadcast_to(count, (8, LANES))
    cnt_base = new("r", W)
    for k in range(1, W):
        put(cnt_ag.at[w], cnt_ag.at[w], cnt_base + k, "wide", wpeer(k))

    kv_fwd(1)
    o_partner()

    lat_all = lat_fin()
    cot_all = cot_fin()
    x_all[M : M + L, :] = lat_all
    if KT > M + L:
        x_all[M + L : KT, :] = jnp.zeros((KT - M - L, D), BF16)
    cot_g[w] = cot_all

    down_in.wait()

    def act_grad(j, carry):
        r = al(j * 256, 256)
        ga[:, pl.ds(r, 256)] = nt(cot_all, down[pl.ds(r, 256), :])
        return carry

    lax.fori_loop(0, F // 256, act_grad, 0)

    media_forward(0)
    for k in range(2, W2):
        kv_fwd(k)
    for c in range(1, NC - 1):
        media_forward(c)
    q_fwd(1)
    for d in own_w:
        d.wait()
    kv_fin()

    def project(start, count):
        def step(i, carry):
            r = al(start + i * CH, 16)
            kv[pl.ds(r, CH), :] = nn(x_all[pl.ds(r, CH), :], kvw[...]).astype(BF16)
            return carry

        lax.fori_loop(0, count // CH, step, 0)

    def project_far(c):
        for j in range(1, X):
            block = lax.rem(xpos + X - j, X) * 2 + core
            project(block * Mo + c * CH, CH)

    def project_mate(c):
        for j in range(1, X):
            block = lax.rem(xpos + X - j, X) * 2 + 1 - core
            got(m_rows(block, c), m_fwd + c * X + j)
            project(block * Mo + c * CH, CH)

    project(n * Mo, Mo)
    project(M, KT - M)
    for c in range(NC):
        got(m_rows(mate, c), m_direct + c * X)
    project(mate * Mo, Mo)
    for c in range(NC - 1):
        project_far(c)
        project_mate(c)
    for k in range(2, W2):
        q_fwd(k)
    if NC > 1:
        media_forward(NC - 1)
    project_far(NC - 1)
    q_fin()
    q_act = nn(lat_all, wq[...]).astype(BF16).astype(F32)
    head_of = lax.div(lax.broadcasted_iota(jnp.int32, (L, C), 1), HEAD_DIM)

    def per_head(v):
        return jnp.concatenate([jnp.where(head_of == h, v, 0.0) for h in range(HL)], axis=0)

    def from_heads(v):
        total = jnp.where(head_of == 0, v[0:L], 0.0)
        for h in range(1, HL):
            total = total + jnp.where(head_of == h, v[h * L : (h + 1) * L], 0.0)
        return total

    q_big32 = per_head(q_act)
    q_big = q_big32.astype(BF16)
    q_big_t = q_big32.T.astype(BF16)
    project_mate(NC - 1)
    for k in range(1, W2 - 2):
        o_fwd(k)

    KB = 128

    def wide_mask(r):
        m = mt[pl.ds(r, KB), :]
        return jnp.concatenate([m] * (R // LANES), axis=1) > 0.0

    def score_step(j, top):
        r = al(j * KB, KB)
        s = nn(kv[pl.ds(r, KB), 0:C], q_big_t) * scale
        s = jnp.where(wide_mask(r), s, NEG)
        st[pl.ds(r, KB), :] = s
        return jnp.maximum(top, jnp.max(s, axis=0, keepdims=True))

    top = lax.fori_loop(0, KT // KB, score_step, jnp.full((1, R), NEG, F32))

    def exp_step(j, carry):
        total, dot = carry
        r = al(j * KB, KB)
        s = st[pl.ds(r, KB), :]
        e = jnp.exp(s - top)
        pt[pl.ds(r, KB), :] = e
        s = jnp.where(wide_mask(r), s, 0.0)
        st[pl.ds(r, KB), :] = s
        return (
            total + jnp.sum(e, axis=0, keepdims=True),
            dot + jnp.sum(e * s, axis=0, keepdims=True),
        )

    zero_row = jnp.zeros((1, R), F32)
    total, dot = lax.fori_loop(0, KT // KB, exp_step, (zero_row, zero_row))
    inv_total = 1.0 / total
    mean_score = dot * inv_total

    def prob_step(j, carry):
        r = al(j * KB, KB)
        pr = pt[pl.ds(r, KB), :] * inv_total
        pt[pl.ds(r, KB), :] = pr
        pn[:, pl.ds(r, KB)] = pr.T.astype(BF16)
        return carry

    o_fwd(W2 - 2)
    lax.fori_loop(0, KT // KB, prob_step, 0)
    attn = from_heads(nn(pn[...], kv[:, C : 2 * C]))
    attn_low = attn.astype(BF16)

    o_fwd(W2 - 1)
    cot_fwd, cot_share = row_gather(cot_g)
    slat_share = spread(0, lat_all)
    at_w = lambda ref: rows(ref, al(w * L, 16), L)
    att_g[pl.ds(al(w * L, 16), L), :] = attn_low

    def narrow_sum(slot, parts):
        base = new("r", N)
        for k in range(1, N):
            put(rs_st.at[slot, npeer(k)], rs_rc.at[slot, k], base + k, "narrow", npeer(k))

        def finish():
            v = rs_st[slot, n].astype(F32)
            for k in range(1, N):
                got(rs_rc.at[slot, k], base + k)
                v = v + rs_rc[slot, k].astype(F32)
            return v

        return finish

    def stage(slot, cols, v):
        for i in range(N):
            rs_st[slot, i, :, cols] = v[i * Lo : (i + 1) * Lo].astype(BF16)

    o_fin()

    def branch_step(j, carry):
        r = al(j * 256, 256)
        stage(0, pl.ds(r, 256), nt(attn_low, wot[pl.ds(r, 256), :]))
        return carry

    lax.fori_loop(0, D // 256, branch_step, 0)
    branch_fin = narrow_sum(0, None)
    mid = lat + branch_fin()
    mid_mean, mid_istd, mid_hat = norm_stats(mid)
    hid_ag[n] = (mid_hat * gain_f + bias_f).astype(BF16)
    hid_fin = narrow_gather(hid_ag)
    up_in.wait()
    hid_all = hid_fin()
    hid_g[w] = hid_all
    hid_fwd, hid_share = row_gather(hid_g)
    att_fwd, att_fin = wide_gather(at_w(att_g), blocks(att_g, L))

    own64 = pl.ds(al(w * L, 16), L)

    def ffn_step(j, carry):
        cs = pl.ds(al(j * 256, 256), 256)
        pre = nn(hid_all, up[:, cs])
        cdf = 0.5 * (1.0 + lax.erf(pre * (1.0 / math.sqrt(2.0))))
        density = jnp.exp(-0.5 * pre * pre) * (1.0 / math.sqrt(2.0 * math.pi))
        act_own[:, cs] = (pre * cdf).astype(BF16)
        pre_own[:, cs] = (ga[:, cs] * (cdf + pre * density)).astype(BF16)
        return carry

    lax.fori_loop(0, F // 256, ffn_step, 0)
    gpre = pre_own[...]

    def hid_back(j, carry):
        r = al(j * 256, 256)
        stage(1, pl.ds(r, 256), nt(gpre, up[pl.ds(r, 256), :]))
        return carry

    lax.fori_loop(0, D // 256, hid_back, 0)
    ghid_fin = narrow_sum(1, None)
    act_all = act_own[...]

    def ffn_out(j, carry):
        cs = pl.ds(al(j * 256, 256), 256)
        stage(2, cs, nn(act_all, down[:, cs]))
        return carry

    lax.fori_loop(0, D // 256, ffn_out, 0)
    ffn_fin = narrow_sum(2, None)
    for k in range(1, W2):
        cot_fwd(k)

    ghid = ghid_fin()
    grad_mid = cot_ref[...].astype(F32) + norm_back(ghid, mid_hat, mid_istd, gain_f)
    gb_ag[n] = grad_mid.astype(BF16)
    gb_fin = narrow_gather(gb_ag)
    acc8[...] = jnp.zeros_like(acc8)
    stat[...] = jnp.zeros_like(stat)
    stat[FRAMES_MAX + 4 : FRAMES_MAX + 5, :] = jnp.sum(ghid * mid_hat, axis=0, keepdims=True)
    stat[FRAMES_MAX + 5 : FRAMES_MAX + 6, :] = jnp.sum(ghid, axis=0, keepdims=True)
    hid_fwd(1)
    for k in range(1, W):
        got(cnt_ag.at[wsrc(k)], cnt_base + k)
    keys = cnt_ag[0]
    for i in range(1, W):
        keys = keys + cnt_ag[i]
    ent1 = ENT_COEF * float(W * M) / keys[0:1, :]
    ent = jnp.concatenate([ent1] * (R // LANES), axis=1)
    gb_all = gb_fin()
    sgb_share = spread(1, gb_all)

    g_attn = nn(gb_all, wot[...]).astype(BF16).astype(F32)
    g_big32 = per_head(g_attn)
    g_big = g_big32.astype(BF16)
    g_big_t = g_big32.T.astype(BF16)
    row_dot = jnp.sum(per_head(g_attn * attn).T, axis=0, keepdims=True)
    shift = row_dot - ent * mean_score

    def back_step(j, carry):
        r = al(j * KB, KB)
        pr = pt[pl.ds(r, KB), :]
        gp = nn(kv[pl.ds(r, KB), C : 2 * C], g_big_t)
        gs = pr * (gp - ent * st[pl.ds(r, KB), :] - shift)
        pn[:, pl.ds(r, KB)] = gs.T.astype(BF16)
        gpair[pl.ds(r, KB), 0:C] = (nn(gs.astype(BF16), q_big) * scale).astype(BF16)
        gpair[pl.ds(r, KB), C : 2 * C] = nn(pr.astype(BF16), g_big).astype(BF16)
        return carry

    lax.fori_loop(0, KT // KB // 2, back_step, 0)
    for k in range(2, W2):
        hid_fwd(k)
    lax.fori_loop(KT // KB // 2, KT // KB, back_step, 0)

    gq = (from_heads(nn(pn[...], kv[:, 0:C])) * scale).astype(BF16)
    gq_g[own64, :] = gq
    gq_fwd, gq_fin = wide_gather(at_w(gq_g), blocks(gq_g, L))

    H = W2 // 2
    half = lax.div(w, 2)
    order = [(lax.rem(half + k, H) + (1 - lax.div(half, H)) * H) for k in range(H)]
    order += [(lax.rem(half + k, H) + lax.div(half, H) * H) for k in list(range(1, H)) + [0]]
    y_base = new("r", W2)
    z_base = new("r", W2)

    def kvg_rows(first):
        def step(j, carry):
            r = al(first * (D // 2) + j * 256, 256)
            kvg[pl.ds(r, 256), :] = tn(x_all[:, pl.ds(r, 256)], gpair[...]).astype(BF16)
            return carry

        lax.fori_loop(0, D // 512, step, 0)

    def kvg_to_partner(i):
        put(
            rows(kvg, al((2 * order[i] + 1 - par) * S, 16), S), rows(kvg_y, i * S, S),
            y_base + i, "wide", partner,
        )

    def kvg_step(i):
        g = order[i]
        got(rows(kvg_y, i * S, S), y_base + i)
        mine = pl.ds(al((2 * g + par) * S, 16), S)
        summed = kvg[mine, :].astype(F32) + kvg_y[i * S : (i + 1) * S, :].astype(F32)
        if i < W2 - 1:
            kvg[mine, :] = summed.astype(BF16)
            put(kvg.at[mine, :], rows(kvg_z, i * S, S), z_base + i, "wide", 2 * g + par)
        else:
            o_kv[...] = summed

    kvg_rows(1 - lax.div(half, H))
    for i in range(H):
        kvg_to_partner(i)

    mate_base = new("r", X * NC)
    xs_base = new("r", X * NC)

    def part(block, c):
        r = al(block * Mo + c * CH, 16)
        return nt(gpair[pl.ds(r, CH), :], kvw[...])

    mate_sent = {}

    def x_of(j):
        return lax.rem(xpos + j, X)

    def to_mate(j, c):
        b = x_of(j) * 2 + 1 - core
        if c in mate_sent:
            mate_sent[c].wait_send()
            sends[:] = [d for d in sends if d is not mate_sent[c]]
        mate_st[c * CH : (c + 1) * CH, :] = part(b, c).astype(BF16)
        mate_sent[c] = put(
            rows(mate_st, c * CH, CH), rows(mate_rc, (j * NC + c) * CH, CH), mate_base + j * NC + c, "narrow", mate
        )

    def from_mate(j, c):
        i = (j * NC + c) * CH
        got(rows(mate_rc, i, CH), mate_base + j * NC + c)
        return part(x_of(j) * 2 + core, c) + mate_rc[i : i + CH, :].astype(F32)

    def rows_out(j, cs):
        for c in cs:
            to_mate(j, c)
        for c in cs:
            i = ((j - 1) * NC + c) * CH
            x_st[i : i + CH, :] = from_mate(j, c).astype(BF16)
            put(
                rows(x_st, i, CH), rows(x_rc, i, CH), xs_base + (j - 1) * NC + c,
                "narrow", x_of(j) * 2 + core,
            )

    rows_out(1, range(NC // 2))
    kvg_rows(lax.div(half, H))
    for i in range(H, W2):
        kvg_to_partner(i)

    gpl = gpair[M : M + L, :]

    def lat_back(j, carry):
        r = al(j * 256, 256)
        stage(3, pl.ds(r, 256), nt(gpl, kvw[pl.ds(r, 256), :]) + nt(gq, wq[pl.ds(r, 256), :]))
        return carry

    lax.fori_loop(0, D // 256, lat_back, 0)
    glat_fin = narrow_sum(3, None)
    rows_out(1, range(NC // 2, NC))
    for j in range(2, X):
        rows_out(j, range(NC))
    for k in range(1, W2):
        att_fwd(k)
    slat_fin = slat_share()
    cot_fin = cot_share()
    hid_fin = hid_share()
    sgb_fin = sgb_share()
    for c in range(NC):
        to_mate(0, c)
    for c in range(NC):
        own_sum[c * CH : (c + 1) * CH, :] = from_mate(0, c)
    third = [i * W2 // 4 for i in range(5)]
    for i in range(third[0], third[1]):
        kvg_step(i)

    cot_fin()
    hid_fin()
    pick = (
        lax.broadcasted_iota(jnp.int32, (D, S), 0) == lax.broadcasted_iota(jnp.int32, (D, S), 1) + w * S
    ).astype(F32).astype(BF16)
    cot_rows = lambda: cot_g[...].reshape(W * L, D)
    hid_rows = lambda: hid_g[...].reshape(W * L, D)

    def pick_step(b, carry):
        at = pl.ds(al(b * L, 16), L)
        cot_sl[at, :] = nn(cot_g[b], pick).astype(BF16)
        hid_sl[at, :] = nn(hid_g[b], pick).astype(BF16)
        return carry

    lax.fori_loop(0, W, pick_step, 0)

    def unit_step(j, carry):
        cs = pl.ds(al(j * 256, 256), 256)
        pre = nn(hid_rows(), up[:, cs])
        grad = nt(cot_rows(), down[cs, :])
        cdf = 0.5 * (1.0 + lax.erf(pre * (1.0 / math.sqrt(2.0))))
        density = jnp.exp(-0.5 * pre * pre) * (1.0 / math.sqrt(2.0 * math.pi))
        o_down[:, cs] = tn(cot_sl[...], (pre * cdf).astype(BF16))
        o_up[:, cs] = tn(hid_sl[...], (grad * (cdf + pre * density)).astype(BF16))
        return carry

    units = F // 256
    for t in range(3):
        lax.fori_loop(t * units // 3, (t + 1) * units // 3, unit_step, 0)
        for i in range(third[t + 1], third[t + 2]):
            kvg_step(i)
    here(o_up, out_up)
    here(o_down, out_down)

    out_l = (mid + ffn_fin()).astype(BF16)
    lat_nf[0] = out_l
    here(lat_nf.at[0], out_lat)
    glat = glat_fin()
    g_lat = grad_mid + norm_back(glat, lat_hat, lat_istd, gain_l)
    lat_nf[1] = g_lat.astype(BF16)
    here(lat_nf.at[1], out_gl)
    stat[FRAMES_MAX + 2 : FRAMES_MAX + 3, :] = jnp.sum(glat * lat_hat, axis=0, keepdims=True)
    stat[FRAMES_MAX + 3 : FRAMES_MAX + 4, :] = jnp.sum(glat, axis=0, keepdims=True)

    for k in range(1, W2):
        gq_fwd(k)
    att_fin()
    sgb_fin()
    o_o[...] = tn(sl_rc[1].reshape(W * L, S), att_g[...])
    here(o_o, out_o)
    gq_fin()
    slat_fin()
    o_q[...] = tn(sl_rc[0].reshape(W * L, S), gq_g[...])
    here(o_q, out_q)

    gm_out = []
    for c in range(NC):
        for j in range(1, X):
            i = ((j - 1) * NC + c) * CH
            got(rows(x_rc, i, CH), xs_base + (j - 1) * NC + c)
        f = frame_of(c)
        te_row = te32[pl.ds(f, 1), :]

        def back_rows(i, carry, c=c, te_row=te_row):
            r = al(c * CH + i * 16, 16)
            dy = own_sum[pl.ds(r, 16), :]
            for j in range(1, X):
                dy = dy + x_rc[pl.ds(al((j - 1) * Mo + r, 16), 16), :].astype(F32)
            mean = mean_s[pl.ds(r, 16), 0:1]
            inv_std = istd_s[pl.ds(r, 16), 0:1]
            hat = (media[pl.ds(r, 16), :].astype(F32) + te_row - mean) * inv_std
            dx = norm_back(dy, hat, inv_std, gain_m)
            media[pl.ds(r, 16), :] = dx.astype(BF16)
            acc8[0:8, :] += fold8(dy * hat)
            acc8[8:16, :] += fold8(dy)
            acc8[16:24, :] += fold8(dx)
            return carry

        lax.fori_loop(0, CH // 16, back_rows, 0)
        stat[pl.ds(f, 1), :] += jnp.sum(acc8[16:24, :], axis=0, keepdims=True)
        acc8[16:24, :] = jnp.zeros((8, D), F32)
        here(rows(media, c * CH, CH), rows(out_gm, c * CH, CH))
    stat[FRAMES_MAX : FRAMES_MAX + 1, :] = jnp.sum(acc8[0:8, :], axis=0, keepdims=True)
    stat[FRAMES_MAX + 1 : FRAMES_MAX + 2, :] = jnp.sum(acc8[8:16, :], axis=0, keepdims=True)

    vec = stat[...]
    for b in range(W):
        vec_st[b] = vec[:, b * S : (b + 1) * S]
    v_base = new("r", W)
    for k in range(1, W):
        put(vec_st.at[wpeer(k)], vec_rc.at[k], v_base + k, "wide", wpeer(k))
    for i in range(W2 - 1):
        got(rows(kvg_z, i * S, S), z_base + i)
        o_kv[...] += kvg_z[i * S : (i + 1) * S, :].astype(F32)
    here(o_kv, out_kv)
    vs = vec_st[w]
    for k in range(1, W):
        got(vec_rc.at[k], v_base + k)
        vs = vs + vec_rc[k]
    for i in range(N):
        vec2_st[i] = vs[:, i * V : (i + 1) * V]
    v2_base = new("r", N)
    for k in range(1, N):
        put(vec2_st.at[npeer(k)], vec2_rc.at[k], v2_base + k, "narrow", npeer(k))
    vs = vec2_st[n]
    for k in range(1, N):
        got(vec2_rc.at[k], v2_base + k)
        vs = vs + vec2_rc[k]
    o_vec[...] = vs
    here(o_vec, out_vec)

    for d in sends:
        d.wait_send()
    for d in local:
        d.wait()
    sem_counts.update(counters)


def finish_kernel(p, pieces, *refs):
    src, dst, buf, sem_in, sem_out = refs[:9], refs[9:24], refs[24:33], refs[33], refs[34]
    V, C = p.V, p.C
    loads = []
    for i in range(9):
        count = src[i].shape[0] // pieces[i]
        for c in range(pieces[i]):
            at = pl.ds(c * count, count)
            d = pltpu.make_async_copy(src[i].at[at, :], buf[i].at[at, :], sem_in.at[len(loads)])
            d.start()
            loads.append((i, at, d))
    stores = []

    def store(a, b):
        d = pltpu.make_async_copy(a, b, sem_out.at[len(stores)])
        d.start()
        stores.append(d)

    first = {0: 0, 1: 1, 2: 2, 4: 10, 5: 11, 6: 12, 7: 13, 8: 14}
    for i, at, d in loads:
        d.wait()
        if i == 3:
            store(buf[3].at[pl.ds(0, FRAMES_MAX), :], dst[3])
            for k in range(6):
                store(buf[3].at[FRAMES_MAX + k], dst[4 + k])
        elif i == 5 and C % LANES == 0:
            for k in range(2):
                store(buf[5].at[:, pl.ds(k * C, C)], dst[11].at[:, k, :])
        else:
            store(buf[i].at[at, :], dst[first[i]].at[at, :])
    for d in stores:
        d.wait()


def finish(p, outs):
    sds = jax.ShapeDtypeStruct
    hbm = pl.BlockSpec(memory_space=pl.ANY)
    pieces = [1, 4, 1, 1, 1, 1, 1, 2, 2]
    shapes = [sds(a.shape, a.dtype) for a in outs]
    vec = [sds((FRAMES_MAX, p.V), F32)] + [sds((p.V,), F32)] * 6
    res = pl.pallas_call(
        functools.partial(finish_kernel, p, pieces),
        out_shape=tuple(shapes[:3] + vec + [shapes[4], sds((p.S, 2, p.C), F32) if p.C % LANES == 0 else shapes[5]] + shapes[6:]),
        in_specs=[hbm] * 9,
        out_specs=[hbm] * 15,
        scratch_shapes=[pltpu.VMEM(a.shape, a.dtype) for a in outs]
        + [pltpu.SemaphoreType.DMA((sum(pieces),)), pltpu.SemaphoreType.DMA((sum(pieces) + 7,))],
        compiler_params=pltpu.CompilerParams(has_side_effects=True),
    )(*outs)
    return res[0], res[1], res[2], res[3:10], res[10], res[11].reshape(p.S, 2, p.C), res[12], res[13], res[14]


def make_body(mesh):
    def body(
        media_feats, latents, frame_counts, media_mask, time_embed, media_gain, media_bias, latent_gain,
        latent_bias, ffn_gain, ffn_bias, query_weight, keyval_weight, output_weight, up_weight,
        down_weight, cotangent,
    ):
        p = Plan(mesh, media_feats, latents, up_weight)
        D, C, S, L, Lo, KT, R, F, N, W, Mo = p.D, p.C, p.S, p.L, p.Lo, p.KT, p.R, p.F, p.N, p.W, p.Mo
        X, W2, NC, V = p.X, p.W2, p.NC, p.V
        vm = pl.BlockSpec(memory_space=pltpu.VMEM)
        hbm = pl.BlockSpec(memory_space=pl.ANY)
        smem = pl.BlockSpec(memory_space=pltpu.SMEM)
        sds = jax.ShapeDtypeStruct
        vmem = pltpu.VMEM
        scratch = [
            vmem((Mo, D), BF16),
            vmem((KT, D), BF16),
            vmem((D, 2 * C), BF16),
            vmem((D, C), BF16),
            vmem((D, C), BF16),
            vmem((D, F), BF16),
            vmem((F, D), BF16),
            vmem((KT, 2 * C), BF16),
            vmem((KT, R), F32),
            vmem((KT, R), F32),
            vmem((R, KT), BF16),
            vmem((KT, 2 * C), BF16),
            vmem((KT, LANES), F32),
            vmem((FRAMES_MAX, D), F32),
            vmem((Mo, LANES), F32),
            vmem((Mo, LANES), F32),
            vmem((2, Lo, D), BF16),
            vmem((N, Lo, D), BF16),
            vmem((N, Lo, D), BF16),
            vmem((W, 8, LANES), F32),
            vmem((4, N, Lo, D), BF16),
            vmem((4, N, Lo, D), BF16),
            vmem((N, Lo, D), BF16),
            vmem((N, Lo, D), BF16),
            vmem((Mo, D), BF16),
            vmem((X * Mo, D), BF16),
            vmem(((X - 1) * Mo, D), BF16),
            vmem(((X - 1) * Mo, D), BF16),
            vmem((Mo, D), F32),
            vmem((W2 * S, 2 * C), BF16),
            vmem((W2 * S, 2 * C), BF16),
            vmem((L, F), BF16),
            vmem((L, F), BF16),
            vmem((W, L, D), BF16),
            vmem((W, L, D), BF16),
            vmem((W * L, C), BF16),
            vmem((W * L, C), BF16),
            vmem((2, W, L, S), BF16),
            vmem((2, W, L, S), BF16),
            vmem((W * L, S), BF16),
            vmem((W * L, S), BF16),
            vmem((L, F), F32),
            vmem((24, D), F32),
            vmem((16, D), F32),
            vmem((W, 16, S), F32),
            vmem((W, 16, S), F32),
            vmem((N, 16, V), F32),
            vmem((N, 16, V), F32),
            vmem((S, F), F32),
            vmem((S, F), F32),
            vmem((S, C), F32),
            vmem((S, C), F32),
            vmem((S, 2 * C), F32),
            vmem((16, V), F32),
            pltpu.SemaphoreType.DMA((24 * W + 8 * N * p.NC + 64,)),
            pltpu.SemaphoreType.DMA((24 * W + 8 * N * p.NC + 64,)),
            pltpu.SemaphoreType.DMA((64,)),
        ]
        outs = pl.pallas_call(
            functools.partial(body_kernel, p, {}),
            out_shape=(
                sds((Lo, D), BF16),
                sds((Mo, D), BF16),
                sds((Lo, D), BF16),
                sds((16, V), F32),
                sds((S, C), F32),
                sds((S, 2 * C), F32),
                sds((S, C), F32),
                sds((S, F), F32),
                sds((S, F), F32),
            ),
            in_specs=[hbm, vm, smem, vm, vm, vm, vm, vm, vm, vm, vm, hbm, vm, hbm, hbm, hbm, vm],
            out_specs=[hbm] * 9,
            scratch_shapes=scratch,
            compiler_params=pltpu.CompilerParams(
                collective_id=0, has_side_effects=True, vmem_limit_bytes=67_043_328
            ),
        )(
            media_feats[0], latents[0], frame_counts, media_mask.reshape(p.M // LANES, LANES), time_embed,
            media_gain, media_bias, latent_gain, latent_bias, ffn_gain, ffn_bias,
            query_weight, keyval_weight, output_weight.T, up_weight, down_weight, cotangent[0],
        )
        lat, gm, gl, vec, gq, gkv, go, gup, gdown = finish(p, outs)
        return (lat[None], gm[None], gl[None]) + tuple(vec) + (gq, gkv, go.T, gup, gdown.T)

    return body


def solution(mesh):
    both = P(("wide", "narrow"))
    rows = P("wide", "narrow", None)
    return jax.shard_map(
        make_body(mesh),
        mesh=mesh,
        in_specs=(
            rows, rows, P("wide"), P("wide", None), P(), P(), P(), P(), P(), P(), P(), P("wide", "narrow"),
            P("wide", None, "narrow"), P("narrow", "wide"), P(None, "narrow"), P("narrow", None), rows,
        ),
        out_specs=(
            rows, rows, rows, P(None, ("wide", "narrow")), both, both, both, both, both, both,
            P("wide", "narrow"), P("wide", None, "narrow"), P("narrow", "wide"), P("wide", "narrow"),
            P("narrow", "wide"),
        ),
        check_vma=False,
    )
```

```python
import functools
import math

import jax
import jax.numpy as jnp
from jax import lax
from jax.experimental import pallas as pl
from jax.experimental.pallas import tpu as pltpu
from jax.sharding import PartitionSpec as P

HEADS = 16
HEAD_DIM = 96
FRAMES_MAX = 8
PATCHES = 256
EPS = 1e-05
ENT_COEF = 4.0
NEG = -1e30
LANES = 128
MESH = pl.DeviceIdType.MESH
F32 = jnp.float32
BF16 = jnp.bfloat16


def nn(a, b):
    return lax.dot_general(a, b, (((1,), (0,)), ((), ())), preferred_element_type=F32)


def nt(a, b):
    return lax.dot_general(a, b, (((1,), (1,)), ((), ())), preferred_element_type=F32)


def tn(a, b):
    return lax.dot_general(a, b, (((0,), (0,)), ((), ())), preferred_element_type=F32)


def rows_mean(v):
    return jnp.mean(v, axis=-1, keepdims=True)


def norm_stats(v):
    mean = rows_mean(v)
    centered = v - mean
    inv_std = lax.rsqrt(rows_mean(centered * centered) + EPS)
    return mean, inv_std, centered * inv_std


def norm_back(dy, hat, inv_std, gain):
    scaled = dy * gain
    return inv_std * (scaled - rows_mean(scaled) - hat * rows_mean(scaled * hat))


def fold8(v):
    return jnp.sum(v.reshape(v.shape[0] // 8, 8, v.shape[1]), axis=0)


class Plan:
    def __init__(self, mesh, media, latents, up):
        self.N = mesh.shape["narrow"]
        self.W = mesh.shape["wide"]
        self.X = self.N // 2
        self.W2 = self.W // 2
        self.Mo, self.D = media.shape[1], media.shape[2]
        self.Lo = latents.shape[1]
        self.M = self.Mo * self.N
        self.L = self.Lo * self.N
        self.HL = HEADS // self.N
        self.C = self.HL * HEAD_DIM
        self.KT = self.M + -(-self.L // LANES) * LANES
        self.F = up.shape[1]
        self.S = self.D // self.W
        self.V = self.S // self.N
        self.R = self.HL * self.L
        self.CH = 128
        self.NC = self.Mo // self.CH


def body_kernel(p, sem_counts, *refs):
    (
        media_h, lat_ref, fc_ref, mm_ref, te_ref, mg_ref, mb_ref, lg_ref, lb_ref, fg_ref, fb_ref,
        wq_h, wkv_ref, wot_h, up_h, down_h, cot_ref,
        out_lat, out_gm, out_gl, out_vec, out_q, out_kv, out_o, out_up, out_down,
        media, x_all, kvw, wq, wot, up, down, kv, st, pt, pn, gpair, mt, te32, mean_s, istd_s,
        lat_nf, lat_ag, cot_ag, cnt_ag,
        rs_st, rs_rc, hid_ag, gb_ag, mate_st, mate_rc, x_st, x_rc, own_sum,
        kvg_y, kvg_z, act_own, pre_own, hid_g, cot_g, att_g, gq_g, sl_st, sl_rc, cot_sl, hid_sl, ga, acc8, stat, vec_st, vec_rc, vec2_st, vec2_rc,
        o_up, o_down, o_o, o_q, o_kv, o_vec, ssem, rsem, lsem,
    ) = refs
    N, W, X, W2 = p.N, p.W, p.X, p.W2
    Mo, Lo, M, L, D, C, R, S, F, KT = p.Mo, p.Lo, p.M, p.L, p.D, p.C, p.R, p.S, p.F, p.KT
    CH, NC, HL, V = p.CH, p.NC, p.HL, p.V
    n = lax.axis_index("narrow")
    w = lax.axis_index("wide")
    core = lax.rem(n, 2)
    xpos = lax.div(n, 2)
    mate = n + 1 - 2 * core
    par = lax.rem(w, 2)
    partner = w + 1 - 2 * par
    scale = HEAD_DIM ** (-0.5)
    gain_m, bias_m, gain_l, bias_l, gain_f, bias_f = (
        ref[...].reshape(1, D) for ref in (mg_ref, mb_ref, lg_ref, lb_ref, fg_ref, fb_ref)
    )

    kvg = kv

    counters = {"s": 0, "r": 0, "l": 0}
    sends = []
    sends_if = []
    local = []

    def new(kind, count=1):
        base = counters[kind]
        counters[kind] = base + count
        return base

    def put(src, dst, recv, axis, peer):
        d = pltpu.make_async_remote_copy(
            src, dst, ssem.at[new("s")], rsem.at[recv], device_id={axis: peer}, device_id_type=MESH
        )
        d.start()
        sends.append(d)
        return d

    def put_if(cond, src, dst, recv, peer):
        sem = ssem.at[new("s")]

        def copy():
            return pltpu.make_async_remote_copy(
                src, dst, sem, rsem.at[recv], device_id={"wide": peer}, device_id_type=MESH
            )

        @pl.when(cond)
        def _():
            copy().start()

        sends_if.append((cond, copy))

    def got(dst, recv):
        pltpu.make_async_remote_copy(
            dst, dst, ssem.at[0], rsem.at[recv], device_id={"narrow": mate}, device_id_type=MESH
        ).wait_recv()

    def here(src, dst, keep=True):
        d = pltpu.make_async_copy(src, dst, lsem.at[new("l")])
        d.start()
        if keep:
            local.append(d)
        return d

    def rows(ref, start, count):
        return ref.at[pl.ds(start, count), :]

    def al(v, m):
        return pl.multiple_of(v, m)

    def npeer(k):
        return lax.rem(n + k, N)

    def nsrc(k):
        return lax.rem(n + N - k, N)

    def wpeer(k):
        return lax.rem(w + k, W)

    def wsrc(k):
        return lax.rem(w + W - k, W)

    media_in = [here(rows(media_h, c * CH, CH), rows(media, c * CH, CH), False) for c in range(NC)]
    down_in = here(down_h, down, False)
    up_in = here(up_h, up, False)

    def own_kv(i, carry):
        v = wkv_ref[pl.ds(i * 16, 16)].astype(F32)
        at = pl.ds(al(w * S + i * 16, 16), 16)
        kvw[at, 0:C] = v[:, 0, :].astype(BF16)
        kvw[at, C : 2 * C] = v[:, 1, :].astype(BF16)
        return carry

    lax.fori_loop(0, S // 16, own_kv, 0)

    barrier = pltpu.get_barrier_semaphore()
    for k in range(1, N):
        pl.semaphore_signal(barrier, inc=1, device_id={"narrow": npeer(k)}, device_id_type=MESH)
    for k in range(1, W):
        pl.semaphore_signal(barrier, inc=1, device_id={"wide": wpeer(k)}, device_id_type=MESH)
    pl.semaphore_wait(barrier, N - 1 + W - 1)

    pos = lax.div(w, 2)
    above, below = pos < W2 - 1, pos > 0

    def wide_gather(src, at, start=True):
        across = new("r")
        up, down, up_across, down_across = (new("r", W2) for _ in range(4))

        def begin():
            put_if(above, src, at(w), up + 1, wpeer(2))
            put_if(below, src, at(w), down + 1, wsrc(2))
            put(src, at(w), across, "wide", partner)

        if start:
            begin()

        def forward(k):
            for arrives, onward, b, flow, to, flow_across in (
                (pos >= k, above, wsrc(2 * k), up, wpeer(2), up_across),
                (pos + k < W2, below, wpeer(2 * k), down, wsrc(2), down_across),
            ):

                @pl.when(arrives)
                def _(b=b, flow=flow):
                    got(at(b), flow + k)

                if k < W2 - 1:
                    put_if(arrives & onward, at(b), at(b), flow + k + 1, to)
                put_if(arrives, at(b), at(b), flow_across + k, partner)

        def finish():
            got(at(partner), across)
            for k in range(1, W2):

                @pl.when(pos >= k)
                def _(k=k):
                    got(at(lax.rem(partner + W - 2 * k, W)), up_across + k)

                @pl.when(pos + k < W2)
                def _(k=k):
                    got(at(lax.rem(partner + 2 * k, W)), down_across + k)

        return (forward, finish) if start else (forward, finish, begin)

    def small_gather(src, at):
        direct = new("r", W2)
        fwd = new("r", W2)
        for k in range(1, W2):
            put(src, at(w), direct + k, "wide", wpeer(2 * k))

        put(src, at(w), direct, "wide", partner)

        def forward(k):
            b = wsrc(2 * k)
            got(at(b), direct + k)
            put(at(b), at(b), fwd + k, "wide", partner)

        def finish():
            got(at(partner), direct)
            for k in range(1, W2):
                b = lax.rem(partner + W - 2 * k, W)
                got(at(b), fwd + k)

        return forward, finish

    def blocks(buf, count):
        return lambda b: rows(buf, al(b * count, 16), count)

    half_of = lambda c: pl.ds(al(c * (L // 2), 16), L // 2)
    mine_half, mate_half = half_of(core), half_of(1 - core)

    def hand_over(buf, base):
        for k in range(1, W):
            at = buf.at[wsrc(k), mine_half, :]
            put(at, at, base + k, "narrow", mate)

        def finish():
            for k in range(1, W):
                got(buf.at[wsrc(k), mate_half, :], base + k)

        return finish

    def row_gather(buf):
        at = lambda b: buf.at[b, mine_half, :]
        forward, finish = small_gather(at(w), at)
        base = new("r", W)

        def share():
            finish()
            return hand_over(buf, base)

        return forward, share

    def spread(which, value):
        for b in range(W):
            sl_st[which, b] = value[:, b * S : (b + 1) * S]
        base = new("r", W)
        base2 = new("r", W)
        for k in range(1, W):
            put(
                sl_st.at[which, wpeer(k), mine_half, :], sl_rc.at[which, w, mine_half, :],
                base + k, "wide", wpeer(k),
            )
        sl_rc[which, w] = sl_st[which, w]

        def share():
            for k in range(1, W):
                got(sl_rc.at[which, wsrc(k), mine_half, :], base + k)
            return hand_over(sl_rc.at[which], base2)

        return share

    own_w = [
        here(wq_h, rows(wq, al(w * S, 16), S), False),
        here(wot_h, rows(wot, al(w * S, 16), S), False),
    ]
    kv_fwd, kv_fin = wide_gather(rows(kvw, al(w * S, 16), S), blocks(kvw, S))
    q_fwd, q_fin = wide_gather(wq_h, blocks(wq, S))
    o_fwd, o_fin, o_begin = wide_gather(wot_h, blocks(wot, S), False)

    lat = lat_ref[...].astype(F32)
    lat_mean, lat_istd, lat_hat = norm_stats(lat)
    lat_ag[n] = (lat_hat * gain_l + bias_l).astype(BF16)
    cot_ag[n] = cot_ref[...]

    def narrow_gather(buf):
        base = new("r", N)
        for k in range(1, N):
            put(buf.at[n], buf.at[n], base + k, "narrow", npeer(k))

        def finish():
            for k in range(1, N):
                got(buf.at[nsrc(k)], base + k)
            return jnp.concatenate([buf[i].astype(F32) for i in range(N)], axis=0).astype(BF16)

        return finish

    te32[...] = te_ref[...].astype(F32)

    m_direct = new("r", NC * X)
    m_fwd = new("r", NC * X)

    def m_rows(block, c):
        return rows(x_all, al(block * Mo + c * CH, 16), CH)

    def frame_of(c):
        return lax.div(n * Mo + c * CH, PATCHES)

    for c in range(NC):
        media_in[c].wait()
        te_row = te32[pl.ds(frame_of(c), 1), :]

        def norm_rows(i, carry, c=c, te_row=te_row):
            r = al(c * CH + i * 16, 16)
            v = media[pl.ds(r, 16), :].astype(F32) + te_row
            mean, inv_std, hat = norm_stats(v)
            mean_s[pl.ds(r, 16), :] = jnp.broadcast_to(mean, (16, LANES))
            istd_s[pl.ds(r, 16), :] = jnp.broadcast_to(inv_std, (16, LANES))
            x_all[pl.ds(al(n * Mo + r, 16), 16), :] = (hat * gain_m + bias_m).astype(BF16)
            return carry

        lax.fori_loop(0, CH // 16, norm_rows, 0, unroll=2)
        for j in range(1, X):
            peer = lax.rem(xpos + j, X) * 2 + core
            put(m_rows(n, c), m_rows(n, c), m_direct + c * X + j, "narrow", peer)
        put(m_rows(n, c), m_rows(n, c), m_direct + c * X, "narrow", mate)
        if c == 0:
            lat_fin = narrow_gather(lat_ag)
            cot_fin = narrow_gather(cot_ag)

    def media_forward(c):
        for j in range(1, X):
            block = lax.rem(xpos + X - j, X) * 2 + core
            got(m_rows(block, c), m_direct + c * X + j)
            put(m_rows(block, c), m_rows(block, c), m_fwd + c * X + j, "narrow", mate)

    kv_fwd(1)

    slot_frame = lax.div(lax.broadcasted_iota(jnp.int32, (M // LANES, LANES), 0), PATCHES // LANES)
    ok = (slot_frame < fc_ref[0]) & (mm_ref[...] > 0)
    okf = jnp.where(ok, 1.0, 0.0).astype(F32)
    tail = jnp.where(
        lax.broadcasted_iota(jnp.int32, (1, KT - M), 1) < L, 1.0, 0.0
    ).astype(F32)
    for j in range(KT // LANES):
        row = okf[j : j + 1, :] if j < M // LANES else tail[:, j * LANES - M : j * LANES - M + LANES]
        mt[j * LANES : (j + 1) * LANES, :] = jnp.broadcast_to(row, (LANES, LANES)).T
    count = jnp.sum(okf, keepdims=True) + float(L)
    cnt_ag[w] = jnp.broadcast_to(count, (8, LANES))
    cnt_base = new("r", W)
    for k in range(1, W):
        put(cnt_ag.at[w], cnt_ag.at[w], cnt_base + k, "wide", wpeer(k))

    if W2 > 2:
        kv_fwd(2)
    o_begin()
    media_forward(0)

    lat_all = lat_fin()
    cot_all = cot_fin()
    x_all[M : M + L, :] = lat_all
    if KT > M + L:
        x_all[M + L : KT, :] = jnp.zeros((KT - M - L, D), BF16)
    cot_g[w] = cot_all

    down_in.wait()

    def act_grad(j, carry):
        r = al(j * 256, 256)
        ga[:, pl.ds(r, 256)] = nt(cot_all, down[pl.ds(r, 256), :])
        return carry

    lax.fori_loop(0, F // 256, act_grad, 0)

    q_fwd(1)
    for k in range(3, W2):
        kv_fwd(k)
    for c in range(1, NC - 1):
        media_forward(c)
    for k in range(2, W2):
        q_fwd(k)
    for d in own_w:
        d.wait()
    kv_fin()

    def project(start, count):
        def step(i, carry):
            r = al(start + i * CH, 16)
            kv[pl.ds(r, CH), :] = nn(x_all[pl.ds(r, CH), :], kvw[...]).astype(BF16)
            return carry

        lax.fori_loop(0, count // CH, step, 0)

    def project_far(c):
        for j in range(1, X):
            block = lax.rem(xpos + X - j, X) * 2 + core
            project(block * Mo + c * CH, CH)

    def project_mate(c):
        for j in range(1, X):
            block = lax.rem(xpos + X - j, X) * 2 + 1 - core
            got(m_rows(block, c), m_fwd + c * X + j)
            project(block * Mo + c * CH, CH)

    project(n * Mo, Mo)
    project(M, KT - M)
    for c in range(NC):
        got(m_rows(mate, c), m_direct + c * X)
    project(mate * Mo, Mo)
    for c in range(NC - 1):
        project_far(c)
        project_mate(c)
    o_fwd(1)
    if NC > 1:
        media_forward(NC - 1)
    project_far(NC - 1)
    q_fin()
    q_act = nn(lat_all, wq[...]).astype(BF16).astype(F32)
    head_of = lax.div(lax.broadcasted_iota(jnp.int32, (L, C), 1), HEAD_DIM)

    def per_head(v):
        return jnp.concatenate([jnp.where(head_of == h, v, 0.0) for h in range(HL)], axis=0)

    def from_heads(v):
        total = jnp.where(head_of == 0, v[0:L], 0.0)
        for h in range(1, HL):
            total = total + jnp.where(head_of == h, v[h * L : (h + 1) * L], 0.0)
        return total

    q_big32 = per_head(q_act)
    q_big = q_big32.astype(BF16)
    q_big_t = q_big32.T.astype(BF16)
    project_mate(NC - 1)
    for k in range(2, W2 - 1):
        o_fwd(k)

    KB = 128

    def wide_mask(r):
        m = mt[pl.ds(r, KB), :]
        return jnp.concatenate([m] * (R // LANES), axis=1) > 0.0

    def score_step(j, top):
        r = al(j * KB, KB)
        s = nn(kv[pl.ds(r, KB), 0:C], q_big_t) * scale
        s = jnp.where(wide_mask(r), s, NEG)
        st[pl.ds(r, KB), :] = s
        return jnp.maximum(top, jnp.max(s, axis=0, keepdims=True))

    top = lax.fori_loop(0, KT // KB, score_step, jnp.full((1, R), NEG, F32))

    def exp_step(j, carry):
        total, dot = carry
        r = al(j * KB, KB)
        s = st[pl.ds(r, KB), :]
        e = jnp.exp(s - top)
        pt[pl.ds(r, KB), :] = e
        s = jnp.where(wide_mask(r), s, 0.0)
        st[pl.ds(r, KB), :] = s
        return (
            total + jnp.sum(e, axis=0, keepdims=True),
            dot + jnp.sum(e * s, axis=0, keepdims=True),
        )

    zero_row = jnp.zeros((1, R), F32)
    total, dot = lax.fori_loop(0, KT // KB, exp_step, (zero_row, zero_row))
    inv_total = 1.0 / total
    mean_score = dot * inv_total

    def prob_step(j, carry):
        r = al(j * KB, KB)
        pr = pt[pl.ds(r, KB), :] * inv_total
        pt[pl.ds(r, KB), :] = pr
        pn[:, pl.ds(r, KB)] = pr.T.astype(BF16)
        return carry

    o_fwd(W2 - 1)
    lax.fori_loop(0, KT // KB, prob_step, 0)
    attn = from_heads(nn(pn[...], kv[:, C : 2 * C]))
    attn_low = attn.astype(BF16)

    cot_fwd, cot_share = row_gather(cot_g)
    slat_share = spread(0, lat_all)
    at_w = lambda ref: rows(ref, al(w * L, 16), L)
    att_g[pl.ds(al(w * L, 16), L), :] = attn_low

    def narrow_sum(slot, parts):
        base = new("r", N)
        for k in range(1, N):
            put(rs_st.at[slot, npeer(k)], rs_rc.at[slot, k], base + k, "narrow", npeer(k))

        def finish():
            v = rs_st[slot, n].astype(F32)
            for k in range(1, N):
                got(rs_rc.at[slot, k], base + k)
                v = v + rs_rc[slot, k].astype(F32)
            return v

        return finish

    def stage(slot, cols, v):
        for i in range(N):
            rs_st[slot, i, :, cols] = v[i * Lo : (i + 1) * Lo].astype(BF16)

    o_fin()

    def branch_step(j, carry):
        r = al(j * 256, 256)
        stage(0, pl.ds(r, 256), nt(attn_low, wot[pl.ds(r, 256), :]))
        return carry

    lax.fori_loop(0, D // 256, branch_step, 0)
    branch_fin = narrow_sum(0, None)
    mid = lat + branch_fin()
    mid_mean, mid_istd, mid_hat = norm_stats(mid)
    hid_ag[n] = (mid_hat * gain_f + bias_f).astype(BF16)
    hid_fin = narrow_gather(hid_ag)
    up_in.wait()
    hid_all = hid_fin()
    hid_g[w] = hid_all
    hid_fwd, hid_share = row_gather(hid_g)
    att_fwd, att_fin = small_gather(at_w(att_g), blocks(att_g, L))

    own64 = pl.ds(al(w * L, 16), L)

    def ffn_step(j, carry):
        cs = pl.ds(al(j * 256, 256), 256)
        pre = nn(hid_all, up[:, cs])
        cdf = 0.5 * (1.0 + lax.erf(pre * (1.0 / math.sqrt(2.0))))
        density = jnp.exp(-0.5 * pre * pre) * (1.0 / math.sqrt(2.0 * math.pi))
        act_own[:, cs] = (pre * cdf).astype(BF16)
        pre_own[:, cs] = (ga[:, cs] * (cdf + pre * density)).astype(BF16)
        return carry

    lax.fori_loop(0, F // 256, ffn_step, 0)
    gpre = pre_own[...]

    def hid_back(j, carry):
        r = al(j * 256, 256)
        stage(1, pl.ds(r, 256), nt(gpre, up[pl.ds(r, 256), :]))
        return carry

    lax.fori_loop(0, D // 256, hid_back, 0)
    ghid_fin = narrow_sum(1, None)
    act_all = act_own[...]

    def ffn_out(j, carry):
        cs = pl.ds(al(j * 256, 256), 256)
        stage(2, cs, nn(act_all, down[:, cs]))
        return carry

    lax.fori_loop(0, D // 256, ffn_out, 0)
    ffn_fin = narrow_sum(2, None)
    for k in range(1, W2):
        cot_fwd(k)

    ghid = ghid_fin()
    grad_mid = cot_ref[...].astype(F32) + norm_back(ghid, mid_hat, mid_istd, gain_f)
    gb_ag[n] = grad_mid.astype(BF16)
    gb_fin = narrow_gather(gb_ag)
    acc8[...] = jnp.zeros_like(acc8)
    stat[...] = jnp.zeros_like(stat)
    stat[FRAMES_MAX + 4 : FRAMES_MAX + 5, :] = jnp.sum(ghid * mid_hat, axis=0, keepdims=True)
    stat[FRAMES_MAX + 5 : FRAMES_MAX + 6, :] = jnp.sum(ghid, axis=0, keepdims=True)
    hid_fwd(1)
    for k in range(1, W):
        got(cnt_ag.at[wsrc(k)], cnt_base + k)
    keys = cnt_ag[0]
    for i in range(1, W):
        keys = keys + cnt_ag[i]
    ent1 = ENT_COEF * float(W * M) / keys[0:1, :]
    ent = jnp.concatenate([ent1] * (R // LANES), axis=1)
    gb_all = gb_fin()
    sgb_share = spread(1, gb_all)

    g_attn = nn(gb_all, wot[...]).astype(BF16).astype(F32)
    g_big32 = per_head(g_attn)
    g_big = g_big32.astype(BF16)
    g_big_t = g_big32.T.astype(BF16)
    row_dot = jnp.sum(per_head(g_attn * attn).T, axis=0, keepdims=True)
    shift = row_dot - ent * mean_score

    def back_step(j, carry):
        r = al(j * KB, KB)
        pr = pt[pl.ds(r, KB), :]
        gp = nn(kv[pl.ds(r, KB), C : 2 * C], g_big_t)
        gs = pr * (gp - ent * st[pl.ds(r, KB), :] - shift)
        pn[:, pl.ds(r, KB)] = gs.T.astype(BF16)
        gpair[pl.ds(r, KB), 0:C] = (nn(gs.astype(BF16), q_big) * scale).astype(BF16)
        gpair[pl.ds(r, KB), C : 2 * C] = nn(pr.astype(BF16), g_big).astype(BF16)
        return carry

    lax.fori_loop(0, KT // KB // 2, back_step, 0)
    for k in range(2, W2):
        hid_fwd(k)
    lax.fori_loop(KT // KB // 2, KT // KB, back_step, 0)

    gq = (from_heads(nn(pn[...], kv[:, 0:C])) * scale).astype(BF16)
    gq_g[own64, :] = gq
    gq_fwd, gq_fin = small_gather(at_w(gq_g), blocks(gq_g, L))

    H = W2 // 2
    half = lax.div(w, 2)
    order = [(lax.rem(half + k, H) + (1 - lax.div(half, H)) * H) for k in range(H)]
    order += [(lax.rem(half + k, H) + lax.div(half, H) * H) for k in list(range(1, H)) + [0]]
    y_base = new("r", W2)
    z_base = new("r", W2)

    def kvg_rows(first):
        def step(j, carry):
            r = al(first * (D // 2) + j * 256, 256)
            kvg[pl.ds(r, 256), :] = tn(x_all[:, pl.ds(r, 256)], gpair[...]).astype(BF16)
            return carry

        lax.fori_loop(0, D // 512, step, 0)

    def kvg_to_partner(i):
        put(
            rows(kvg, al((2 * order[i] + 1 - par) * S, 16), S), rows(kvg_y, i * S, S),
            y_base + i, "wide", partner,
        )

    def kvg_step(i):
        g = order[i]
        got(rows(kvg_y, i * S, S), y_base + i)
        mine = pl.ds(al((2 * g + par) * S, 16), S)
        summed = kvg[mine, :].astype(F32) + kvg_y[i * S : (i + 1) * S, :].astype(F32)
        if i < W2 - 1:
            kvg[mine, :] = summed.astype(BF16)
            put(kvg.at[mine, :], rows(kvg_z, i * S, S), z_base + i, "wide", 2 * g + par)
        else:
            o_kv[...] = summed

    kvg_rows(1 - lax.div(half, H))
    for i in range(H):
        kvg_to_partner(i)

    mate_base = new("r", X * NC)
    xs_base = new("r", X * NC)

    def part(block, c):
        r = al(block * Mo + c * CH, 16)
        return nt(gpair[pl.ds(r, CH), :], kvw[...])

    mate_sent = {}

    def x_of(j):
        return lax.rem(xpos + j, X)

    def to_mate(j, c):
        b = x_of(j) * 2 + 1 - core
        if c in mate_sent:
            mate_sent[c].wait_send()
            sends[:] = [d for d in sends if d is not mate_sent[c]]
        mate_st[c * CH : (c + 1) * CH, :] = part(b, c).astype(BF16)
        mate_sent[c] = put(
            rows(mate_st, c * CH, CH), rows(mate_rc, (j * NC + c) * CH, CH), mate_base + j * NC + c, "narrow", mate
        )

    def from_mate(j, c):
        i = (j * NC + c) * CH
        got(rows(mate_rc, i, CH), mate_base + j * NC + c)
        return part(x_of(j) * 2 + core, c) + mate_rc[i : i + CH, :].astype(F32)

    def rows_out(j, cs):
        for c in cs:
            to_mate(j, c)
        for c in cs:
            i = ((j - 1) * NC + c) * CH
            x_st[i : i + CH, :] = from_mate(j, c).astype(BF16)
            put(
                rows(x_st, i, CH), rows(x_rc, i, CH), xs_base + (j - 1) * NC + c,
                "narrow", x_of(j) * 2 + core,
            )

    rows_out(1, range(NC // 2))
    kvg_rows(lax.div(half, H))
    for i in range(H, W2):
        kvg_to_partner(i)

    gpl = gpair[M : M + L, :]

    def lat_back(j, carry):
        r = al(j * 256, 256)
        stage(3, pl.ds(r, 256), nt(gpl, kvw[pl.ds(r, 256), :]) + nt(gq, wq[pl.ds(r, 256), :]))
        return carry

    lax.fori_loop(0, D // 256, lat_back, 0)
    glat_fin = narrow_sum(3, None)
    rows_out(1, range(NC // 2, NC))
    for j in range(2, X):
        rows_out(j, range(NC))
    for k in range(1, W2):
        att_fwd(k)
    slat_fin = slat_share()
    cot_fin = cot_share()
    hid_fin = hid_share()
    sgb_fin = sgb_share()
    for c in range(NC):
        to_mate(0, c)
    for c in range(NC):
        own_sum[c * CH : (c + 1) * CH, :] = from_mate(0, c)
    third = [i * W2 // 4 for i in range(5)]
    for i in range(third[0], third[1]):
        kvg_step(i)

    cot_fin()
    hid_fin()
    pick = (
        lax.broadcasted_iota(jnp.int32, (D, S), 0) == lax.broadcasted_iota(jnp.int32, (D, S), 1) + w * S
    ).astype(F32).astype(BF16)
    cot_rows = lambda: cot_g[...].reshape(W * L, D)
    hid_rows = lambda: hid_g[...].reshape(W * L, D)

    def pick_step(b, carry):
        at = pl.ds(al(b * L, 16), L)
        cot_sl[at, :] = nn(cot_g[b], pick).astype(BF16)
        hid_sl[at, :] = nn(hid_g[b], pick).astype(BF16)
        return carry

    lax.fori_loop(0, W, pick_step, 0)

    def unit_step(j, carry):
        cs = pl.ds(al(j * 256, 256), 256)
        pre = nn(hid_rows(), up[:, cs])
        grad = nt(cot_rows(), down[cs, :])
        cdf = 0.5 * (1.0 + lax.erf(pre * (1.0 / math.sqrt(2.0))))
        density = jnp.exp(-0.5 * pre * pre) * (1.0 / math.sqrt(2.0 * math.pi))
        o_down[:, cs] = tn(cot_sl[...], (pre * cdf).astype(BF16))
        o_up[:, cs] = tn(hid_sl[...], (grad * (cdf + pre * density)).astype(BF16))
        return carry

    units = F // 256
    for t in range(3):
        lax.fori_loop(t * units // 3, (t + 1) * units // 3, unit_step, 0)
        for i in range(third[t + 1], third[t + 2]):
            kvg_step(i)
    here(o_up, out_up)
    here(o_down, out_down)

    out_l = (mid + ffn_fin()).astype(BF16)
    lat_nf[0] = out_l
    here(lat_nf.at[0], out_lat)
    glat = glat_fin()
    g_lat = grad_mid + norm_back(glat, lat_hat, lat_istd, gain_l)
    lat_nf[1] = g_lat.astype(BF16)
    here(lat_nf.at[1], out_gl)
    stat[FRAMES_MAX + 2 : FRAMES_MAX + 3, :] = jnp.sum(glat * lat_hat, axis=0, keepdims=True)
    stat[FRAMES_MAX + 3 : FRAMES_MAX + 4, :] = jnp.sum(glat, axis=0, keepdims=True)

    for k in range(1, W2):
        gq_fwd(k)
    att_fin()
    sgb_fin()
    o_o[...] = tn(sl_rc[1].reshape(W * L, S), att_g[...])
    here(o_o, out_o)
    gq_fin()
    slat_fin()
    o_q[...] = tn(sl_rc[0].reshape(W * L, S), gq_g[...])
    here(o_q, out_q)

    gm_out = []
    for c in range(NC):
        for j in range(1, X):
            i = ((j - 1) * NC + c) * CH
            got(rows(x_rc, i, CH), xs_base + (j - 1) * NC + c)
        f = frame_of(c)
        te_row = te32[pl.ds(f, 1), :]

        def back_rows(i, carry, c=c, te_row=te_row):
            r = al(c * CH + i * 16, 16)
            dy = own_sum[pl.ds(r, 16), :]
            for j in range(1, X):
                dy = dy + x_rc[pl.ds(al((j - 1) * Mo + r, 16), 16), :].astype(F32)
            mean = mean_s[pl.ds(r, 16), 0:1]
            inv_std = istd_s[pl.ds(r, 16), 0:1]
            hat = (media[pl.ds(r, 16), :].astype(F32) + te_row - mean) * inv_std
            dx = norm_back(dy, hat, inv_std, gain_m)
            media[pl.ds(r, 16), :] = dx.astype(BF16)
            acc8[0:8, :] += fold8(dy * hat)
            acc8[8:16, :] += fold8(dy)
            acc8[16:24, :] += fold8(dx)
            return carry

        lax.fori_loop(0, CH // 16, back_rows, 0)
        stat[pl.ds(f, 1), :] += jnp.sum(acc8[16:24, :], axis=0, keepdims=True)
        acc8[16:24, :] = jnp.zeros((8, D), F32)
        here(rows(media, c * CH, CH), rows(out_gm, c * CH, CH))
    stat[FRAMES_MAX : FRAMES_MAX + 1, :] = jnp.sum(acc8[0:8, :], axis=0, keepdims=True)
    stat[FRAMES_MAX + 1 : FRAMES_MAX + 2, :] = jnp.sum(acc8[8:16, :], axis=0, keepdims=True)

    vec = stat[...]
    for b in range(W):
        vec_st[b] = vec[:, b * S : (b + 1) * S]
    v_base = new("r", W)
    for k in range(1, W):
        put(vec_st.at[wpeer(k)], vec_rc.at[k], v_base + k, "wide", wpeer(k))
    for i in range(W2 - 1):
        got(rows(kvg_z, i * S, S), z_base + i)
        o_kv[...] += kvg_z[i * S : (i + 1) * S, :].astype(F32)
    here(o_kv, out_kv)
    vs = vec_st[w]
    for k in range(1, W):
        got(vec_rc.at[k], v_base + k)
        vs = vs + vec_rc[k]
    for i in range(N):
        vec2_st[i] = vs[:, i * V : (i + 1) * V]
    v2_base = new("r", N)
    for k in range(1, N):
        put(vec2_st.at[npeer(k)], vec2_rc.at[k], v2_base + k, "narrow", npeer(k))
    vs = vec2_st[n]
    for k in range(1, N):
        got(vec2_rc.at[k], v2_base + k)
        vs = vs + vec2_rc[k]
    o_vec[...] = vs
    here(o_vec, out_vec)

    for d in sends:
        d.wait_send()
    for cond, copy in sends_if:

        @pl.when(cond)
        def _(copy=copy):
            copy().wait_send()

    for d in local:
        d.wait()
    sem_counts.update(counters)


def finish_kernel(p, pieces, *refs):
    src, dst, buf, sem_in, sem_out = refs[:9], refs[9:24], refs[24:33], refs[33], refs[34]
    V, C = p.V, p.C
    loads = []
    for i in range(9):
        count = src[i].shape[0] // pieces[i]
        for c in range(pieces[i]):
            at = pl.ds(c * count, count)
            d = pltpu.make_async_copy(src[i].at[at, :], buf[i].at[at, :], sem_in.at[len(loads)])
            d.start()
            loads.append((i, at, d))
    stores = []

    def store(a, b):
        d = pltpu.make_async_copy(a, b, sem_out.at[len(stores)])
        d.start()
        stores.append(d)

    first = {0: 0, 1: 1, 2: 2, 4: 10, 5: 11, 6: 12, 7: 13, 8: 14}
    for i, at, d in loads:
        d.wait()
        if i == 3:
            store(buf[3].at[pl.ds(0, FRAMES_MAX), :], dst[3])
            for k in range(6):
                store(buf[3].at[FRAMES_MAX + k], dst[4 + k])
        elif i == 5 and C % LANES == 0:
            for k in range(2):
                store(buf[5].at[:, pl.ds(k * C, C)], dst[11].at[:, k, :])
        else:
            store(buf[i].at[at, :], dst[first[i]].at[at, :])
    for d in stores:
        d.wait()


def finish(p, outs):
    sds = jax.ShapeDtypeStruct
    hbm = pl.BlockSpec(memory_space=pl.ANY)
    pieces = [1, 4, 1, 1, 1, 1, 1, 2, 2]
    shapes = [sds(a.shape, a.dtype) for a in outs]
    vec = [sds((FRAMES_MAX, p.V), F32)] + [sds((p.V,), F32)] * 6
    res = pl.pallas_call(
        functools.partial(finish_kernel, p, pieces),
        out_shape=tuple(shapes[:3] + vec + [shapes[4], sds((p.S, 2, p.C), F32) if p.C % LANES == 0 else shapes[5]] + shapes[6:]),
        in_specs=[hbm] * 9,
        out_specs=[hbm] * 15,
        scratch_shapes=[pltpu.VMEM(a.shape, a.dtype) for a in outs]
        + [pltpu.SemaphoreType.DMA((sum(pieces),)), pltpu.SemaphoreType.DMA((sum(pieces) + 7,))],
        compiler_params=pltpu.CompilerParams(has_side_effects=True),
    )(*outs)
    return res[0], res[1], res[2], res[3:10], res[10], res[11].reshape(p.S, 2, p.C), res[12], res[13], res[14]


def make_body(mesh):
    def body(
        media_feats, latents, frame_counts, media_mask, time_embed, media_gain, media_bias, latent_gain,
        latent_bias, ffn_gain, ffn_bias, query_weight, keyval_weight, output_weight, up_weight,
        down_weight, cotangent,
    ):
        p = Plan(mesh, media_feats, latents, up_weight)
        D, C, S, L, Lo, KT, R, F, N, W, Mo = p.D, p.C, p.S, p.L, p.Lo, p.KT, p.R, p.F, p.N, p.W, p.Mo
        X, W2, NC, V = p.X, p.W2, p.NC, p.V
        vm = pl.BlockSpec(memory_space=pltpu.VMEM)
        hbm = pl.BlockSpec(memory_space=pl.ANY)
        smem = pl.BlockSpec(memory_space=pltpu.SMEM)
        sds = jax.ShapeDtypeStruct
        vmem = pltpu.VMEM
        scratch = [
            vmem((Mo, D), BF16),
            vmem((KT, D), BF16),
            vmem((D, 2 * C), BF16),
            vmem((D, C), BF16),
            vmem((D, C), BF16),
            vmem((D, F), BF16),
            vmem((F, D), BF16),
            vmem((KT, 2 * C), BF16),
            vmem((KT, R), F32),
            vmem((KT, R), F32),
            vmem((R, KT), BF16),
            vmem((KT, 2 * C), BF16),
            vmem((KT, LANES), F32),
            vmem((FRAMES_MAX, D), F32),
            vmem((Mo, LANES), F32),
            vmem((Mo, LANES), F32),
            vmem((2, Lo, D), BF16),
            vmem((N, Lo, D), BF16),
            vmem((N, Lo, D), BF16),
            vmem((W, 8, LANES), F32),
            vmem((4, N, Lo, D), BF16),
            vmem((4, N, Lo, D), BF16),
            vmem((N, Lo, D), BF16),
            vmem((N, Lo, D), BF16),
            vmem((Mo, D), BF16),
            vmem((X * Mo, D), BF16),
            vmem(((X - 1) * Mo, D), BF16),
            vmem(((X - 1) * Mo, D), BF16),
            vmem((Mo, D), F32),
            vmem((W2 * S, 2 * C), BF16),
            vmem((W2 * S, 2 * C), BF16),
            vmem((L, F), BF16),
            vmem((L, F), BF16),
            vmem((W, L, D), BF16),
            vmem((W, L, D), BF16),
            vmem((W * L, C), BF16),
            vmem((W * L, C), BF16),
            vmem((2, W, L, S), BF16),
            vmem((2, W, L, S), BF16),
            vmem((W * L, S), BF16),
            vmem((W * L, S), BF16),
            vmem((L, F), F32),
            vmem((24, D), F32),
            vmem((16, D), F32),
            vmem((W, 16, S), F32),
            vmem((W, 16, S), F32),
            vmem((N, 16, V), F32),
            vmem((N, 16, V), F32),
            vmem((S, F), F32),
            vmem((S, F), F32),
            vmem((S, C), F32),
            vmem((S, C), F32),
            vmem((S, 2 * C), F32),
            vmem((16, V), F32),
            pltpu.SemaphoreType.DMA((40 * W + 8 * N * p.NC + 64,)),
            pltpu.SemaphoreType.DMA((40 * W + 8 * N * p.NC + 64,)),
            pltpu.SemaphoreType.DMA((64,)),
        ]
        outs = pl.pallas_call(
            functools.partial(body_kernel, p, {}),
            out_shape=(
                sds((Lo, D), BF16),
                sds((Mo, D), BF16),
                sds((Lo, D), BF16),
                sds((16, V), F32),
                sds((S, C), F32),
                sds((S, 2 * C), F32),
                sds((S, C), F32),
                sds((S, F), F32),
                sds((S, F), F32),
            ),
            in_specs=[hbm, vm, smem, vm, vm, vm, vm, vm, vm, vm, vm, hbm, vm, hbm, hbm, hbm, vm],
            out_specs=[hbm] * 9,
            scratch_shapes=scratch,
            compiler_params=pltpu.CompilerParams(
                collective_id=0, has_side_effects=True, vmem_limit_bytes=67_043_328
            ),
        )(
            media_feats[0], latents[0], frame_counts, media_mask.reshape(p.M // LANES, LANES), time_embed,
            media_gain, media_bias, latent_gain, latent_bias, ffn_gain, ffn_bias,
            query_weight, keyval_weight, output_weight.T, up_weight, down_weight, cotangent[0],
        )
        lat, gm, gl, vec, gq, gkv, go, gup, gdown = finish(p, outs)
        return (lat[None], gm[None], gl[None]) + tuple(vec) + (gq, gkv, go.T, gup, gdown.T)

    return body


def solution(mesh):
    both = P(("wide", "narrow"))
    rows = P("wide", "narrow", None)
    return jax.shard_map(
        make_body(mesh),
        mesh=mesh,
        in_specs=(
            rows, rows, P("wide"), P("wide", None), P(), P(), P(), P(), P(), P(), P(), P("wide", "narrow"),
            P("wide", None, "narrow"), P("narrow", "wide"), P(None, "narrow"), P("narrow", None), rows,
        ),
        out_specs=(
            rows, rows, rows, P(None, ("wide", "narrow")), both, both, both, both, both, both,
            P("wide", "narrow"), P("wide", None, "narrow"), P("narrow", "wide"), P("wide", "narrow"),
            P("narrow", "wide"),
        ),
        check_vma=False,
    )
```

```python
import functools
import math

import jax
import jax.numpy as jnp
from jax import lax
from jax.experimental import pallas as pl
from jax.experimental.pallas import tpu as pltpu
from jax.sharding import PartitionSpec as P

HEADS = 16
HEAD_DIM = 96
FRAMES_MAX = 8
PATCHES = 256
EPS = 1e-05
ENT_COEF = 4.0
NEG = -1e30
LANES = 128
MESH = pl.DeviceIdType.MESH
F32 = jnp.float32
BF16 = jnp.bfloat16


def nn(a, b):
    return lax.dot_general(a, b, (((1,), (0,)), ((), ())), preferred_element_type=F32)


def nt(a, b):
    return lax.dot_general(a, b, (((1,), (1,)), ((), ())), preferred_element_type=F32)


def tn(a, b):
    return lax.dot_general(a, b, (((0,), (0,)), ((), ())), preferred_element_type=F32)


def rows_mean(v):
    return jnp.mean(v, axis=-1, keepdims=True)


def norm_stats(v):
    mean = rows_mean(v)
    centered = v - mean
    inv_std = lax.rsqrt(rows_mean(centered * centered) + EPS)
    return mean, inv_std, centered * inv_std


def norm_back(dy, hat, inv_std, gain):
    scaled = dy * gain
    return inv_std * (scaled - rows_mean(scaled) - hat * rows_mean(scaled * hat))


def fold8(v):
    return jnp.sum(v.reshape(v.shape[0] // 8, 8, v.shape[1]), axis=0)


class Plan:
    def __init__(self, mesh, media, latents, up):
        self.N = mesh.shape["narrow"]
        self.W = mesh.shape["wide"]
        self.X = self.N // 2
        self.W2 = self.W // 2
        self.Mo, self.D = media.shape[1], media.shape[2]
        self.Lo = latents.shape[1]
        self.M = self.Mo * self.N
        self.L = self.Lo * self.N
        self.HL = HEADS // self.N
        self.C = self.HL * HEAD_DIM
        self.KT = self.M + -(-self.L // LANES) * LANES
        self.F = up.shape[1]
        self.S = self.D // self.W
        self.V = self.S // self.N
        self.R = self.HL * self.L
        self.CH = 128
        self.NC = self.Mo // self.CH


def body_kernel(p, sem_counts, *refs):
    (
        media_h, lat_ref, fc_ref, mm_ref, te_ref, mg_ref, mb_ref, lg_ref, lb_ref, fg_ref, fb_ref,
        wq_h, wkv_ref, wot_h, up_h, down_h, cot_ref,
        out_lat, out_gm, out_gl, out_vec, out_q, out_kv, out_o, out_up, out_down,
        media, x_all, kvw, wq, wot, up, down, kv, st, pt, pn, gpair, mt, te32, mean_s, istd_s,
        lat_nf, lat_ag, cot_ag, cnt_ag,
        rs_st, rs_rc, hid_ag, gb_ag, mate_st, mate_rc, x_st, x_rc, own_sum,
        kvg_y, kvg_z, act_own, pre_own, hid_g, cot_g, att_g, gq_g, sl_st, sl_rc, cot_sl, hid_sl, ga, acc8, stat, vec_st, vec_rc, vec2_st, vec2_rc,
        o_up, o_down, o_o, o_q, o_kv, o_vec, ssem, rsem, lsem,
    ) = refs
    N, W, X, W2 = p.N, p.W, p.X, p.W2
    Mo, Lo, M, L, D, C, R, S, F, KT = p.Mo, p.Lo, p.M, p.L, p.D, p.C, p.R, p.S, p.F, p.KT
    CH, NC, HL, V = p.CH, p.NC, p.HL, p.V
    n = lax.axis_index("narrow")
    w = lax.axis_index("wide")
    core = lax.rem(n, 2)
    xpos = lax.div(n, 2)
    mate = n + 1 - 2 * core
    par = lax.rem(w, 2)
    partner = w + 1 - 2 * par
    scale = HEAD_DIM ** (-0.5)
    gain_m, bias_m, gain_l, bias_l, gain_f, bias_f = (
        ref[...].reshape(1, D) for ref in (mg_ref, mb_ref, lg_ref, lb_ref, fg_ref, fb_ref)
    )

    kvg = kv

    counters = {"s": 0, "r": 0, "l": 0}
    sends = []
    sends_if = []
    local = []

    def new(kind, count=1):
        base = counters[kind]
        counters[kind] = base + count
        return base

    def put(src, dst, recv, axis, peer):
        d = pltpu.make_async_remote_copy(
            src, dst, ssem.at[new("s")], rsem.at[recv], device_id={axis: peer}, device_id_type=MESH
        )
        d.start()
        sends.append(d)
        return d

    def put_if(cond, src, dst, recv, peer):
        sem = ssem.at[new("s")]

        def copy():
            return pltpu.make_async_remote_copy(
                src, dst, sem, rsem.at[recv], device_id={"wide": peer}, device_id_type=MESH
            )

        @pl.when(cond)
        def _():
            copy().start()

        sends_if.append((cond, copy))

    def got(dst, recv):
        pltpu.make_async_remote_copy(
            dst, dst, ssem.at[0], rsem.at[recv], device_id={"narrow": mate}, device_id_type=MESH
        ).wait_recv()

    def here(src, dst, keep=True):
        d = pltpu.make_async_copy(src, dst, lsem.at[new("l")])
        d.start()
        if keep:
            local.append(d)
        return d

    def rows(ref, start, count):
        return ref.at[pl.ds(start, count), :]

    def al(v, m):
        return pl.multiple_of(v, m)

    def npeer(k):
        return lax.rem(n + k, N)

    def nsrc(k):
        return lax.rem(n + N - k, N)

    def wpeer(k):
        return lax.rem(w + k, W)

    def wsrc(k):
        return lax.rem(w + W - k, W)

    media_in = [here(rows(media_h, c * CH, CH), rows(media, c * CH, CH), False) for c in range(NC)]
    down_in = here(down_h, down, False)
    up_in = here(up_h, up, False)

    def own_kv(i, carry):
        v = wkv_ref[pl.ds(i * 16, 16)].astype(F32)
        at = pl.ds(al(w * S + i * 16, 16), 16)
        kvw[at, 0:C] = v[:, 0, :].astype(BF16)
        kvw[at, C : 2 * C] = v[:, 1, :].astype(BF16)
        return carry

    lax.fori_loop(0, S // 16, own_kv, 0)

    barrier = pltpu.get_barrier_semaphore()
    for k in range(1, N):
        pl.semaphore_signal(barrier, inc=1, device_id={"narrow": npeer(k)}, device_id_type=MESH)
    for k in range(1, W):
        pl.semaphore_signal(barrier, inc=1, device_id={"wide": wpeer(k)}, device_id_type=MESH)
    pl.semaphore_wait(barrier, N - 1 + W - 1)

    pos = lax.div(w, 2)
    above, below = pos < W2 - 1, pos > 0

    def wide_gather(src, at, start=True):
        across = new("r")
        up, down, up_across, down_across = (new("r", W2) for _ in range(4))

        def begin():
            put_if(above, src, at(w), up + 1, wpeer(2))
            put_if(below, src, at(w), down + 1, wsrc(2))
            put(src, at(w), across, "wide", partner)

        if start:
            begin()

        def forward(k):
            for arrives, onward, b, flow, to, flow_across in (
                (pos >= k, above, wsrc(2 * k), up, wpeer(2), up_across),
                (pos + k < W2, below, wpeer(2 * k), down, wsrc(2), down_across),
            ):

                @pl.when(arrives)
                def _(b=b, flow=flow):
                    got(at(b), flow + k)

                if k < W2 - 1:
                    put_if(arrives & onward, at(b), at(b), flow + k + 1, to)
                put_if(arrives, at(b), at(b), flow_across + k, partner)

        def finish():
            got(at(partner), across)
            for k in range(1, W2):

                @pl.when(pos >= k)
                def _(k=k):
                    got(at(lax.rem(partner + W - 2 * k, W)), up_across + k)

                @pl.when(pos + k < W2)
                def _(k=k):
                    got(at(lax.rem(partner + 2 * k, W)), down_across + k)

        return (forward, finish) if start else (forward, finish, begin)

    def small_gather(src, at):
        direct = new("r", W2)
        fwd = new("r", W2)
        for k in range(1, W2):
            put(src, at(w), direct + k, "wide", wpeer(2 * k))

        put(src, at(w), direct, "wide", partner)

        def forward(k):
            b = wsrc(2 * k)
            got(at(b), direct + k)
            put(at(b), at(b), fwd + k, "wide", partner)

        def finish():
            got(at(partner), direct)
            for k in range(1, W2):
                b = lax.rem(partner + W - 2 * k, W)
                got(at(b), fwd + k)

        return forward, finish

    def blocks(buf, count):
        return lambda b: rows(buf, al(b * count, 16), count)

    half_of = lambda c: pl.ds(al(c * (L // 2), 16), L // 2)
    mine_half, mate_half = half_of(core), half_of(1 - core)

    def hand_over(buf, base):
        for k in range(1, W):
            at = buf.at[wsrc(k), mine_half, :]
            put(at, at, base + k, "narrow", mate)

        def finish():
            for k in range(1, W):
                got(buf.at[wsrc(k), mate_half, :], base + k)

        return finish

    def row_gather(buf):
        at = lambda b: buf.at[b, mine_half, :]
        forward, finish = small_gather(at(w), at)
        base = new("r", W)

        def share():
            finish()
            return hand_over(buf, base)

        return forward, share

    def spread(which, value):
        for b in range(W):
            sl_st[which, b] = value[:, b * S : (b + 1) * S]
        base = new("r", W)
        base2 = new("r", W)
        for k in range(1, W):
            put(
                sl_st.at[which, wpeer(k), mine_half, :], sl_rc.at[which, w, mine_half, :],
                base + k, "wide", wpeer(k),
            )
        sl_rc[which, w] = sl_st[which, w]

        def share():
            for k in range(1, W):
                got(sl_rc.at[which, wsrc(k), mine_half, :], base + k)
            return hand_over(sl_rc.at[which], base2)

        return share

    own_w = [
        here(wq_h, rows(wq, al(w * S, 16), S), False),
        here(wot_h, rows(wot, al(w * S, 16), S), False),
    ]
    kv_fwd, kv_fin = wide_gather(rows(kvw, al(w * S, 16), S), blocks(kvw, S))
    q_fwd, q_fin = wide_gather(wq_h, blocks(wq, S))
    o_fwd, o_fin, o_begin = wide_gather(wot_h, blocks(wot, S), False)

    lat = lat_ref[...].astype(F32)
    lat_mean, lat_istd, lat_hat = norm_stats(lat)
    lat_ag[n] = (lat_hat * gain_l + bias_l).astype(BF16)
    cot_ag[n] = cot_ref[...]

    def narrow_gather(buf):
        base = new("r", N)
        for k in range(1, N):
            put(buf.at[n], buf.at[n], base + k, "narrow", npeer(k))

        def finish():
            for k in range(1, N):
                got(buf.at[nsrc(k)], base + k)
            return jnp.concatenate([buf[i].astype(F32) for i in range(N)], axis=0).astype(BF16)

        return finish

    te32[...] = te_ref[...].astype(F32)

    m_direct = new("r", NC * X)
    m_fwd = new("r", NC * X)

    def m_rows(block, c):
        return rows(x_all, al(block * Mo + c * CH, 16), CH)

    def frame_of(c):
        return lax.div(n * Mo + c * CH, PATCHES)

    for c in range(NC):
        media_in[c].wait()
        te_row = te32[pl.ds(frame_of(c), 1), :]

        def norm_rows(i, carry, c=c, te_row=te_row):
            r = al(c * CH + i * 16, 16)
            v = media[pl.ds(r, 16), :].astype(F32) + te_row
            mean, inv_std, hat = norm_stats(v)
            mean_s[pl.ds(r, 16), :] = jnp.broadcast_to(mean, (16, LANES))
            istd_s[pl.ds(r, 16), :] = jnp.broadcast_to(inv_std, (16, LANES))
            x_all[pl.ds(al(n * Mo + r, 16), 16), :] = (hat * gain_m + bias_m).astype(BF16)
            return carry

        lax.fori_loop(0, CH // 16, norm_rows, 0, unroll=2)
        for j in range(1, X):
            peer = lax.rem(xpos + j, X) * 2 + core
            put(m_rows(n, c), m_rows(n, c), m_direct + c * X + j, "narrow", peer)
        put(m_rows(n, c), m_rows(n, c), m_direct + c * X, "narrow", mate)
        if c == 0:
            lat_fin = narrow_gather(lat_ag)
            cot_fin = narrow_gather(cot_ag)

    def media_forward(c):
        for j in range(1, X):
            block = lax.rem(xpos + X - j, X) * 2 + core
            got(m_rows(block, c), m_direct + c * X + j)
            put(m_rows(block, c), m_rows(block, c), m_fwd + c * X + j, "narrow", mate)

    kv_fwd(1)

    slot_frame = lax.div(lax.broadcasted_iota(jnp.int32, (M // LANES, LANES), 0), PATCHES // LANES)
    ok = (slot_frame < fc_ref[0]) & (mm_ref[...] > 0)
    okf = jnp.where(ok, 1.0, 0.0).astype(F32)
    tail = jnp.where(
        lax.broadcasted_iota(jnp.int32, (1, KT - M), 1) < L, 1.0, 0.0
    ).astype(F32)
    for j in range(KT // LANES):
        row = okf[j : j + 1, :] if j < M // LANES else tail[:, j * LANES - M : j * LANES - M + LANES]
        mt[j * LANES : (j + 1) * LANES, :] = jnp.broadcast_to(row, (LANES, LANES)).T
    count = jnp.sum(okf, keepdims=True) + float(L)
    cnt_ag[w] = jnp.broadcast_to(count, (8, LANES))
    cnt_base = new("r", W)
    for k in range(1, W):
        put(cnt_ag.at[w], cnt_ag.at[w], cnt_base + k, "wide", wpeer(k))

    if W2 > 2:
        kv_fwd(2)
    o_begin()
    media_forward(0)

    lat_all = lat_fin()
    cot_all = cot_fin()
    x_all[M : M + L, :] = lat_all
    if KT > M + L:
        x_all[M + L : KT, :] = jnp.zeros((KT - M - L, D), BF16)
    cot_g[w] = cot_all

    down_in.wait()

    def act_grad(j, carry):
        r = al(j * 256, 256)
        ga[:, pl.ds(r, 256)] = nt(cot_all, down[pl.ds(r, 256), :])
        return carry

    lax.fori_loop(0, F // 256, act_grad, 0)

    q_fwd(1)
    for k in range(3, W2):
        kv_fwd(k)
    for c in range(1, NC - 1):
        media_forward(c)
    for k in range(2, W2):
        q_fwd(k)
    for d in own_w:
        d.wait()
    kv_fin()

    def project(start, count):
        def step(i, carry):
            r = al(start + i * CH, 16)
            kv[pl.ds(r, CH), :] = nn(x_all[pl.ds(r, CH), :], kvw[...]).astype(BF16)
            return carry

        lax.fori_loop(0, count // CH, step, 0)

    def project_far(c):
        for j in range(1, X):
            block = lax.rem(xpos + X - j, X) * 2 + core
            project(block * Mo + c * CH, CH)

    def project_mate(c):
        for j in range(1, X):
            block = lax.rem(xpos + X - j, X) * 2 + 1 - core
            got(m_rows(block, c), m_fwd + c * X + j)
            project(block * Mo + c * CH, CH)

    project(n * Mo, Mo)
    project(M, KT - M)
    for c in range(NC):
        got(m_rows(mate, c), m_direct + c * X)
    project(mate * Mo, Mo)
    for c in range(NC - 1):
        project_far(c)
        project_mate(c)
    o_fwd(1)
    if NC > 1:
        media_forward(NC - 1)
    project_far(NC - 1)
    q_fin()
    q_act = nn(lat_all, wq[...]).astype(BF16).astype(F32)
    head_of = lax.div(lax.broadcasted_iota(jnp.int32, (L, C), 1), HEAD_DIM)

    def per_head(v):
        return jnp.concatenate([jnp.where(head_of == h, v, 0.0) for h in range(HL)], axis=0)

    def from_heads(v):
        total = jnp.where(head_of == 0, v[0:L], 0.0)
        for h in range(1, HL):
            total = total + jnp.where(head_of == h, v[h * L : (h + 1) * L], 0.0)
        return total

    q_big32 = per_head(q_act)
    q_big = q_big32.astype(BF16)
    q_big_t = q_big32.T.astype(BF16)
    project_mate(NC - 1)
    for k in range(2, W2 - 1):
        o_fwd(k)

    KB = 128

    def wide_mask(r):
        m = mt[pl.ds(r, KB), :]
        return jnp.concatenate([m] * (R // LANES), axis=1) > 0.0

    def score_step(j, top):
        r = al(j * KB, KB)
        s = nn(kv[pl.ds(r, KB), 0:C], q_big_t) * scale
        s = jnp.where(wide_mask(r), s, NEG)
        st[pl.ds(r, KB), :] = s
        return jnp.maximum(top, jnp.max(s, axis=0, keepdims=True))

    top = lax.fori_loop(0, KT // KB, score_step, jnp.full((1, R), NEG, F32))

    def exp_step(j, carry):
        total, dot = carry
        r = al(j * KB, KB)
        s = st[pl.ds(r, KB), :]
        e = jnp.exp(s - top)
        pt[pl.ds(r, KB), :] = e
        s = jnp.where(wide_mask(r), s, 0.0)
        st[pl.ds(r, KB), :] = s
        return (
            total + jnp.sum(e, axis=0, keepdims=True),
            dot + jnp.sum(e * s, axis=0, keepdims=True),
        )

    zero_row = jnp.zeros((1, R), F32)
    total, dot = lax.fori_loop(0, KT // KB, exp_step, (zero_row, zero_row))
    inv_total = 1.0 / total
    mean_score = dot * inv_total

    def prob_step(j, carry):
        r = al(j * KB, KB)
        pr = pt[pl.ds(r, KB), :] * inv_total
        pt[pl.ds(r, KB), :] = pr
        pn[:, pl.ds(r, KB)] = pr.T.astype(BF16)
        return carry

    o_fwd(W2 - 1)
    lax.fori_loop(0, KT // KB, prob_step, 0)
    attn = from_heads(nn(pn[...], kv[:, C : 2 * C]))
    attn_low = attn.astype(BF16)

    cot_fwd, cot_share = row_gather(cot_g)
    slat_share = spread(0, lat_all)
    at_w = lambda ref: rows(ref, al(w * L, 16), L)
    att_g[pl.ds(al(w * L, 16), L), :] = attn_low

    def narrow_sum(slot, parts):
        base = new("r", N)
        for k in range(1, N):
            put(rs_st.at[slot, npeer(k)], rs_rc.at[slot, k], base + k, "narrow", npeer(k))

        def finish():
            v = rs_st[slot, n].astype(F32)
            for k in range(1, N):
                got(rs_rc.at[slot, k], base + k)
                v = v + rs_rc[slot, k].astype(F32)
            return v

        return finish

    def stage(slot, cols, v):
        for i in range(N):
            rs_st[slot, i, :, cols] = v[i * Lo : (i + 1) * Lo].astype(BF16)

    o_fin()

    def branch_step(j, carry):
        r = al(j * 256, 256)
        stage(0, pl.ds(r, 256), nt(attn_low, wot[pl.ds(r, 256), :]))
        return carry

    lax.fori_loop(0, D // 256, branch_step, 0)
    branch_fin = narrow_sum(0, None)
    mid = lat + branch_fin()
    mid_mean, mid_istd, mid_hat = norm_stats(mid)
    hid_ag[n] = (mid_hat * gain_f + bias_f).astype(BF16)
    hid_fin = narrow_gather(hid_ag)
    up_in.wait()
    hid_all = hid_fin()
    hid_g[w] = hid_all
    hid_fwd, hid_share = row_gather(hid_g)
    att_fwd, att_fin = small_gather(at_w(att_g), blocks(att_g, L))

    own64 = pl.ds(al(w * L, 16), L)

    def ffn_step(j, carry):
        cs = pl.ds(al(j * 256, 256), 256)
        pre = nn(hid_all, up[:, cs])
        cdf = 0.5 * (1.0 + lax.erf(pre * (1.0 / math.sqrt(2.0))))
        density = jnp.exp(-0.5 * pre * pre) * (1.0 / math.sqrt(2.0 * math.pi))
        act_own[:, cs] = (pre * cdf).astype(BF16)
        pre_own[:, cs] = (ga[:, cs] * (cdf + pre * density)).astype(BF16)
        return carry

    lax.fori_loop(0, F // 256, ffn_step, 0)
    gpre = pre_own[...]

    def hid_back(j, carry):
        r = al(j * 256, 256)
        stage(1, pl.ds(r, 256), nt(gpre, up[pl.ds(r, 256), :]))
        return carry

    lax.fori_loop(0, D // 256, hid_back, 0)
    ghid_fin = narrow_sum(1, None)
    act_all = act_own[...]

    def ffn_out(j, carry):
        cs = pl.ds(al(j * 256, 256), 256)
        stage(2, cs, nn(act_all, down[:, cs]))
        return carry

    lax.fori_loop(0, D // 256, ffn_out, 0)
    ffn_fin = narrow_sum(2, None)
    for k in range(1, W2):
        cot_fwd(k)

    ghid = ghid_fin()
    grad_mid = cot_ref[...].astype(F32) + norm_back(ghid, mid_hat, mid_istd, gain_f)
    gb_ag[n] = grad_mid.astype(BF16)
    gb_fin = narrow_gather(gb_ag)
    acc8[...] = jnp.zeros_like(acc8)
    stat[...] = jnp.zeros_like(stat)
    stat[FRAMES_MAX + 4 : FRAMES_MAX + 5, :] = jnp.sum(ghid * mid_hat, axis=0, keepdims=True)
    stat[FRAMES_MAX + 5 : FRAMES_MAX + 6, :] = jnp.sum(ghid, axis=0, keepdims=True)
    hid_fwd(1)
    for k in range(1, W):
        got(cnt_ag.at[wsrc(k)], cnt_base + k)
    keys = cnt_ag[0]
    for i in range(1, W):
        keys = keys + cnt_ag[i]
    ent1 = ENT_COEF * float(W * M) / keys[0:1, :]
    ent = jnp.concatenate([ent1] * (R // LANES), axis=1)
    gb_all = gb_fin()
    sgb_share = spread(1, gb_all)

    g_attn = nn(gb_all, wot[...]).astype(BF16).astype(F32)
    g_big32 = per_head(g_attn)
    g_big = g_big32.astype(BF16)
    g_big_t = g_big32.T.astype(BF16)
    row_dot = jnp.sum(per_head(g_attn * attn).T, axis=0, keepdims=True)
    shift = row_dot - ent * mean_score

    def back_step(j, carry):
        r = al(j * KB, KB)
        pr = pt[pl.ds(r, KB), :]
        gp = nn(kv[pl.ds(r, KB), C : 2 * C], g_big_t)
        gs = pr * (gp - ent * st[pl.ds(r, KB), :] - shift)
        pn[:, pl.ds(r, KB)] = gs.T.astype(BF16)
        gpair[pl.ds(r, KB), 0:C] = (nn(gs.astype(BF16), q_big) * scale).astype(BF16)
        gpair[pl.ds(r, KB), C : 2 * C] = nn(pr.astype(BF16), g_big).astype(BF16)
        return carry

    lax.fori_loop(0, KT // KB // 2, back_step, 0)
    for k in range(2, W2):
        hid_fwd(k)
    lax.fori_loop(KT // KB // 2, KT // KB, back_step, 0)

    gq = (from_heads(nn(pn[...], kv[:, 0:C])) * scale).astype(BF16)
    gq_g[own64, :] = gq
    gq_fwd, gq_fin = small_gather(at_w(gq_g), blocks(gq_g, L))

    H = W2 // 2
    half = lax.div(w, 2)
    order = [(lax.rem(half + k, H) + (1 - lax.div(half, H)) * H) for k in range(H)]
    order += [(lax.rem(half + k, H) + lax.div(half, H) * H) for k in list(range(1, H)) + [0]]
    y_base = new("r", W2)
    z_base = new("r", W2)

    def kvg_rows(first):
        def step(j, carry):
            r = al(first * (D // 2) + j * 256, 256)
            kvg[pl.ds(r, 256), :] = tn(x_all[:, pl.ds(r, 256)], gpair[...]).astype(BF16)
            return carry

        lax.fori_loop(0, D // 512, step, 0)

    def kvg_to_partner(i):
        put(
            rows(kvg, al((2 * order[i] + 1 - par) * S, 16), S), rows(kvg_y, i * S, S),
            y_base + i, "wide", partner,
        )

    def kvg_step(i):
        g = order[i]
        got(rows(kvg_y, i * S, S), y_base + i)
        mine = pl.ds(al((2 * g + par) * S, 16), S)
        summed = kvg[mine, :].astype(F32) + kvg_y[i * S : (i + 1) * S, :].astype(F32)
        if i < W2 - 1:
            kvg[mine, :] = summed.astype(BF16)
            put(kvg.at[mine, :], rows(kvg_z, i * S, S), z_base + i, "wide", 2 * g + par)
        else:
            o_kv[...] = summed

    kvg_rows(1 - lax.div(half, H))
    for i in range(H):
        kvg_to_partner(i)

    mate_base = new("r", X * NC)
    xs_base = new("r", X * NC)

    def part(block, c):
        r = al(block * Mo + c * CH, 16)
        return nt(gpair[pl.ds(r, CH), :], kvw[...])

    mate_sent = {}

    def x_of(j):
        return lax.rem(xpos + j, X)

    def to_mate(j, c):
        b = x_of(j) * 2 + 1 - core
        if c in mate_sent:
            mate_sent[c].wait_send()
            sends[:] = [d for d in sends if d is not mate_sent[c]]
        mate_st[c * CH : (c + 1) * CH, :] = part(b, c).astype(BF16)
        mate_sent[c] = put(
            rows(mate_st, c * CH, CH), rows(mate_rc, (j * NC + c) * CH, CH), mate_base + j * NC + c, "narrow", mate
        )

    def from_mate(j, c):
        i = (j * NC + c) * CH
        got(rows(mate_rc, i, CH), mate_base + j * NC + c)
        return part(x_of(j) * 2 + core, c) + mate_rc[i : i + CH, :].astype(F32)

    def rows_out(j, cs):
        for c in cs:
            to_mate(j, c)
        for c in cs:
            i = ((j - 1) * NC + c) * CH
            x_st[i : i + CH, :] = from_mate(j, c).astype(BF16)
            put(
                rows(x_st, i, CH), rows(x_rc, i, CH), xs_base + (j - 1) * NC + c,
                "narrow", x_of(j) * 2 + core,
            )

    rows_out(1, range(NC // 2))
    kvg_rows(lax.div(half, H))
    for i in range(H, W2):
        kvg_to_partner(i)

    gpl = gpair[M : M + L, :]

    def lat_back(j, carry):
        r = al(j * 256, 256)
        stage(3, pl.ds(r, 256), nt(gpl, kvw[pl.ds(r, 256), :]) + nt(gq, wq[pl.ds(r, 256), :]))
        return carry

    lax.fori_loop(0, D // 256, lat_back, 0)
    glat_fin = narrow_sum(3, None)
    rows_out(1, range(NC // 2, NC))
    for j in range(2, X):
        rows_out(j, range(NC))
    for k in range(1, W2):
        att_fwd(k)
    slat_fin = slat_share()
    cot_fin = cot_share()
    hid_fin = hid_share()
    sgb_fin = sgb_share()
    third = [i * W2 // 4 for i in range(5)]
    for i in range(third[0], third[1]):
        kvg_step(i)
    for c in range(NC):
        to_mate(0, c)
    for c in range(NC):
        own_sum[c * CH : (c + 1) * CH, :] = from_mate(0, c)
    for i in range(third[1], third[2]):
        kvg_step(i)

    cot_fin()
    hid_fin()
    pick = (
        lax.broadcasted_iota(jnp.int32, (D, S), 0) == lax.broadcasted_iota(jnp.int32, (D, S), 1) + w * S
    ).astype(F32).astype(BF16)
    cot_rows = lambda: cot_g[...].reshape(W * L, D)
    hid_rows = lambda: hid_g[...].reshape(W * L, D)

    def pick_step(b, carry):
        at = pl.ds(al(b * L, 16), L)
        cot_sl[at, :] = nn(cot_g[b], pick).astype(BF16)
        hid_sl[at, :] = nn(hid_g[b], pick).astype(BF16)
        return carry

    lax.fori_loop(0, W, pick_step, 0)

    def unit_step(j, carry):
        cs = pl.ds(al(j * 256, 256), 256)
        pre = nn(hid_rows(), up[:, cs])
        grad = nt(cot_rows(), down[cs, :])
        cdf = 0.5 * (1.0 + lax.erf(pre * (1.0 / math.sqrt(2.0))))
        density = jnp.exp(-0.5 * pre * pre) * (1.0 / math.sqrt(2.0 * math.pi))
        o_down[:, cs] = tn(cot_sl[...], (pre * cdf).astype(BF16))
        o_up[:, cs] = tn(hid_sl[...], (grad * (cdf + pre * density)).astype(BF16))
        return carry

    units = F // 256
    for t in range(3):
        lax.fori_loop(t * units // 3, (t + 1) * units // 3, unit_step, 0)
        for i in range(third[min(t + 2, 4)], third[min(t + 3, 4)]):
            kvg_step(i)
    here(o_up, out_up)
    here(o_down, out_down)

    out_l = (mid + ffn_fin()).astype(BF16)
    lat_nf[0] = out_l
    here(lat_nf.at[0], out_lat)
    glat = glat_fin()
    g_lat = grad_mid + norm_back(glat, lat_hat, lat_istd, gain_l)
    lat_nf[1] = g_lat.astype(BF16)
    here(lat_nf.at[1], out_gl)
    stat[FRAMES_MAX + 2 : FRAMES_MAX + 3, :] = jnp.sum(glat * lat_hat, axis=0, keepdims=True)
    stat[FRAMES_MAX + 3 : FRAMES_MAX + 4, :] = jnp.sum(glat, axis=0, keepdims=True)

    for k in range(1, W2):
        gq_fwd(k)
    att_fin()
    sgb_fin()
    o_o[...] = tn(sl_rc[1].reshape(W * L, S), att_g[...])
    here(o_o, out_o)
    gq_fin()
    slat_fin()
    o_q[...] = tn(sl_rc[0].reshape(W * L, S), gq_g[...])
    here(o_q, out_q)

    gm_out = []
    for c in range(NC):
        for j in range(1, X):
            i = ((j - 1) * NC + c) * CH
            got(rows(x_rc, i, CH), xs_base + (j - 1) * NC + c)
        f = frame_of(c)
        te_row = te32[pl.ds(f, 1), :]

        def back_rows(i, carry, c=c, te_row=te_row):
            r = al(c * CH + i * 16, 16)
            dy = own_sum[pl.ds(r, 16), :]
            for j in range(1, X):
                dy = dy + x_rc[pl.ds(al((j - 1) * Mo + r, 16), 16), :].astype(F32)
            mean = mean_s[pl.ds(r, 16), 0:1]
            inv_std = istd_s[pl.ds(r, 16), 0:1]
            hat = (media[pl.ds(r, 16), :].astype(F32) + te_row - mean) * inv_std
            dx = norm_back(dy, hat, inv_std, gain_m)
            media[pl.ds(r, 16), :] = dx.astype(BF16)
            acc8[0:8, :] += fold8(dy * hat)
            acc8[8:16, :] += fold8(dy)
            acc8[16:24, :] += fold8(dx)
            return carry

        lax.fori_loop(0, CH // 16, back_rows, 0, unroll=2)
        stat[pl.ds(f, 1), :] += jnp.sum(acc8[16:24, :], axis=0, keepdims=True)
        acc8[16:24, :] = jnp.zeros((8, D), F32)
        here(rows(media, c * CH, CH), rows(out_gm, c * CH, CH))
    stat[FRAMES_MAX : FRAMES_MAX + 1, :] = jnp.sum(acc8[0:8, :], axis=0, keepdims=True)
    stat[FRAMES_MAX + 1 : FRAMES_MAX + 2, :] = jnp.sum(acc8[8:16, :], axis=0, keepdims=True)

    vec = stat[...]
    for b in range(W):
        vec_st[b] = vec[:, b * S : (b + 1) * S]
    v_base = new("r", W)
    for k in range(1, W):
        put(vec_st.at[wpeer(k)], vec_rc.at[k], v_base + k, "wide", wpeer(k))
    for i in range(W2 - 1):
        got(rows(kvg_z, i * S, S), z_base + i)
        o_kv[...] += kvg_z[i * S : (i + 1) * S, :].astype(F32)
    here(o_kv, out_kv)
    vs = vec_st[w]
    for k in range(1, W):
        got(vec_rc.at[k], v_base + k)
        vs = vs + vec_rc[k]
    for i in range(N):
        vec2_st[i] = vs[:, i * V : (i + 1) * V]
    v2_base = new("r", N)
    for k in range(1, N):
        put(vec2_st.at[npeer(k)], vec2_rc.at[k], v2_base + k, "narrow", npeer(k))
    vs = vec2_st[n]
    for k in range(1, N):
        got(vec2_rc.at[k], v2_base + k)
        vs = vs + vec2_rc[k]
    o_vec[...] = vs
    here(o_vec, out_vec)

    for d in sends:
        d.wait_send()
    for cond, copy in sends_if:

        @pl.when(cond)
        def _(copy=copy):
            copy().wait_send()

    for d in local:
        d.wait()
    sem_counts.update(counters)


def finish_kernel(p, pieces, *refs):
    src, dst, buf, sem_in, sem_out = refs[:9], refs[9:24], refs[24:33], refs[33], refs[34]
    V, C = p.V, p.C
    loads = []
    for i in range(9):
        count = src[i].shape[0] // pieces[i]
        for c in range(pieces[i]):
            at = pl.ds(c * count, count)
            d = pltpu.make_async_copy(src[i].at[at, :], buf[i].at[at, :], sem_in.at[len(loads)])
            d.start()
            loads.append((i, at, d))
    stores = []

    def store(a, b):
        d = pltpu.make_async_copy(a, b, sem_out.at[len(stores)])
        d.start()
        stores.append(d)

    first = {0: 0, 1: 1, 2: 2, 4: 10, 5: 11, 6: 12, 7: 13, 8: 14}
    for i, at, d in loads:
        d.wait()
        if i == 3:
            store(buf[3].at[pl.ds(0, FRAMES_MAX), :], dst[3])
            for k in range(6):
                store(buf[3].at[FRAMES_MAX + k], dst[4 + k])
        elif i == 5 and C % LANES == 0:
            for k in range(2):
                store(buf[5].at[:, pl.ds(k * C, C)], dst[11].at[:, k, :])
        else:
            store(buf[i].at[at, :], dst[first[i]].at[at, :])
    for d in stores:
        d.wait()


def finish(p, outs):
    sds = jax.ShapeDtypeStruct
    hbm = pl.BlockSpec(memory_space=pl.ANY)
    pieces = [1, 4, 1, 1, 1, 1, 1, 2, 2]
    shapes = [sds(a.shape, a.dtype) for a in outs]
    vec = [sds((FRAMES_MAX, p.V), F32)] + [sds((p.V,), F32)] * 6
    res = pl.pallas_call(
        functools.partial(finish_kernel, p, pieces),
        out_shape=tuple(shapes[:3] + vec + [shapes[4], sds((p.S, 2, p.C), F32) if p.C % LANES == 0 else shapes[5]] + shapes[6:]),
        in_specs=[hbm] * 9,
        out_specs=[hbm] * 15,
        scratch_shapes=[pltpu.VMEM(a.shape, a.dtype) for a in outs]
        + [pltpu.SemaphoreType.DMA((sum(pieces),)), pltpu.SemaphoreType.DMA((sum(pieces) + 7,))],
        compiler_params=pltpu.CompilerParams(has_side_effects=True),
    )(*outs)
    return res[0], res[1], res[2], res[3:10], res[10], res[11].reshape(p.S, 2, p.C), res[12], res[13], res[14]


def make_body(mesh):
    def body(
        media_feats, latents, frame_counts, media_mask, time_embed, media_gain, media_bias, latent_gain,
        latent_bias, ffn_gain, ffn_bias, query_weight, keyval_weight, output_weight, up_weight,
        down_weight, cotangent,
    ):
        p = Plan(mesh, media_feats, latents, up_weight)
        D, C, S, L, Lo, KT, R, F, N, W, Mo = p.D, p.C, p.S, p.L, p.Lo, p.KT, p.R, p.F, p.N, p.W, p.Mo
        X, W2, NC, V = p.X, p.W2, p.NC, p.V
        vm = pl.BlockSpec(memory_space=pltpu.VMEM)
        hbm = pl.BlockSpec(memory_space=pl.ANY)
        smem = pl.BlockSpec(memory_space=pltpu.SMEM)
        sds = jax.ShapeDtypeStruct
        vmem = pltpu.VMEM
        scratch = [
            vmem((Mo, D), BF16),
            vmem((KT, D), BF16),
            vmem((D, 2 * C), BF16),
            vmem((D, C), BF16),
            vmem((D, C), BF16),
            vmem((D, F), BF16),
            vmem((F, D), BF16),
            vmem((KT, 2 * C), BF16),
            vmem((KT, R), F32),
            vmem((KT, R), F32),
            vmem((R, KT), BF16),
            vmem((KT, 2 * C), BF16),
            vmem((KT, LANES), F32),
            vmem((FRAMES_MAX, D), F32),
            vmem((Mo, LANES), F32),
            vmem((Mo, LANES), F32),
            vmem((2, Lo, D), BF16),
            vmem((N, Lo, D), BF16),
            vmem((N, Lo, D), BF16),
            vmem((W, 8, LANES), F32),
            vmem((4, N, Lo, D), BF16),
            vmem((4, N, Lo, D), BF16),
            vmem((N, Lo, D), BF16),
            vmem((N, Lo, D), BF16),
            vmem((Mo, D), BF16),
            vmem((X * Mo, D), BF16),
            vmem(((X - 1) * Mo, D), BF16),
            vmem(((X - 1) * Mo, D), BF16),
            vmem((Mo, D), F32),
            vmem((W2 * S, 2 * C), BF16),
            vmem((W2 * S, 2 * C), BF16),
            vmem((L, F), BF16),
            vmem((L, F), BF16),
            vmem((W, L, D), BF16),
            vmem((W, L, D), BF16),
            vmem((W * L, C), BF16),
            vmem((W * L, C), BF16),
            vmem((2, W, L, S), BF16),
            vmem((2, W, L, S), BF16),
            vmem((W * L, S), BF16),
            vmem((W * L, S), BF16),
            vmem((L, F), F32),
            vmem((24, D), F32),
            vmem((16, D), F32),
            vmem((W, 16, S), F32),
            vmem((W, 16, S), F32),
            vmem((N, 16, V), F32),
            vmem((N, 16, V), F32),
            vmem((S, F), F32),
            vmem((S, F), F32),
            vmem((S, C), F32),
            vmem((S, C), F32),
            vmem((S, 2 * C), F32),
            vmem((16, V), F32),
            pltpu.SemaphoreType.DMA((40 * W + 8 * N * p.NC + 64,)),
            pltpu.SemaphoreType.DMA((40 * W + 8 * N * p.NC + 64,)),
            pltpu.SemaphoreType.DMA((64,)),
        ]
        outs = pl.pallas_call(
            functools.partial(body_kernel, p, {}),
            out_shape=(
                sds((Lo, D), BF16),
                sds((Mo, D), BF16),
                sds((Lo, D), BF16),
                sds((16, V), F32),
                sds((S, C), F32),
                sds((S, 2 * C), F32),
                sds((S, C), F32),
                sds((S, F), F32),
                sds((S, F), F32),
            ),
            in_specs=[hbm, vm, smem, vm, vm, vm, vm, vm, vm, vm, vm, hbm, vm, hbm, hbm, hbm, vm],
            out_specs=[hbm] * 9,
            scratch_shapes=scratch,
            compiler_params=pltpu.CompilerParams(
                collective_id=0, has_side_effects=True, vmem_limit_bytes=67_043_328
            ),
        )(
            media_feats[0], latents[0], frame_counts, media_mask.reshape(p.M // LANES, LANES), time_embed,
            media_gain, media_bias, latent_gain, latent_bias, ffn_gain, ffn_bias,
            query_weight, keyval_weight, output_weight.T, up_weight, down_weight, cotangent[0],
        )
        lat, gm, gl, vec, gq, gkv, go, gup, gdown = finish(p, outs)
        return (lat[None], gm[None], gl[None]) + tuple(vec) + (gq, gkv, go.T, gup, gdown.T)

    return body


def solution(mesh):
    both = P(("wide", "narrow"))
    rows = P("wide", "narrow", None)
    return jax.shard_map(
        make_body(mesh),
        mesh=mesh,
        in_specs=(
            rows, rows, P("wide"), P("wide", None), P(), P(), P(), P(), P(), P(), P(), P("wide", "narrow"),
            P("wide", None, "narrow"), P("narrow", "wide"), P(None, "narrow"), P("narrow", None), rows,
        ),
        out_specs=(
            rows, rows, rows, P(None, ("wide", "narrow")), both, both, both, both, both, both,
            P("wide", "narrow"), P("wide", None, "narrow"), P("narrow", "wide"), P("wide", "narrow"),
            P("narrow", "wide"),
        ),
        check_vma=False,
    )
```
